256 devices in a mesh: dp: 32 (over z_hi, y, core), expert: 8 (over x, z_lo).
Axes of the slice: x: 4, y: 4, z: 8 (z_hi: 4, z_lo: 2; z = z_hi * 2 + z_lo), core: 2. Of those that a mesh axis runs over, the one named last changes fastest.
Arguments:
- tokens: bfloat16 [49152, 2048], P(('dp', 'expert')), may hold values from -24 to 24
- routes: int32 [49152, 6], P(('dp', 'expert')), may hold values from 0 to 63, as said below
- gate_scale: float32 [49152, 6], P(('dp', 'expert')), may hold values from 0.2 to 2
- w_gate: bfloat16 [8, 2048, 768], P('expert', 'dp'), may hold values from -0.125 to 0.125
- w_up: bfloat16 [8, 2048, 768], P('expert', 'dp'), may hold values from -0.125 to 0.125
- w_down: bfloat16 [8, 2048, 768], P('expert', 'dp'), may hold values from -0.21875 to 0.21875
- d_out: bfloat16 [49152, 2048], P(('dp', 'expert')), may hold values from -24 to 24
Outputs:
- layer_out: bfloat16 [49152, 2048], P(('dp', 'expert'))
- d_tokens: bfloat16 [49152, 2048], P(('dp', 'expert'))
- grad_gate: float32 [8, 2048, 768], P('expert', 'dp')
- grad_up: float32 [8, 2048, 768], P('expert', 'dp')
- grad_down: float32 [8, 2048, 768], P('expert', 'dp')
The draws below stay inside these ranges and needn't reach their ends.
Inputs may be any that keep to these rules, and one draw needn't show every extreme that they name: `routes`: each token names 6 different experts. The experts of this window are 0 to 7; among the 192 tokens of one device no window expert is named by more than 32 tokens.
All inputs are finite; a program needn't handle non-finite values.
Results may differ from the reference program's by a relative error of at most 0.02.
Values may be sent and summed in bfloat16 or wider, within the bound.
A program may use at most 64 MiB of HBM per device.

```python
import math
import jax
import jax.numpy as jnp
from jax import lax

D = 2048
EXPERTS = 64
TOP = 6
H = 768
TOK_DEV = 192
CAP = 32
WINDOW = 8
TOKENS = 49152


def draw_routes(key, part):
    blocks = TOKENS // TOK_DEV
    stride = TOK_DEV // WINDOW
    others_count = EXPERTS - WINDOW
    k_count, k_rank, k_other, k_order = jax.random.split(key, 4)
    lower = (CAP + 3) // 4
    counts = jax.random.randint(k_count, (blocks, WINDOW), lower, CAP + 1)
    full_expert = jnp.arange(blocks) // WINDOW % WINDOW
    counts = jnp.where(jnp.arange(WINDOW)[None, :] == full_expert[:, None], CAP, counts)
    scores = jax.random.randint(k_rank, (blocks, TOK_DEV), 0, 2 ** 20) * TOK_DEV + jnp.arange(TOK_DEV)[None, :]
    order = jnp.argsort(scores, axis=1)
    rank = jnp.argsort(order, axis=1)
    offset = (rank[:, :, None] - stride * jnp.arange(WINDOW)[None, None, :]) % TOK_DEV
    member = offset < counts[:, None, :]
    number = jnp.sum(member.astype(jnp.int32), axis=2)
    window_key = jnp.where(member, jnp.arange(WINDOW)[None, None, :], WINDOW + jnp.arange(WINDOW)[None, None, :])
    window_sorted = jnp.sort(window_key, axis=2)
    other_scores = jax.random.randint(k_other, (blocks, TOK_DEV, others_count), 0, 2 ** 20) * others_count + jnp.arange(others_count)[None, None, :]
    other_ids = WINDOW + jnp.argsort(other_scores, axis=2)[:, :, :TOP]
    slot = jnp.broadcast_to(jnp.arange(TOP)[None, None, :], (blocks, TOK_DEV, TOP))
    pick_window = jnp.take_along_axis(window_sorted, jnp.minimum(slot, WINDOW - 1), axis=2)
    pick_other = jnp.take_along_axis(other_ids, jnp.clip(slot - number[:, :, None], 0, TOP - 1), axis=2)
    ids = jnp.where(slot < number[:, :, None], pick_window, pick_other)
    column_scores = jax.random.randint(k_order, (blocks, TOK_DEV, TOP), 0, 2 ** 20) * TOP + slot
    ids = jnp.take_along_axis(ids, jnp.argsort(column_scores, axis=2), axis=2)
    return ids.reshape(TOKENS, TOP).astype(jnp.int32)


def raised(result, stream_key, source, target, blocks, factor):
    def block_of(dim):
        return (jnp.arange(result.shape[dim]) // (result.shape[dim] // blocks)).reshape((-1,) + (1,) * (result.ndim - 1 - dim))

    one_side = jax.random.permutation(stream_key, blocks)[block_of(target)]
    other_side = (block_of(target) + blocks // 2) % blocks
    return jnp.where((block_of(source) == one_side) | (block_of(source) == other_side), factor * result, result)


def levels(key, extent, cuts, low, high):
    loudness, own = 1.0, jax.random.fold_in(key, 6)
    for dim, blocks in cuts:
        draws = jnp.exp(jax.random.uniform(jax.random.fold_in(own, dim), (blocks,), jnp.float32, low / len(cuts), high / len(cuts)))
        loudness = loudness * jnp.repeat(draws, extent[dim] // blocks).reshape([-1 if axis == dim else 1 for axis in range(len(extent))])
    return loudness


def normal_values(rng, shape, scale, limit, cuts=(), held_as=jnp.bfloat16):
    loudness = levels(rng, shape, cuts, -0.22, 0.18) if cuts else 1.0
    result = jax.random.normal(rng, shape, jnp.float32) * scale * loudness
    return jnp.minimum(jnp.maximum(result, -limit), limit).astype(held_as)


def gaussian_with(own_key, extent, width, reach, cuts, heavy, kind=jnp.bfloat16):
    drawn = width * jax.random.normal(own_key, extent, jnp.float32)
    if cuts:
        drawn = drawn * levels(own_key, extent, cuts, -0.22, 0.18)
    return jnp.clip(raised(drawn, jax.random.fold_in(own_key, 3), *heavy), -reach, reach).astype(kind)


def setup_inputs(seed: int = 0) -> dict:
    arg_keys = jax.random.split(jax.random.key(seed), 8)
    return {
        "tokens": gaussian_with(arg_keys[0], (TOKENS, D), 1.0, 24.0, ((0, 256),), (0, 1, 256, 6.0)),
        "routes": draw_routes(jax.random.fold_in(arg_keys[7], 71), 0),
        "gate_scale": jnp.clip(jnp.exp(math.log(2.0) - 2.3025851 * jax.random.uniform(arg_keys[2], (TOKENS, TOP), jnp.float32) ** levels(arg_keys[2], (TOKENS, TOP), ((0, 256),), -0.2, 0.2)), 0.2, 2.0),
        "w_gate": normal_values(arg_keys[3], (WINDOW, D, H), D ** -0.5, 0.125, ((0, 8), (1, 32))),
        "w_up": normal_values(arg_keys[4], (WINDOW, D, H), D ** -0.5, 0.125, ((0, 8), (1, 32))),
        "w_down": normal_values(arg_keys[5], (WINDOW, D, H), H ** -0.5, 0.21875, ((0, 8), (1, 32))),
        "d_out": gaussian_with(arg_keys[6], (TOKENS, D), 1.0, 24.0, ((0, 256),), (0, 1, 256, 6.0)),
    }


def reference(tokens, routes, gate_scale, w_gate, w_up, w_down, d_out):
    blocks = TOKENS // TOK_DEV
    slots = WINDOW * CAP
    per_block = TOK_DEV * TOP
    groups = blocks // WINDOW
    combine = gate_scale / jnp.sum(gate_scale, axis=1, keepdims=True)
    ids = routes.reshape(blocks, per_block)
    route_weight = combine.reshape(blocks, per_block)
    live = ids < WINDOW
    onehot = ((ids[:, :, None] == jnp.arange(WINDOW, dtype=jnp.int32)[None, None, :]) & live[:, :, None]).astype(jnp.int32)
    position = jnp.sum((jnp.cumsum(onehot, axis=1) - onehot) * onehot, axis=2)
    dest = jnp.where(live, ids * CAP + position, slots).astype(jnp.int32)
    block_idx = jnp.broadcast_to(jnp.arange(blocks, dtype=jnp.int32)[:, None], dest.shape)
    token_idx = block_idx * TOK_DEV + (jnp.arange(per_block, dtype=jnp.int32) // TOP)[None, :]
    source = jnp.zeros((blocks, slots + 1), jnp.int32).at[block_idx, dest].set(token_idx)[:, :slots]
    filled = jnp.zeros((blocks, slots + 1), jnp.int32).at[block_idx, dest].set(1)[:, :slots]
    slot_weight = jnp.zeros((blocks, slots + 1), jnp.float32).at[block_idx, dest].set(route_weight)[:, :slots]

    def regroup(values):
        return values.reshape(groups, WINDOW, WINDOW, CAP).transpose(2, 0, 1, 3).reshape(WINDOW, groups, WINDOW * CAP)

    source = regroup(source)
    filled = regroup(filled)
    slot_weight = regroup(slot_weight)

    def expert(index):
        src = source[index]
        used = filled[index][:, :, None] > 0
        x_rows = jnp.where(used, tokens[src], jnp.zeros((), jnp.bfloat16)).astype(jnp.bfloat16)
        d_rows = jnp.where(used, d_out[src].astype(jnp.float32) * slot_weight[index][:, :, None], 0.0).astype(jnp.bfloat16)
        wg = w_gate[index].astype(jnp.float32)
        wu = w_up[index].astype(jnp.float32)
        wd = w_down[index].astype(jnp.float32)
        xf = x_rows.astype(jnp.float32)
        df = d_rows.astype(jnp.float32)
        gate = jnp.einsum("grd,dh->grh", xf, wg)
        up = jnp.einsum("grd,dh->grh", xf, wu)
        sig = jax.nn.sigmoid(gate)
        act = gate * sig
        hidden = (act * up).astype(jnp.bfloat16)
        hf = hidden.astype(jnp.float32)
        expert_out = jnp.einsum("grh,dh->grd", hf, wd).astype(jnp.bfloat16)
        d_hidden = jnp.einsum("grd,dh->grh", df, wd)
        d_gate = (d_hidden * up * sig * (1.0 + gate * (1.0 - sig))).astype(jnp.bfloat16)
        d_up = (d_hidden * act).astype(jnp.bfloat16)
        dgf = d_gate.astype(jnp.float32)
        duf = d_up.astype(jnp.float32)
        d_in = (jnp.einsum("grh,dh->grd", dgf, wg) + jnp.einsum("grh,dh->grd", duf, wu)).astype(jnp.bfloat16)
        part_gate = jnp.einsum("grd,grh->gdh", xf, dgf).astype(jnp.bfloat16).astype(jnp.float32)
        part_up = jnp.einsum("grd,grh->gdh", xf, duf).astype(jnp.bfloat16).astype(jnp.float32)
        part_down = jnp.einsum("grd,grh->gdh", df, hf).astype(jnp.bfloat16).astype(jnp.float32)
        return expert_out, d_in, jnp.sum(part_gate, axis=0), jnp.sum(part_up, axis=0), jnp.sum(part_down, axis=0)

    expert_out, d_in, grad_gate, grad_up, grad_down = lax.map(expert, jnp.arange(WINDOW, dtype=jnp.int32))
    rows = WINDOW * CAP
    owner_expert = dest // CAP
    owner_slot = dest % CAP
    group_of = block_idx // WINDOW
    source_of = block_idx % WINDOW
    flat_row = (owner_expert * groups + group_of) * rows + source_of * CAP + owner_slot
    flat_row = jnp.where(live, flat_row, 0).astype(jnp.int32).reshape(TOKENS, TOP)
    live_tok = live.reshape(TOKENS, TOP)
    weight_tok = jnp.where(live_tok, combine, 0.0)
    flat_out = expert_out.reshape(-1, D)
    flat_in = d_in.reshape(-1, D)
    total_out = jnp.zeros((TOKENS, D), jnp.float32)
    total_in = jnp.zeros((TOKENS, D), jnp.float32)
    for choice_index in range(TOP):
        rows_pick = flat_row[:, choice_index]
        total_out = total_out + weight_tok[:, choice_index:choice_index + 1] * flat_out[rows_pick].astype(jnp.float32)
        total_in = total_in + jnp.where(live_tok[:, choice_index:choice_index + 1], flat_in[rows_pick].astype(jnp.float32), 0.0)
    return total_out.astype(jnp.bfloat16), total_in.astype(jnp.bfloat16), grad_gate, grad_up, grad_down
```

```python
import jax
import jax.numpy as jnp
from jax import lax
from jax.experimental import pallas as pl
from jax.experimental.pallas import tpu as pltpu
from jax.sharding import PartitionSpec as P

CAP = 32
MESH = pl.DeviceIdType.MESH
F32 = jnp.float32
BF16 = jnp.bfloat16

NY, NZ, SH = 4, 4, 128
HH = 384
HC = 3 * HH
YB = NZ * SH
NE = 8
TOK = 192
ROWS = NE * CAP

S_SIB = 0
S_LOC = 3
S_AGZ = 6
S_AGY = 10
S_A2X = 26
S_A2D = 34
S_SX = 42
S_SO = 44
S_BO = 46
S_BI = 54
S_RY1 = 62
S_RY2 = 70
S_RZ1 = 78
S_RZ2 = 80
S_FIN = 82
S_ALL = 83


def kernel(
    tok_ref, rt_ref, gs_ref, wg_ref, wu_ref, wd_ref, do_ref,
    lo_ref, dt_ref, gg_ref, gu_ref, gd_ref,
    W, X, D, XT, DT, SX, SD, SEL, ACC, CAT, T, R1, R2, Z1, Z2, ZS, FS, FR,
    OS, OR, BS, BK, ss, rs,
):
    i = lax.axis_index("dp")
    j = lax.axis_index("expert")
    c = lax.rem(i, 2)
    o = 1 - c
    p = lax.div(i, 2)
    y = lax.rem(p, 4)
    z = lax.div(p, 4)
    yp, ym, y2 = lax.rem(y + 1, 4), lax.rem(y + 3, 4), lax.rem(y + 2, 4)
    zp, zm, z2 = lax.rem(z + 1, 4), lax.rem(z + 3, 4), lax.rem(z + 2, 4)

    def place(yy, zz, cc):
        return {"dp": (zz * 4 + yy) * 2 + cc}

    sib = place(y, z, o)
    to_yp, to_ym = place(yp, z, c), place(ym, z, c)
    to_zp, to_zm = place(y, zp, c), place(y, zm, c)

    def peer(k):
        return lax.rem(j + k, NE)

    def source(k):
        return lax.rem(j + NE - k, NE)

    sent = []

    def send(src, dst, k, to):
        copy = pltpu.make_async_remote_copy(
            src_ref=src, dst_ref=dst, send_sem=ss.at[k], recv_sem=rs.at[k],
            device_id=to, device_id_type=MESH,
        )
        copy.start()
        sent.append(copy)

    def arrived(ref, k, to=None):
        pltpu.make_async_remote_copy(
            src_ref=ref, dst_ref=ref, send_sem=ss.at[k], recv_sem=rs.at[k],
            device_id=sib if to is None else to, device_id_type=MESH,
        ).wait_recv()

    barrier = pltpu.get_barrier_semaphore()
    for to in (sib, to_yp, to_ym, to_zp, to_zm):
        pl.semaphore_signal(barrier, inc=1, device_id=to, device_id_type=MESH)
    for k in range(1, NE):
        pl.semaphore_signal(barrier, inc=1, device_id={"expert": peer(k)}, device_id_type=MESH)
    pl.semaphore_wait(barrier, 5 + NE - 1)

    mine = pl.ds(pl.multiple_of(c * 64, 64), 64)
    theirs = pl.ds(pl.multiple_of(o * 64, 64), 64)
    half_c = pl.ds(pl.multiple_of(c * HH, 128), HH)
    half_o = pl.ds(pl.multiple_of(o * HH, 128), HH)
    local = []
    for n, w_ref in enumerate((wg_ref, wu_ref, wd_ref)):
        cols = pl.ds(n * HH, HH)
        send(w_ref.at[0, :, half_o], W.at[y, z, mine, cols], S_SIB + n, sib)
        copy = pltpu.make_async_copy(
            w_ref.at[0, :, half_c], W.at[y, z, mine, cols], rs.at[S_LOC + n]
        )
        copy.start()
        local.append(copy)
    for copy in local:
        copy.wait()
    for n in range(3):
        arrived(W.at[y, z, theirs, pl.ds(n * HH, HH)], S_SIB + n)

    low, high = pl.ds(0, 64), pl.ds(64, 64)

    def along_y(step, zz):
        send(W.at[y, zz], W.at[y, zz], S_AGY + 4 * step, to_yp)
        send(W.at[y, zz], W.at[y, zz], S_AGY + 4 * step + 1, to_ym)

    def onward_y(step, zz):
        arrived(W.at[ym, zz], S_AGY + 4 * step)
        send(W.at[ym, zz, low], W.at[ym, zz, low], S_AGY + 4 * step + 2, to_yp)
        arrived(W.at[yp, zz], S_AGY + 4 * step + 1)
        send(W.at[yp, zz, high], W.at[yp, zz, high], S_AGY + 4 * step + 3, to_ym)

    send(W.at[y, z], W.at[y, z], S_AGZ, to_zp)
    send(W.at[y, z], W.at[y, z], S_AGZ + 1, to_zm)
    along_y(0, z)

    shape = (TOK, ROWS)
    lane = lax.broadcasted_iota(jnp.int32, shape, 1)
    lane_e = lax.div(lane, CAP)
    lane_s = lax.rem(lane, CAP).astype(F32)
    scale = gs_ref[...]
    combine = scale / jnp.sum(scale, axis=1, keepdims=True)
    routes = rt_ref[...]
    named = jnp.zeros(shape, F32)
    weight = jnp.zeros(shape, F32)
    for s in range(6):
        same = routes[:, s:s + 1] == lane_e
        named = jnp.where(same, 1.0, named)
        weight = jnp.where(same, combine[:, s:s + 1], weight)
    earlier = (
        lax.broadcasted_iota(jnp.int32, (TOK, TOK), 1)
        < lax.broadcasted_iota(jnp.int32, (TOK, TOK), 0)
    ).astype(F32).astype(BF16)
    position = jnp.dot(earlier, named.astype(BF16), preferred_element_type=F32)
    chosen = jnp.where(position == lane_s, named, 0.0)
    weight = weight * chosen
    SEL[0] = chosen.astype(BF16)
    rest = weight
    for n in range(1, 4):
        part = rest.astype(BF16)
        SEL[n] = part
        rest = rest - part.astype(F32)

    tn = (((0,), (0,)), ((), ()))
    ones = jnp.ones((TOK, 128), BF16)
    slot_weight = sum(
        lax.dot_general(SEL[n], ones, tn, preferred_element_type=F32) for n in (3, 2, 1)
    )
    slot_weight = jnp.concatenate([slot_weight] * 4, axis=1)

    def columns(ref, yy):
        return jnp.concatenate(
            [ref[:, (zz * 4 + yy) * SH:(zz * 4 + yy + 1) * SH] for zz in range(NZ)], axis=1
        )

    for yy in range(NY):
        rows = lax.dot_general(SEL[0], columns(tok_ref, yy), tn, preferred_element_type=F32)
        SX[yy] = rows.astype(BF16).reshape(NE, CAP, YB)
        rows = lax.dot_general(SEL[0], columns(do_ref, yy), tn, preferred_element_type=F32)
        SD[yy] = (rows * slot_weight).astype(BF16).reshape(NE, CAP, YB)

    here = c * NE + j
    for src, dst, base in ((SX, X, S_A2X), (SD, D, S_A2D)):
        for k in range(1, NE):
            send(src.at[:, peer(k)], dst.at[:, here], base + k, {"expert": peer(k)})
    local = []
    for src, dst, base in ((SX, X, S_A2X), (SD, D, S_A2D)):
        copy = pltpu.make_async_copy(src.at[:, j], dst.at[:, here], rs.at[base])
        copy.start()
        local.append(copy)

    arrived(W.at[y, zm], S_AGZ)
    send(W.at[y, zm, low], W.at[y, zm, low], S_AGZ + 2, to_zp)
    along_y(1, zm)
    arrived(W.at[y, zp], S_AGZ + 1)
    send(W.at[y, zp, high], W.at[y, zp, high], S_AGZ + 3, to_zm)
    along_y(2, zp)
    onward_y(0, z)
    arrived(W.at[y, z2, low], S_AGZ + 2)
    arrived(W.at[y, z2, high], S_AGZ + 3)
    along_y(3, z2)

    for n, (dst, base) in enumerate(((X, S_A2X), (D, S_A2D))):
        local[n].wait()
        for k in range(1, NE):
            arrived(dst.at[:, c * NE + source(k)], base + k)
        own = dst.at[:, pl.ds(c * NE, NE)]
        send(own, own, S_SX + n, sib)
    onward_y(1, zm)
    onward_y(2, zp)
    arrived(X.at[:, pl.ds(o * NE, NE)], S_SX)
    arrived(D.at[:, pl.ds(o * NE, NE)], S_SX + 1)

    def turn(yy, carry):
        XT[yy] = X[yy].reshape(2 * ROWS, YB).T
        DT[yy] = D[yy].reshape(2 * ROWS, YB).T
        return carry

    lax.fori_loop(0, NY, turn, 0)

    def accumulate(yy, first):
        def tile(m, carry):
            rows = pl.ds(pl.multiple_of(m * ROWS, ROWS), ROWS)
            blocks = pl.ds(m * NE, NE)
            for ref, cols in ((X, (0, 256)), (X, (256, 512)), (X, (512, 768)), (D, (768, 1152))):
                lo, hi = cols
                got = jnp.dot(
                    ref[yy, blocks].reshape(ROWS, YB),
                    W[yy, :, :, lo:hi].reshape(YB, hi - lo),
                    preferred_element_type=F32,
                )
                if first:
                    ACC[rows, lo:hi] = got
                else:
                    ACC[rows, lo:hi] += got
            return carry

        lax.fori_loop(0, 2, tile, 0)

    accumulate(y, True)
    onward_y(3, z2)
    accumulate(ym, False)
    accumulate(yp, False)
    for step, zz in enumerate((z, zm, zp, z2)):
        arrived(W.at[y2, zz, low], S_AGY + 4 * step + 2)
        arrived(W.at[y2, zz, high], S_AGY + 4 * step + 3)
    accumulate(y2, False)

    def activate(m, carry):
        rows = pl.ds(pl.multiple_of(m * 64, 64), 64)
        gate, up, d_hidden = ACC[rows, 0:HH], ACC[rows, HH:2 * HH], ACC[rows, 2 * HH:HC]
        sig = jax.nn.sigmoid(gate)
        act = gate * sig
        CAT[rows, 0:HH] = (d_hidden * up * sig * (1.0 + gate * (1.0 - sig))).astype(BF16)
        CAT[rows, HH:2 * HH] = (d_hidden * act).astype(BF16)
        CAT[rows, 2 * HH:HC] = (act * up).astype(BF16)
        return carry

    lax.fori_loop(0, 2 * ROWS // 64, activate, 0)

    def partials(yy):
        for ref, lo, hi in ((XT, 0, 256), (XT, 256, 512), (XT, 512, 768), (DT, 768, 1152)):
            got = jnp.dot(ref[yy], CAT[:, lo:hi], preferred_element_type=F32)
            T[yy, :, :, lo:hi] = got.astype(BF16).reshape(NZ, SH, hi - lo)

    nt = (((1,), (1,)), ((), ()))

    def outputs(side, write):
        rows = pl.ds(pl.multiple_of(side * ROWS, ROWS), ROWS)

        def tile(yy, carry):
            out = lax.dot_general(
                CAT[rows, 2 * HH:HC], W[yy, :, :, 2 * HH:HC].reshape(YB, HH), nt,
                preferred_element_type=F32,
            )
            write(0, yy, out)
            d_in = lax.dot_general(
                CAT[rows, 0:2 * HH], W[yy, :, :, 0:2 * HH].reshape(YB, 2 * HH), nt,
                preferred_element_type=F32,
            )
            write(1, yy, d_in)
            return carry

        lax.fori_loop(0, NY, tile, 0)

    order = (z2, zp, zm, z)
    partials(y2)
    for step, zz in enumerate(order):
        send(T.at[y2, zz, low], R1.at[0, step], S_RY1 + 2 * step, to_yp)
        send(T.at[y2, zz, high], R1.at[1, step], S_RY1 + 2 * step + 1, to_ym)

    def write_sibling(n, yy, value):
        OS[n, yy] = value.astype(BF16).reshape(NE, CAP, YB)

    outputs(o, write_sibling)
    for n in range(2):
        send(OS.at[n], OR.at[n], S_SO + n, sib)
    partials(yp)
    partials(ym)

    def second_y(step, zz):
        arrived(R1.at[0, step], S_RY1 + 2 * step)
        T[yp, zz, 0:64] = (T[yp, zz, 0:64].astype(F32) + R1[0, step].astype(F32)).astype(BF16)
        send(T.at[yp, zz], R2.at[0, step], S_RY2 + 2 * step, to_yp)
        arrived(R1.at[1, step], S_RY1 + 2 * step + 1)
        T[ym, zz, 64:128] = (T[ym, zz, 64:128].astype(F32) + R1[1, step].astype(F32)).astype(BF16)
        send(T.at[ym, zz], R2.at[1, step], S_RY2 + 2 * step + 1, to_ym)

    second_y(0, order[0])

    for n in range(2):
        arrived(OR.at[n], S_SO + n)

    def write_own(n, yy, value):
        value = value + OR[n, yy].reshape(ROWS, YB).astype(F32)
        BS[n, yy] = value.astype(BF16).reshape(NE, CAP, YB)

    outputs(c, write_own)
    for n, base in ((0, S_BO), (1, S_BI)):
        for k in range(1, NE):
            send(BS.at[n, :, peer(k)], BK.at[n, :, j], base + k, {"expert": peer(k)})
    local = []
    for n, base in ((0, S_BO), (1, S_BI)):
        copy = pltpu.make_async_copy(BS.at[n, :, j], BK.at[n, :, j], rs.at[base])
        copy.start()
        local.append(copy)

    second_y(1, order[1])
    partials(y)
    second_y(2, order[2])
    second_y(3, order[3])

    def summed_y(step, zz):
        arrived(R2.at[0, step], S_RY2 + 2 * step)
        arrived(R2.at[1, step], S_RY2 + 2 * step + 1)
        return T[y, zz].astype(F32) + R2[0, step].astype(F32) + R2[1, step].astype(F32)

    ZS[0] = summed_y(0, z2).astype(BF16)
    send(ZS.at[0, low], Z1.at[0], S_RZ1, to_zp)
    send(ZS.at[0, high], Z1.at[1], S_RZ1 + 1, to_zm)

    total = summed_y(1, zp)
    arrived(Z1.at[0], S_RZ1)
    ZS[1, 0:64] = (total[0:64] + Z1[0].astype(F32)).astype(BF16)
    ZS[1, 64:128] = total[64:128].astype(BF16)
    send(ZS.at[1], Z2.at[0], S_RZ2, to_zp)

    total = summed_y(2, zm)
    arrived(Z1.at[1], S_RZ1 + 1)
    ZS[2, 0:64] = total[0:64].astype(BF16)
    ZS[2, 64:128] = (total[64:128] + Z1[1].astype(F32)).astype(BF16)
    send(ZS.at[2], Z2.at[1], S_RZ2 + 1, to_zm)

    for n, base in ((0, S_BO), (1, S_BI)):
        local[n].wait()
        for k in range(1, NE):
            arrived(BK.at[n, :, source(k)], base + k)
    for yy in range(NY):
        back = BK[0, yy].reshape(ROWS, YB)
        out = sum(jnp.dot(SEL[n], back, preferred_element_type=F32) for n in (3, 2, 1))
        back = BK[1, yy].reshape(ROWS, YB)
        d_in = jnp.dot(SEL[0], back, preferred_element_type=F32)
        for zz in range(NZ):
            cols = slice((zz * 4 + yy) * SH, (zz * 4 + yy + 1) * SH)
            lo_ref[:, cols] = out[:, zz * SH:(zz + 1) * SH].astype(BF16)
            dt_ref[:, cols] = d_in[:, zz * SH:(zz + 1) * SH].astype(BF16)

    total = summed_y(3, z)
    arrived(Z2.at[0], S_RZ2)
    arrived(Z2.at[1], S_RZ2 + 1)
    total = total + Z2[0].astype(F32) + Z2[1].astype(F32)
    FS[...] = total.reshape(2, 64, HC)
    send(FS.at[o], FR, S_FIN, sib)
    for n, ref in enumerate((gg_ref, gu_ref, gd_ref)):
        ref[0, :, half_c] = FS[c, :, n * HH:(n + 1) * HH]
    arrived(FR, S_FIN)
    for n, ref in enumerate((gg_ref, gu_ref, gd_ref)):
        ref[0, :, half_o] = FR[:, n * HH:(n + 1) * HH]

    for copy in sent:
        copy.wait_send()


def shards(tokens, routes, gate_scale, w_gate, w_up, w_down, d_out):
    vm = pl.BlockSpec(memory_space=pltpu.VMEM)
    grad = jax.ShapeDtypeStruct(w_gate.shape, F32)
    rows = jax.ShapeDtypeStruct(tokens.shape, BF16)
    return pl.pallas_call(
        kernel,
        out_shape=(rows, rows, grad, grad, grad),
        in_specs=[vm] * 7,
        out_specs=(vm,) * 5,
        scratch_shapes=[
            pltpu.VMEM((NY, NZ, SH, HC), BF16),
            pltpu.VMEM((NY, 2 * NE, CAP, YB), BF16),
            pltpu.VMEM((NY, 2 * NE, CAP, YB), BF16),
            pltpu.VMEM((NY, YB, 2 * ROWS), BF16),
            pltpu.VMEM((NY, YB, 2 * ROWS), BF16),
            pltpu.VMEM((NY, NE, CAP, YB), BF16),
            pltpu.VMEM((NY, NE, CAP, YB), BF16),
            pltpu.VMEM((4, TOK, ROWS), BF16),
            pltpu.VMEM((2 * ROWS, HC), F32),
            pltpu.VMEM((2 * ROWS, HC), BF16),
            pltpu.VMEM((NY, NZ, SH, HC), BF16),
            pltpu.VMEM((2, NZ, 64, HC), BF16),
            pltpu.VMEM((2, NZ, SH, HC), BF16),
            pltpu.VMEM((2, 64, HC), BF16),
            pltpu.VMEM((2, SH, HC), BF16),
            pltpu.VMEM((3, SH, HC), BF16),
            pltpu.VMEM((2, 64, HC), F32),
            pltpu.VMEM((64, HC), F32),
            pltpu.VMEM((2, NY, NE, CAP, YB), BF16),
            pltpu.VMEM((2, NY, NE, CAP, YB), BF16),
            pltpu.VMEM((2, NY, NE, CAP, YB), BF16),
            pltpu.VMEM((2, NY, NE, CAP, YB), BF16),
            pltpu.SemaphoreType.DMA((S_ALL,)),
            pltpu.SemaphoreType.DMA((S_ALL,)),
        ],
        compiler_params=pltpu.CompilerParams(
            collective_id=0, has_side_effects=True, vmem_limit_bytes=60 * 1024 * 1024
        ),
    )(tokens, routes, gate_scale, w_gate, w_up, w_down, d_out)


def solution(mesh):
    tok = P(("dp", "expert"), None)
    wei = P("expert", "dp", None)
    return jax.shard_map(
        shards,
        mesh=mesh,
        in_specs=(tok, tok, tok, wei, wei, wei, tok),
        out_specs=(tok, tok, wei, wei, wei),
        check_vma=False,
    )
```

```python
import jax
import jax.numpy as jnp
from jax import lax
from jax.experimental import pallas as pl
from jax.experimental.pallas import tpu as pltpu
from jax.sharding import PartitionSpec as P

CAP = 32
MESH = pl.DeviceIdType.MESH
F32 = jnp.float32
BF16 = jnp.bfloat16

NY, NZ, SH = 4, 4, 128
HH = 384
HC = 3 * HH
YB = NZ * SH
NE = 8
TOK = 192
ROWS = NE * CAP

N_SEM = 128


def kernel(
    tok_ref, rt_ref, gs_ref, wg_ref, wu_ref, wd_ref, do_ref,
    lo_ref, dt_ref, gg_ref, gu_ref, gd_ref,
    W, X, D, XT, DT, SX, SD, SEL, ACC, CAT, T, R1, R2, Z1, Z2, ZS, FS, FR,
    OS, OR, BS, BK, ss, rs,
):
    i = lax.axis_index("dp")
    j = lax.axis_index("expert")
    c = lax.rem(i, 2)
    o = 1 - c
    p = lax.div(i, 2)
    y = lax.rem(p, 4)
    z = lax.div(p, 4)
    x = lax.div(j, 2)
    side = lax.rem(j, 2)
    yp, ym, y2 = lax.rem(y + 1, 4), lax.rem(y + 3, 4), lax.rem(y + 2, 4)
    zp, zm, z2 = lax.rem(z + 1, 4), lax.rem(z + 3, 4), lax.rem(z + 2, 4)
    zn = lax.rem(z + 3 + 2 * side, 4)

    def place(yy, zz, cc):
        return {"dp": (zz * 4 + yy) * 2 + cc}

    sib = place(y, z, o)
    up_y, down_y = place(yp, z, c), place(ym, z, c)
    up_z, down_z = place(y, zp, c), place(y, zm, c)

    near, far = pl.ds(0, 16), pl.ds(16, 16)

    def partners(q):
        to, fro = lax.rem(x + q, 4), lax.rem(x + 4 - q, 4)
        across = [
            (near, to * 2 + 1 - side, fro * 2 + 1 - side, {"expert": to * 2 + 1 - side}),
            (far, to * 2 + 1 - side, fro * 2 + 1 - side,
             {"dp": (zn * 4 + y) * 2 + c, "expert": to * 2 + 1 - side}),
        ]
        same = [(pl.ds(0, CAP), to * 2 + side, fro * 2 + side, {"expert": to * 2 + side})]
        return same if q else [], across

    numbers = {}

    def number(*name):
        return numbers.setdefault(name, len(numbers))

    sent = []

    def send(src, dst, name, to):
        k = number(*name)
        copy = pltpu.make_async_remote_copy(
            src_ref=src, dst_ref=dst, send_sem=ss.at[k], recv_sem=rs.at[k],
            device_id=to, device_id_type=MESH,
        )
        copy.start()
        sent.append(copy)

    def arrived(ref, *name):
        k = number(*name)
        pltpu.make_async_remote_copy(
            src_ref=ref, dst_ref=ref, send_sem=ss.at[k], recv_sem=rs.at[k],
            device_id=sib, device_id_type=MESH,
        ).wait_recv()

    barrier = pltpu.get_barrier_semaphore()
    greet = [sib, up_y, down_y, up_z, down_z]
    for q in range(4):
        same, across = partners(q)
        greet += [to for _, _, _, to in same + across]
    for to in greet:
        pl.semaphore_signal(barrier, inc=1, device_id=to, device_id_type=MESH)
    pl.semaphore_wait(barrier, len(greet))

    f = pl.ds(pl.multiple_of(c * 64, 64), 64)
    g = pl.ds(pl.multiple_of(o * 64, 64), 64)
    half_c = pl.ds(pl.multiple_of(c * HH, 128), HH)
    half_o = pl.ds(pl.multiple_of(o * HH, 128), HH)
    local = []
    for n, w_ref in enumerate((wg_ref, wu_ref, wd_ref)):
        cols = pl.ds(n * HH, HH)
        send(w_ref.at[0, :, half_o], W.at[y, z, f, cols], ("sib", n), sib)
        copy = pltpu.make_async_copy(
            w_ref.at[0, :, half_c], W.at[y, z, f, cols], rs.at[number("own", n)]
        )
        copy.start()
        local.append(copy)
    for copy in local:
        copy.wait()

    def along(yy, zz, piece, name, to):
        send(W.at[yy, zz, piece], W.at[yy, zz, piece], name, to)

    def here(yy, zz, piece, *name):
        arrived(W.at[yy, zz, piece], *name)

    along(y, z, f, ("gz", "f", "up"), up_z)
    along(y, z, f, ("gy", 0, "f", "up"), up_y)
    for n in range(3):
        arrived(W.at[y, z, g, pl.ds(n * HH, HH)], "sib", n)
    along(y, z, g, ("gz", "g", "down"), down_z)
    along(y, z, g, ("gy", 0, "g", "down"), down_y)
    along(y, z, g, ("gz", "g", "up"), up_z)
    along(y, z, g, ("gy", 0, "g", "up"), up_y)
    along(y, z, f, ("gz", "f", "down"), down_z)
    along(y, z, f, ("gy", 0, "f", "down"), down_y)

    shape = (TOK, ROWS)
    lane = lax.broadcasted_iota(jnp.int32, shape, 1)
    lane_e = lax.div(lane, CAP)
    lane_s = lax.rem(lane, CAP).astype(F32)
    scale = gs_ref[...]
    combine = scale / jnp.sum(scale, axis=1, keepdims=True)
    routes = rt_ref[...]
    named = jnp.zeros(shape, F32)
    weight = jnp.zeros(shape, F32)
    for s in range(6):
        same = routes[:, s:s + 1] == lane_e
        named = jnp.where(same, 1.0, named)
        weight = jnp.where(same, combine[:, s:s + 1], weight)
    earlier = (
        lax.broadcasted_iota(jnp.int32, (TOK, TOK), 1)
        < lax.broadcasted_iota(jnp.int32, (TOK, TOK), 0)
    ).astype(F32).astype(BF16)
    position = jnp.dot(earlier, named.astype(BF16), preferred_element_type=F32)
    chosen = jnp.where(position == lane_s, named, 0.0)
    weight = weight * chosen
    SEL[0] = chosen.astype(BF16)
    rest = weight
    for n in range(1, 4):
        part = rest.astype(BF16)
        SEL[n] = part
        rest = rest - part.astype(F32)

    tn = (((0,), (0,)), ((), ()))
    ones = jnp.ones((TOK, 128), BF16)
    slot_weight = sum(
        lax.dot_general(SEL[n], ones, tn, preferred_element_type=F32) for n in (3, 2, 1)
    )
    slot_weight = jnp.concatenate([slot_weight] * 4, axis=1)

    def columns(ref, yy):
        return jnp.concatenate(
            [ref[:, (zz * 4 + yy) * SH:(zz * 4 + yy + 1) * SH] for zz in range(NZ)], axis=1
        )

    for yy in range(NY):
        rows = lax.dot_general(SEL[0], columns(tok_ref, yy), tn, preferred_element_type=F32)
        SX[yy] = rows.astype(BF16).reshape(NE, CAP, YB)
        rows = lax.dot_general(SEL[0], columns(do_ref, yy), tn, preferred_element_type=F32)
        SD[yy] = (rows * slot_weight).astype(BF16).reshape(NE, CAP, YB)
    mine = c * NE + j
    rows_out = ((SX, X, "x"), (SD, D, "d"))

    def exchange(crossing):
        for src, dst, what in rows_out:
            for q in range(4):
                for rows, to, _, device in partners(q)[crossing]:
                    which = 0 if rows is near else 1
                    send(src.at[:, to, rows], dst.at[:, mine, rows],
                         ("to", what, crossing, q, which), device)

    exchange(0)
    local = []
    for src, dst, what in rows_out:
        copy = pltpu.make_async_copy(src.at[:, j], dst.at[:, mine], rs.at[number("keep", what)])
        copy.start()
        local.append(copy)

    def spread_y(step, zz, piece, kind):
        along(y, zz, piece, ("gy", step, kind, "up"), up_y)
        along(y, zz, piece, ("gy", step, kind, "down"), down_y)

    def onward_f(step, zz):
        here(ym, zz, f, "gy", step, "f", "up")
        along(ym, zz, f, ("gy", step, "f", "on"), up_y)

    def onward_g(step, zz):
        here(yp, zz, g, "gy", step, "g", "down")
        along(yp, zz, g, ("gy", step, "g", "on"), down_y)

    here(y, zm, f, "gz", "f", "up")
    along(y, zm, f, ("gz", "f", "on"), up_z)
    spread_y(1, zm, f, "f")
    here(y, zp, g, "gz", "g", "down")
    along(y, zp, g, ("gz", "g", "on"), down_z)
    spread_y(2, zp, g, "g")
    exchange(1)
    onward_f(0, z)
    onward_g(0, z)
    here(y, zm, g, "gz", "g", "up")
    spread_y(1, zm, g, "g")
    here(y, zp, f, "gz", "f", "down")
    spread_y(2, zp, f, "f")
    onward_f(1, zm)
    onward_g(2, zp)
    here(y, z2, f, "gz", "f", "on")
    spread_y(3, z2, f, "f")
    here(y, z2, g, "gz", "g", "on")
    spread_y(3, z2, g, "g")
    onward_g(1, zm)
    onward_f(2, zp)
    for n, (_, dst, what) in enumerate(rows_out):
        local[n].wait()
        for q in range(4):
            for crossing in range(2):
                for rows, _, fro, _ in partners(q)[crossing]:
                    which = 0 if rows is near else 1
                    arrived(dst.at[:, c * NE + fro, rows], "to", what, crossing, q, which)
        own = dst.at[:, pl.ds(c * NE, NE)]
        send(own, own, ("rows", what), sib)
    onward_f(3, z2)
    onward_g(3, z2)
    arrived(X.at[:, pl.ds(o * NE, NE)], "rows", "x")
    arrived(D.at[:, pl.ds(o * NE, NE)], "rows", "d")

    def turn(yy, carry):
        XT[yy] = X[yy].reshape(2 * ROWS, YB).T
        DT[yy] = D[yy].reshape(2 * ROWS, YB).T
        return carry

    lax.fori_loop(0, NY, turn, 0)

    def accumulate(yy, first):
        def tile(m, carry):
            rows = pl.ds(pl.multiple_of(m * ROWS, ROWS), ROWS)
            blocks = pl.ds(m * NE, NE)
            for ref, cols in ((X, (0, 256)), (X, (256, 512)), (X, (512, 768)), (D, (768, 1152))):
                lo, hi = cols
                got = jnp.dot(
                    ref[yy, blocks].reshape(ROWS, YB),
                    W[yy, :, :, lo:hi].reshape(YB, hi - lo),
                    preferred_element_type=F32,
                )
                if first:
                    ACC[rows, lo:hi] = got
                else:
                    ACC[rows, lo:hi] += got
            return carry

        lax.fori_loop(0, 2, tile, 0)
    accumulate(y, True)
    steps = ((0, z), (1, zm), (2, zp), (3, z2))
    for step, zz in steps:
        here(ym, zz, g, "gy", step, "g", "up")
    accumulate(ym, False)
    for step, zz in steps:
        here(yp, zz, f, "gy", step, "f", "down")
    accumulate(yp, False)
    for step, zz in steps:
        here(y2, zz, f, "gy", step, "f", "on")
        here(y2, zz, g, "gy", step, "g", "on")
    accumulate(y2, False)

    def activate(m, carry):
        rows = pl.ds(pl.multiple_of(m * 64, 64), 64)
        gate, up, d_hidden = ACC[rows, 0:HH], ACC[rows, HH:2 * HH], ACC[rows, 2 * HH:HC]
        sig = jax.nn.sigmoid(gate)
        act = gate * sig
        CAT[rows, 0:HH] = (d_hidden * up * sig * (1.0 + gate * (1.0 - sig))).astype(BF16)
        CAT[rows, HH:2 * HH] = (d_hidden * act).astype(BF16)
        CAT[rows, 2 * HH:HC] = (act * up).astype(BF16)
        return carry

    lax.fori_loop(0, 2 * ROWS // 64, activate, 0)

    def partials(yy):
        for ref, lo, hi in ((XT, 0, 256), (XT, 256, 512), (XT, 512, 768), (DT, 768, 1152)):
            got = jnp.dot(ref[yy], CAT[:, lo:hi], preferred_element_type=F32)
            T[yy, :, :, lo:hi] = got.astype(BF16).reshape(NZ, SH, hi - lo)

    nt = (((1,), (1,)), ((), ()))

    def outputs(side, write):
        rows = pl.ds(pl.multiple_of(side * ROWS, ROWS), ROWS)

        def tile(yy, carry):
            out = lax.dot_general(
                CAT[rows, 2 * HH:HC], W[yy, :, :, 2 * HH:HC].reshape(YB, HH), nt,
                preferred_element_type=F32,
            )
            write(0, yy, out)
            d_in = lax.dot_general(
                CAT[rows, 0:2 * HH], W[yy, :, :, 0:2 * HH].reshape(YB, 2 * HH), nt,
                preferred_element_type=F32,
            )
            write(1, yy, d_in)
            return carry

        lax.fori_loop(0, NY, tile, 0)

    def first_y(step, zz):
        send(T.at[y2, zz, f], R1.at[0, step], ("r1", step, "f"), up_y)
        send(T.at[y2, zz, g], R1.at[1, step], ("r1", step, "g"), down_y)

    def second_y(step, zz):
        send(T.at[yp, zz, g], R2.at[0, step, g], ("r2", step, "g", "up"), up_y)
        send(T.at[ym, zz, f], R2.at[1, step, f], ("r2", step, "f", "down"), down_y)

    def third_y(step, zz):
        arrived(R1.at[0, step], "r1", step, "f")
        T[yp, zz, f] = (T[yp, zz, f].astype(F32) + R1[0, step].astype(F32)).astype(BF16)
        send(T.at[yp, zz, f], R2.at[0, step, f], ("r2", step, "f", "up"), up_y)
        arrived(R1.at[1, step], "r1", step, "g")
        T[ym, zz, g] = (T[ym, zz, g].astype(F32) + R1[1, step].astype(F32)).astype(BF16)
        send(T.at[ym, zz, g], R2.at[1, step, g], ("r2", step, "g", "down"), down_y)

    partials(y2)
    first_y(0, z2)
    partials(yp)
    partials(ym)
    second_y(0, z2)
    first_y(1, zp)

    def write_sibling(n, yy, value):
        OS[n, yy] = value.astype(BF16).reshape(NE, CAP, YB)

    outputs(o, write_sibling)
    for n in range(2):
        send(OS.at[n], OR.at[n], ("part", n), sib)
    third_y(0, z2)
    first_y(2, zm)
    second_y(1, zp)
    second_y(2, zm)

    for n in range(2):
        arrived(OR.at[n], "part", n)

    def write_own(n, yy, value):
        value = value + OR[n, yy].reshape(ROWS, YB).astype(F32)
        BS[n, yy] = value.astype(BF16).reshape(NE, CAP, YB)

    outputs(c, write_own)
    for crossing in (1, 0):
        for n in range(2):
            for q in range(4):
                for rows, to, _, device in partners(q)[crossing]:
                    which = 0 if rows is near else 1
                    send(BS.at[n, :, to, rows], BK.at[n, :, j, rows],
                         ("back", n, crossing, q, which), device)
    local = []
    for n in range(2):
        copy = pltpu.make_async_copy(BS.at[n, :, j], BK.at[n, :, j], rs.at[number("stay", n)])
        copy.start()
        local.append(copy)

    third_y(1, zp)
    first_y(3, z)
    third_y(2, zm)
    second_y(3, z)
    partials(y)

    def summed_y(step, zz):
        for d in range(2):
            for piece, kind in ((f, "f"), (g, "g")):
                arrived(R2.at[d, step, piece], "r2", step, kind, ("up", "down")[d])
        return T[y, zz].astype(F32) + R2[0, step].astype(F32) + R2[1, step].astype(F32)

    ZS[0] = summed_y(0, z2).astype(BF16)
    send(ZS.at[0, f], Z1.at[0], ("z1", "f"), up_z)
    send(ZS.at[0, g], Z1.at[1], ("z1", "g"), down_z)
    third_y(3, z)

    def second_z(n, zz, late, early, name, to):
        FS[...] = summed_y(n, zz).reshape(2, 64, HC)
        (piece, at), (first, first_at) = late, early
        ZS[n, first] = FS[first_at].astype(BF16)
        send(ZS.at[n, first], Z2.at[n - 1, first], ("z2", n, 0), to)
        arrived(Z1.at[n - 1], "z1", name)
        ZS[n, piece] = (FS[at] + Z1[n - 1].astype(F32)).astype(BF16)
        send(ZS.at[n, piece], Z2.at[n - 1, piece], ("z2", n, 1), to)

    second_z(1, zp, (f, c), (g, o), "f", up_z)
    second_z(2, zm, (g, o), (f, c), "g", down_z)

    for n in range(2):
        local[n].wait()
        for q in range(4):
            for crossing in range(2):
                for rows, _, fro, _ in partners(q)[crossing]:
                    which = 0 if rows is near else 1
                    arrived(BK.at[n, :, fro, rows], "back", n, crossing, q, which)
    for yy in range(NY):
        back = BK[0, yy].reshape(ROWS, YB)
        out = sum(jnp.dot(SEL[n], back, preferred_element_type=F32) for n in (3, 2, 1))
        back = BK[1, yy].reshape(ROWS, YB)
        d_in = jnp.dot(SEL[0], back, preferred_element_type=F32)
        for zz in range(NZ):
            cols = slice((zz * 4 + yy) * SH, (zz * 4 + yy + 1) * SH)
            lo_ref[:, cols] = out[:, zz * SH:(zz + 1) * SH].astype(BF16)
            dt_ref[:, cols] = d_in[:, zz * SH:(zz + 1) * SH].astype(BF16)
    total = summed_y(3, z)
    arrived(Z2.at[0, g], "z2", 1, 0)
    arrived(Z2.at[0, f], "z2", 1, 1)
    arrived(Z2.at[1, f], "z2", 2, 0)
    arrived(Z2.at[1, g], "z2", 2, 1)
    total = total + Z2[0].astype(F32) + Z2[1].astype(F32)
    FS[...] = total.reshape(2, 64, HC)
    send(FS.at[o], FR, ("fin",), sib)
    for n, ref in enumerate((gg_ref, gu_ref, gd_ref)):
        ref[0, :, half_c] = FS[c, :, n * HH:(n + 1) * HH]
    arrived(FR, "fin")
    for n, ref in enumerate((gg_ref, gu_ref, gd_ref)):
        ref[0, :, half_o] = FR[:, n * HH:(n + 1) * HH]

    for copy in sent:
        copy.wait_send()
    assert len(numbers) <= N_SEM


def shards(tokens, routes, gate_scale, w_gate, w_up, w_down, d_out):
    vm = pl.BlockSpec(memory_space=pltpu.VMEM)
    grad = jax.ShapeDtypeStruct(w_gate.shape, F32)
    rows = jax.ShapeDtypeStruct(tokens.shape, BF16)
    return pl.pallas_call(
        kernel,
        out_shape=(rows, rows, grad, grad, grad),
        in_specs=[vm] * 7,
        out_specs=(vm,) * 5,
        scratch_shapes=[
            pltpu.VMEM((NY, NZ, SH, HC), BF16),
            pltpu.VMEM((NY, 2 * NE, CAP, YB), BF16),
            pltpu.VMEM((NY, 2 * NE, CAP, YB), BF16),
            pltpu.VMEM((NY, YB, 2 * ROWS), BF16),
            pltpu.VMEM((NY, YB, 2 * ROWS), BF16),
            pltpu.VMEM((NY, NE, CAP, YB), BF16),
            pltpu.VMEM((NY, NE, CAP, YB), BF16),
            pltpu.VMEM((4, TOK, ROWS), BF16),
            pltpu.VMEM((2 * ROWS, HC), F32),
            pltpu.VMEM((2 * ROWS, HC), BF16),
            pltpu.VMEM((NY, NZ, SH, HC), BF16),
            pltpu.VMEM((2, NZ, 64, HC), BF16),
            pltpu.VMEM((2, NZ, SH, HC), BF16),
            pltpu.VMEM((2, 64, HC), BF16),
            pltpu.VMEM((2, SH, HC), BF16),
            pltpu.VMEM((3, SH, HC), BF16),
            pltpu.VMEM((2, 64, HC), F32),
            pltpu.VMEM((64, HC), F32),
            pltpu.VMEM((2, NY, NE, CAP, YB), BF16),
            pltpu.VMEM((2, NY, NE, CAP, YB), BF16),
            pltpu.VMEM((2, NY, NE, CAP, YB), BF16),
            pltpu.VMEM((2, NY, NE, CAP, YB), BF16),
            pltpu.SemaphoreType.DMA((N_SEM,)),
            pltpu.SemaphoreType.DMA((N_SEM,)),
        ],
        compiler_params=pltpu.CompilerParams(
            collective_id=0, has_side_effects=True, vmem_limit_bytes=60 * 1024 * 1024
        ),
    )(tokens, routes, gate_scale, w_gate, w_up, w_down, d_out)


def solution(mesh):
    tok = P(("dp", "expert"), None)
    wei = P("expert", "dp", None)
    return jax.shard_map(
        shards,
        mesh=mesh,
        in_specs=(tok, tok, tok, wei, wei, wei, tok),
        out_specs=(tok, tok, wei, wei, wei),
        check_vma=False,
    )
```

```python
import jax
import jax.numpy as jnp
from jax import lax
from jax.experimental import pallas as pl
from jax.experimental.pallas import tpu as pltpu
from jax.sharding import PartitionSpec as P

CAP = 32
MESH = pl.DeviceIdType.MESH
F32 = jnp.float32
BF16 = jnp.bfloat16

NY, NZ, SH = 4, 4, 128
HH = 384
HC = 3 * HH
YB = NZ * SH
NE = 8
TOK = 192
ROWS = NE * CAP

N_SEM = 128
VMEM_MB = 50


def kernel(
    tok_hbm, rt_hbm, gs_hbm, wg_ref, wu_ref, wd_ref, do_hbm,
    lo_ref, dt_ref, gg_ref, gu_ref, gd_ref,
    W, X, D, XT, DT, SX, SD, SEL, ACC, CAT, T, R1, R2, Z1, Z2, ZS, FS, FR,
    OS, OR, BS, BK, tok_ref, do_ref, rt_ref, gs_ref, ss, rs,
):
    i = lax.axis_index("dp")
    j = lax.axis_index("expert")
    c = lax.rem(i, 2)
    o = 1 - c
    p = lax.div(i, 2)
    y = lax.rem(p, 4)
    z = lax.div(p, 4)
    x = lax.div(j, 2)
    side = lax.rem(j, 2)
    yp, ym, y2 = lax.rem(y + 1, 4), lax.rem(y + 3, 4), lax.rem(y + 2, 4)
    zp, zm, z2 = lax.rem(z + 1, 4), lax.rem(z + 3, 4), lax.rem(z + 2, 4)
    zn = lax.rem(z + 3 + 2 * side, 4)

    def place(yy, zz, cc):
        return {"dp": (zz * 4 + yy) * 2 + cc}

    sib = place(y, z, o)
    up_y, down_y = place(yp, z, c), place(ym, z, c)
    up_z, down_z = place(y, zp, c), place(y, zm, c)

    near, far = pl.ds(0, 16), pl.ds(16, 16)

    def partners(q):
        to, fro = lax.rem(x + q, 4), lax.rem(x + 4 - q, 4)
        across = [
            (near, to * 2 + 1 - side, fro * 2 + 1 - side, {"expert": to * 2 + 1 - side}),
            (far, to * 2 + 1 - side, fro * 2 + 1 - side,
             {"dp": (zn * 4 + y) * 2 + c, "expert": to * 2 + 1 - side}),
        ]
        same = [(pl.ds(0, CAP), to * 2 + side, fro * 2 + side, {"expert": to * 2 + side})]
        return same if q else [], across

    numbers = {}

    def number(*name):
        return numbers.setdefault(name, len(numbers))

    sent = []

    def send(src, dst, name, to):
        k = number(*name)
        copy = pltpu.make_async_remote_copy(
            src_ref=src, dst_ref=dst, send_sem=ss.at[k], recv_sem=rs.at[k],
            device_id=to, device_id_type=MESH,
        )
        copy.start()
        sent.append(copy)

    def arrived(ref, *name):
        k = number(*name)
        pltpu.make_async_remote_copy(
            src_ref=ref, dst_ref=ref, send_sem=ss.at[k], recv_sem=rs.at[k],
            device_id=sib, device_id_type=MESH,
        ).wait_recv()

    loads = []
    for src, dst, what in (
        (rt_hbm, rt_ref, "r"), (gs_hbm, gs_ref, "s"), (tok_hbm, tok_ref, "x"), (do_hbm, do_ref, "d")
    ):
        copy = pltpu.make_async_copy(src, dst, rs.at[number("load", what)])
        copy.start()
        loads.append(copy)
    barrier = pltpu.get_barrier_semaphore()
    greet = [sib, up_y, down_y, up_z, down_z]
    for q in range(4):
        same, across = partners(q)
        greet += [to for _, _, _, to in same + across]
    for to in greet:
        pl.semaphore_signal(barrier, inc=1, device_id=to, device_id_type=MESH)
    pl.semaphore_wait(barrier, len(greet))

    f = pl.ds(pl.multiple_of(c * 64, 64), 64)
    g = pl.ds(pl.multiple_of(o * 64, 64), 64)
    half_c = pl.ds(pl.multiple_of(c * HH, 128), HH)
    half_o = pl.ds(pl.multiple_of(o * HH, 128), HH)
    local = []
    for n, w_ref in enumerate((wg_ref, wu_ref, wd_ref)):
        cols = pl.ds(n * HH, HH)
        send(w_ref.at[0, :, half_o], W.at[y, z, f, cols], ("sib", n), sib)
        copy = pltpu.make_async_copy(
            w_ref.at[0, :, half_c], W.at[y, z, f, cols], rs.at[number("own", n)]
        )
        copy.start()
        local.append(copy)
    for copy in local:
        copy.wait()

    def along(yy, zz, piece, name, to):
        send(W.at[yy, zz, piece], W.at[yy, zz, piece], name, to)

    def here(yy, zz, piece, *name):
        arrived(W.at[yy, zz, piece], *name)

    along(y, z, f, ("gz", "f", "up"), up_z)
    along(y, z, f, ("gy", 0, "f", "up"), up_y)
    for n in range(3):
        arrived(W.at[y, z, g, pl.ds(n * HH, HH)], "sib", n)
    along(y, z, g, ("gz", "g", "down"), down_z)
    along(y, z, g, ("gy", 0, "g", "down"), down_y)
    along(y, z, g, ("gz", "g", "up"), up_z)
    along(y, z, g, ("gy", 0, "g", "up"), up_y)
    along(y, z, f, ("gz", "f", "down"), down_z)
    along(y, z, f, ("gy", 0, "f", "down"), down_y)

    shape = (ROWS, TOK)
    row = lax.broadcasted_iota(jnp.int32, shape, 0)
    row_e = lax.div(row, CAP)
    row_s = lax.rem(row, CAP).astype(F32)
    for copy in loads[:2]:
        copy.wait()
    scale = gs_ref[...]
    combine = scale / jnp.sum(scale, axis=0, keepdims=True)
    routes = rt_ref[...]
    named = jnp.zeros(shape, F32)
    weight = jnp.zeros(shape, F32)
    for s in range(6):
        same = routes[s:s + 1, :] == row_e
        named = jnp.where(same, 1.0, named)
        weight = jnp.where(same, combine[s:s + 1, :], weight)
    earlier = (
        lax.broadcasted_iota(jnp.int32, (TOK, TOK), 0)
        < lax.broadcasted_iota(jnp.int32, (TOK, TOK), 1)
    ).astype(F32).astype(BF16)
    position = jnp.dot(named.astype(BF16), earlier, preferred_element_type=F32)
    chosen = jnp.where(position == row_s, named, 0.0)
    weight = weight * chosen
    slot_weight = jnp.sum(weight, axis=1, keepdims=True)
    select = chosen.astype(BF16)
    SEL[0] = select
    rest = weight
    for n in range(1, 4):
        part = rest.astype(BF16)
        SEL[n] = part
        rest = rest - part.astype(F32)

    def columns(ref, yy):
        return jnp.concatenate(
            [ref[:, (zz * 4 + yy) * SH:(zz * 4 + yy + 1) * SH] for zz in range(NZ)], axis=1
        )

    for copy in loads[2:]:
        copy.wait()
    for yy in range(NY):
        rows = jnp.dot(select, columns(tok_ref, yy), preferred_element_type=F32)
        SX[yy] = rows.astype(BF16).reshape(NE, CAP, YB)
        rows = jnp.dot(select, columns(do_ref, yy), preferred_element_type=F32)
        SD[yy] = (rows * slot_weight).astype(BF16).reshape(NE, CAP, YB)

    mine = c * NE + j
    rows_out = ((SX, X, "x"), (SD, D, "d"))

    def exchange(crossing):
        for src, dst, what in rows_out:
            for q in range(4):
                for rows, to, _, device in partners(q)[crossing]:
                    which = 0 if rows is near else 1
                    send(src.at[:, to, rows], dst.at[:, mine, rows],
                         ("to", what, crossing, q, which), device)

    exchange(0)
    local = []
    for src, dst, what in rows_out:
        copy = pltpu.make_async_copy(src.at[:, j], dst.at[:, mine], rs.at[number("keep", what)])
        copy.start()
        local.append(copy)

    def spread_y(step, zz, piece, kind):
        along(y, zz, piece, ("gy", step, kind, "up"), up_y)
        along(y, zz, piece, ("gy", step, kind, "down"), down_y)

    def onward_f(step, zz):
        here(ym, zz, f, "gy", step, "f", "up")
        along(ym, zz, f, ("gy", step, "f", "on"), up_y)

    def onward_g(step, zz):
        here(yp, zz, g, "gy", step, "g", "down")
        along(yp, zz, g, ("gy", step, "g", "on"), down_y)

    here(y, zm, f, "gz", "f", "up")
    along(y, zm, f, ("gz", "f", "on"), up_z)
    spread_y(1, zm, f, "f")
    here(y, zp, g, "gz", "g", "down")
    along(y, zp, g, ("gz", "g", "on"), down_z)
    spread_y(2, zp, g, "g")
    exchange(1)
    onward_f(0, z)
    onward_g(0, z)
    here(y, zm, g, "gz", "g", "up")
    spread_y(1, zm, g, "g")
    here(y, zp, f, "gz", "f", "down")
    spread_y(2, zp, f, "f")
    onward_f(1, zm)
    onward_g(2, zp)
    here(y, z2, f, "gz", "f", "on")
    spread_y(3, z2, f, "f")
    here(y, z2, g, "gz", "g", "on")
    spread_y(3, z2, g, "g")
    onward_g(1, zm)
    onward_f(2, zp)
    for n, (_, dst, what) in enumerate(rows_out):
        local[n].wait()
        for q in range(4):
            for crossing in range(2):
                for rows, _, fro, _ in partners(q)[crossing]:
                    which = 0 if rows is near else 1
                    arrived(dst.at[:, c * NE + fro, rows], "to", what, crossing, q, which)
        own = dst.at[:, pl.ds(c * NE, NE)]
        send(own, own, ("rows", what), sib)
    onward_f(3, z2)
    onward_g(3, z2)
    def turn(m):
        def body(yy, carry):
            cols = pl.ds(pl.multiple_of(m * ROWS, ROWS), ROWS)
            blocks = pl.ds(m * NE, NE)
            XT[yy, :, cols] = X[yy, blocks].reshape(ROWS, YB).T
            DT[yy, :, cols] = D[yy, blocks].reshape(ROWS, YB).T
            return carry

        lax.fori_loop(0, NY, body, 0)

    def accumulate(yy, m, first):
        rows = pl.ds(pl.multiple_of(m * ROWS, ROWS), ROWS)
        blocks = pl.ds(m * NE, NE)
        for ref, lo, hi in ((X, 0, 256), (X, 256, 512), (X, 512, 768), (D, 768, 1152)):
            got = jnp.dot(
                ref[yy, blocks].reshape(ROWS, YB),
                W[yy, :, :, lo:hi].reshape(YB, hi - lo),
                preferred_element_type=F32,
            )
            if first:
                ACC[rows, lo:hi] = got
            else:
                ACC[rows, lo:hi] += got

    steps = ((0, z), (1, zm), (2, zp), (3, z2))
    turn(c)
    accumulate(y, c, True)
    for step, zz in steps:
        here(ym, zz, g, "gy", step, "g", "up")
    accumulate(ym, c, False)
    for step, zz in steps:
        here(yp, zz, f, "gy", step, "f", "down")
    accumulate(yp, c, False)
    arrived(X.at[:, pl.ds(o * NE, NE)], "rows", "x")
    arrived(D.at[:, pl.ds(o * NE, NE)], "rows", "d")
    turn(o)
    accumulate(y, o, True)
    accumulate(ym, o, False)
    accumulate(yp, o, False)
    for step, zz in steps:
        here(y2, zz, f, "gy", step, "f", "on")
        here(y2, zz, g, "gy", step, "g", "on")
    accumulate(y2, c, False)
    accumulate(y2, o, False)

    def activate(m, carry):
        rows = pl.ds(pl.multiple_of(m * 64, 64), 64)
        gate, up, d_hidden = ACC[rows, 0:HH], ACC[rows, HH:2 * HH], ACC[rows, 2 * HH:HC]
        sig = jax.nn.sigmoid(gate)
        act = gate * sig
        CAT[rows, 0:HH] = (d_hidden * up * sig * (1.0 + gate * (1.0 - sig))).astype(BF16)
        CAT[rows, HH:2 * HH] = (d_hidden * act).astype(BF16)
        CAT[rows, 2 * HH:HC] = (act * up).astype(BF16)
        return carry

    lax.fori_loop(0, 2 * ROWS // 64, activate, 0)

    def partials(yy):
        for ref, lo, hi in ((XT, 0, 256), (XT, 256, 512), (XT, 512, 768), (DT, 768, 1152)):
            got = jnp.dot(ref[yy], CAT[:, lo:hi], preferred_element_type=F32)
            T[yy, :, :, lo:hi] = got.astype(BF16).reshape(NZ, SH, hi - lo)

    nt = (((1,), (1,)), ((), ()))

    def outputs(side, write):
        rows = pl.ds(pl.multiple_of(side * ROWS, ROWS), ROWS)

        def tile(yy, carry):
            out = lax.dot_general(
                CAT[rows, 2 * HH:HC], W[yy, :, :, 2 * HH:HC].reshape(YB, HH), nt,
                preferred_element_type=F32,
            )
            write(0, yy, out)
            d_in = lax.dot_general(
                CAT[rows, 0:2 * HH], W[yy, :, :, 0:2 * HH].reshape(YB, 2 * HH), nt,
                preferred_element_type=F32,
            )
            write(1, yy, d_in)
            return carry

        lax.fori_loop(0, NY, tile, 0)

    def first_f(step, zz):
        send(T.at[y2, zz, f], R1.at[0, step], ("r1", step, "f"), up_y)

    def first_g(step, zz):
        send(T.at[y2, zz, g], R1.at[1, step], ("r1", step, "g"), down_y)

    def plain_g(step, zz):
        send(T.at[yp, zz, g], R2.at[0, step, g], ("r2", step, "g", "up"), up_y)

    def plain_f(step, zz):
        send(T.at[ym, zz, f], R2.at[1, step, f], ("r2", step, "f", "down"), down_y)

    def joined_f(step, zz):
        arrived(R1.at[0, step], "r1", step, "f")
        T[yp, zz, f] = (T[yp, zz, f].astype(F32) + R1[0, step].astype(F32)).astype(BF16)
        send(T.at[yp, zz, f], R2.at[0, step, f], ("r2", step, "f", "up"), up_y)

    def joined_g(step, zz):
        arrived(R1.at[1, step], "r1", step, "g")
        T[ym, zz, g] = (T[ym, zz, g].astype(F32) + R1[1, step].astype(F32)).astype(BF16)
        send(T.at[ym, zz, g], R2.at[1, step, g], ("r2", step, "g", "down"), down_y)

    partials(y2)
    first_f(0, z2)
    first_g(0, z2)
    partials(yp)
    partials(ym)
    plain_g(0, z2)
    plain_f(0, z2)
    first_f(1, zp)
    first_g(2, zm)

    def write_sibling(n, yy, value):
        OS[n, yy] = value.astype(BF16).reshape(NE, CAP, YB)

    outputs(o, write_sibling)
    for n in range(2):
        send(OS.at[n], OR.at[n], ("part", n), sib)
    joined_f(0, z2)
    joined_g(0, z2)
    first_f(2, zm)
    first_g(1, zp)
    plain_g(2, zm)
    plain_f(1, zp)
    plain_g(1, zp)
    plain_f(2, zm)

    for n in range(2):
        arrived(OR.at[n], "part", n)

    def write_own(n, yy, value):
        value = value + OR[n, yy].reshape(ROWS, YB).astype(F32)
        BS[n, yy] = value.astype(BF16).reshape(NE, CAP, YB)

    outputs(c, write_own)
    for crossing in (1, 0):
        for n in range(2):
            for q in range(4):
                for rows, to, _, device in partners(q)[crossing]:
                    which = 0 if rows is near else 1
                    send(BS.at[n, :, to, rows], BK.at[n, :, j, rows],
                         ("back", n, crossing, q, which), device)
    local = []
    for n in range(2):
        copy = pltpu.make_async_copy(BS.at[n, :, j], BK.at[n, :, j], rs.at[number("stay", n)])
        copy.start()
        local.append(copy)

    partials(y)
    joined_f(1, zp)
    joined_g(2, zm)
    joined_f(2, zm)
    joined_g(1, zp)
    first_f(3, z)
    first_g(3, z)
    plain_g(3, z)
    plain_f(3, z)

    def summed_y(step, zz, piece, kind):
        for d in range(2):
            arrived(R2.at[d, step, piece], "r2", step, kind, ("up", "down")[d])
        return (
            T[y, zz, piece].astype(F32)
            + R2[0, step, piece].astype(F32)
            + R2[1, step, piece].astype(F32)
        )

    ZS[0, f] = summed_y(0, z2, f, "f").astype(BF16)
    send(ZS.at[0, f], Z1.at[0], ("z1", "f"), up_z)
    ZS[0, g] = summed_y(0, z2, g, "g").astype(BF16)
    send(ZS.at[0, g], Z1.at[1], ("z1", "g"), down_z)
    total = summed_y(1, zp, f, "f")
    arrived(Z1.at[0], "z1", "f")
    ZS[1, f] = (total + Z1[0].astype(F32)).astype(BF16)
    send(ZS.at[1, f], Z2.at[0, f], ("z2", "f", "up"), up_z)
    total = summed_y(2, zm, g, "g")
    arrived(Z1.at[1], "z1", "g")
    ZS[2, g] = (total + Z1[1].astype(F32)).astype(BF16)
    send(ZS.at[2, g], Z2.at[1, g], ("z2", "g", "down"), down_z)
    ZS[2, f] = summed_y(2, zm, f, "f").astype(BF16)
    send(ZS.at[2, f], Z2.at[1, f], ("z2", "f", "down"), down_z)
    ZS[1, g] = summed_y(1, zp, g, "g").astype(BF16)
    send(ZS.at[1, g], Z2.at[0, g], ("z2", "g", "up"), up_z)
    joined_f(3, z)
    joined_g(3, z)

    for n in range(2):
        local[n].wait()
        for q in range(4):
            for crossing in range(2):
                for rows, _, fro, _ in partners(q)[crossing]:
                    which = 0 if rows is near else 1
                    arrived(BK.at[n, :, fro, rows], "back", n, crossing, q, which)
    tn = (((0,), (0,)), ((), ()))
    for yy in range(NY):
        back = BK[0, yy].reshape(ROWS, YB)
        out = sum(
            lax.dot_general(SEL[n], back, tn, preferred_element_type=F32) for n in (3, 2, 1)
        )
        back = BK[1, yy].reshape(ROWS, YB)
        d_in = lax.dot_general(SEL[0], back, tn, preferred_element_type=F32)
        for zz in range(NZ):
            cols = slice((zz * 4 + yy) * SH, (zz * 4 + yy + 1) * SH)
            lo_ref[:, cols] = out[:, zz * SH:(zz + 1) * SH].astype(BF16)
            dt_ref[:, cols] = d_in[:, zz * SH:(zz + 1) * SH].astype(BF16)

    def total_z(piece, kind):
        total = summed_y(3, z, piece, kind)
        arrived(Z2.at[0, piece], "z2", kind, "up")
        arrived(Z2.at[1, piece], "z2", kind, "down")
        return total + Z2[0, piece].astype(F32) + Z2[1, piece].astype(F32)

    FS[...] = total_z(g, "g")
    send(FS, FR, ("fin",), sib)
    total = total_z(f, "f")
    for n, ref in enumerate((gg_ref, gu_ref, gd_ref)):
        ref[0, :, half_c] = total[:, n * HH:(n + 1) * HH]
    arrived(FR, "fin")
    for n, ref in enumerate((gg_ref, gu_ref, gd_ref)):
        ref[0, :, half_o] = FR[:, n * HH:(n + 1) * HH]

    for copy in sent:
        copy.wait_send()
    assert len(numbers) <= N_SEM


def hand_out(*refs):
    count = len(refs) // 2
    done = refs[-1]
    copies = [
        pltpu.make_async_copy(refs[n], refs[count + n], done.at[n]) for n in range(count)
    ]
    for copy in copies:
        copy.start()
    for copy in copies:
        copy.wait()


def shards(tokens, routes, gate_scale, w_gate, w_up, w_down, d_out):
    vm = pl.BlockSpec(memory_space=pltpu.VMEM)
    hbm = pl.BlockSpec(memory_space=pltpu.HBM)
    grad = jax.ShapeDtypeStruct(w_gate.shape, F32)
    rows = jax.ShapeDtypeStruct(tokens.shape, BF16)
    results = (rows, rows, grad, grad, grad)
    found = pl.pallas_call(
        kernel,
        out_shape=results,
        in_specs=[hbm] * 7,
        out_specs=(vm,) * 5,
        scratch_shapes=[
            pltpu.VMEM((NY, NZ, SH, HC), BF16),
            pltpu.VMEM((NY, 2 * NE, CAP, YB), BF16),
            pltpu.VMEM((NY, 2 * NE, CAP, YB), BF16),
            pltpu.VMEM((NY, YB, 2 * ROWS), BF16),
            pltpu.VMEM((NY, YB, 2 * ROWS), BF16),
            pltpu.VMEM((NY, NE, CAP, YB), BF16),
            pltpu.VMEM((NY, NE, CAP, YB), BF16),
            pltpu.VMEM((4, ROWS, TOK), BF16),
            pltpu.VMEM((2 * ROWS, HC), F32),
            pltpu.VMEM((2 * ROWS, HC), BF16),
            pltpu.VMEM((NY, NZ, SH, HC), BF16),
            pltpu.VMEM((2, NZ, 64, HC), BF16),
            pltpu.VMEM((2, NZ, SH, HC), BF16),
            pltpu.VMEM((2, 64, HC), BF16),
            pltpu.VMEM((2, SH, HC), BF16),
            pltpu.VMEM((3, SH, HC), BF16),
            pltpu.VMEM((64, HC), F32),
            pltpu.VMEM((64, HC), F32),
            pltpu.VMEM((2, NY, NE, CAP, YB), BF16),
            pltpu.VMEM((2, NY, NE, CAP, YB), BF16),
            pltpu.VMEM((2, NY, NE, CAP, YB), BF16),
            pltpu.VMEM((2, NY, NE, CAP, YB), BF16),
            pltpu.VMEM(tokens.shape, BF16),
            pltpu.VMEM(tokens.shape, BF16),
            pltpu.VMEM(routes.shape[::-1], jnp.int32),
            pltpu.VMEM(routes.shape[::-1], F32),
            pltpu.SemaphoreType.DMA((N_SEM,)),
            pltpu.SemaphoreType.DMA((N_SEM,)),
        ],
        compiler_params=pltpu.CompilerParams(
            collective_id=0, has_side_effects=True, vmem_limit_bytes=VMEM_MB * 1024 * 1024
        ),
    )(*(
        pltpu.with_memory_space_constraint(value, pltpu.HBM)
        for value in (tokens, routes.T, gate_scale.T, w_gate, w_up, w_down, d_out)
    ))
    return pl.pallas_call(
        hand_out,
        out_shape=results,
        in_specs=[vm] * 5,
        out_specs=(hbm,) * 5,
        scratch_shapes=[pltpu.SemaphoreType.DMA((5,))],
        compiler_params=pltpu.CompilerParams(vmem_limit_bytes=8 * 1024 * 1024),
    )(*found)


def solution(mesh):
    tok = P(("dp", "expert"), None)
    wei = P("expert", "dp", None)
    return jax.shard_map(
        shards,
        mesh=mesh,
        in_specs=(tok, tok, tok, wei, wei, wei, tok),
        out_specs=(tok, tok, wei, wei, wei),
        check_vma=False,
    )
```

```python
import jax
import jax.numpy as jnp
from jax import lax
from jax.experimental import pallas as pl
from jax.experimental.pallas import tpu as pltpu
from jax.sharding import PartitionSpec as P

CAP = 32
MESH = pl.DeviceIdType.MESH
F32 = jnp.float32
BF16 = jnp.bfloat16

NY, NZ, SH = 4, 4, 128
HH = 384
HC = 3 * HH
YB = NZ * SH
NE = 8
TOK = 192
ROWS = NE * CAP

N_SEM = 128
VMEM_MB = 50


def kernel(
    tok_hbm, rt_hbm, gs_hbm, wg_ref, wu_ref, wd_ref, do_hbm,
    lo_ref, dt_ref, gg_ref, gu_ref, gd_ref,
    W, X, D, XT, DT, SX, SD, SEL, ACC, CAT, T, R1, R2, Z1, Z2, ZS, FS, FR,
    OS, OR, BS, BK, tok_ref, do_ref, rt_ref, gs_ref, ss, rs,
):
    i = lax.axis_index("dp")
    j = lax.axis_index("expert")
    c = lax.rem(i, 2)
    o = 1 - c
    p = lax.div(i, 2)
    y = lax.rem(p, 4)
    z = lax.div(p, 4)
    x = lax.div(j, 2)
    side = lax.rem(j, 2)
    yp, ym, y2 = lax.rem(y + 1, 4), lax.rem(y + 3, 4), lax.rem(y + 2, 4)
    zp, zm, z2 = lax.rem(z + 1, 4), lax.rem(z + 3, 4), lax.rem(z + 2, 4)
    zn = lax.rem(z + 3 + 2 * side, 4)

    def place(yy, zz, cc):
        return {"dp": (zz * 4 + yy) * 2 + cc}

    sib = place(y, z, o)
    up_y, down_y = place(yp, z, c), place(ym, z, c)
    up_z, down_z = place(y, zp, c), place(y, zm, c)

    near, far = pl.ds(0, 16), pl.ds(16, 16)

    def partners(q):
        to, fro = lax.rem(x + q, 4), lax.rem(x + 4 - q, 4)
        across = [
            (near, to * 2 + 1 - side, fro * 2 + 1 - side, {"expert": to * 2 + 1 - side}),
            (far, to * 2 + 1 - side, fro * 2 + 1 - side,
             {"dp": (zn * 4 + y) * 2 + c, "expert": to * 2 + 1 - side}),
        ]
        same = [(pl.ds(0, CAP), to * 2 + side, fro * 2 + side, {"expert": to * 2 + side})]
        return same if q else [], across

    numbers = {}

    def number(*name):
        return numbers.setdefault(name, len(numbers))

    sent = []

    def send(src, dst, name, to):
        k = number(*name)
        copy = pltpu.make_async_remote_copy(
            src_ref=src, dst_ref=dst, send_sem=ss.at[k], recv_sem=rs.at[k],
            device_id=to, device_id_type=MESH,
        )
        copy.start()
        sent.append(copy)

    def arrived(ref, *name):
        k = number(*name)
        pltpu.make_async_remote_copy(
            src_ref=ref, dst_ref=ref, send_sem=ss.at[k], recv_sem=rs.at[k],
            device_id=sib, device_id_type=MESH,
        ).wait_recv()

    loads = []
    for src, dst, what in (
        (rt_hbm, rt_ref, "r"), (gs_hbm, gs_ref, "s"), (tok_hbm, tok_ref, "x"), (do_hbm, do_ref, "d")
    ):
        copy = pltpu.make_async_copy(src, dst, rs.at[number("load", what)])
        copy.start()
        loads.append(copy)
    barrier = pltpu.get_barrier_semaphore()
    greet = [sib, up_y, down_y, up_z, down_z]
    for q in range(4):
        same, across = partners(q)
        greet += [to for _, _, _, to in same + across]
    for to in greet:
        pl.semaphore_signal(barrier, inc=1, device_id=to, device_id_type=MESH)
    pl.semaphore_wait(barrier, len(greet))

    f = pl.ds(pl.multiple_of(c * 64, 64), 64)
    g = pl.ds(pl.multiple_of(o * 64, 64), 64)
    half_c = pl.ds(pl.multiple_of(c * HH, 128), HH)
    half_o = pl.ds(pl.multiple_of(o * HH, 128), HH)
    local = []
    for n, w_ref in enumerate((wg_ref, wu_ref, wd_ref)):
        cols = pl.ds(n * HH, HH)
        send(w_ref.at[0, :, half_o], W.at[y, z, f, cols], ("sib", n), sib)
        copy = pltpu.make_async_copy(
            w_ref.at[0, :, half_c], W.at[y, z, f, cols], rs.at[number("own", n)]
        )
        copy.start()
        local.append(copy)
    for copy in local:
        copy.wait()

    def along(yy, zz, piece, name, to):
        send(W.at[yy, zz, piece], W.at[yy, zz, piece], name, to)

    def here(yy, zz, piece, *name):
        arrived(W.at[yy, zz, piece], *name)

    along(y, z, f, ("gz", "f", "up"), up_z)
    along(y, z, f, ("gy", 0, "f", "up"), up_y)
    for n in range(3):
        arrived(W.at[y, z, g, pl.ds(n * HH, HH)], "sib", n)
    along(y, z, g, ("gz", "g", "down"), down_z)
    along(y, z, g, ("gy", 0, "g", "down"), down_y)
    along(y, z, g, ("gz", "g", "up"), up_z)
    along(y, z, g, ("gy", 0, "g", "up"), up_y)
    along(y, z, f, ("gz", "f", "down"), down_z)
    along(y, z, f, ("gy", 0, "f", "down"), down_y)

    shape = (ROWS, TOK)
    row = lax.broadcasted_iota(jnp.int32, shape, 0)
    row_e = lax.div(row, CAP)
    row_s = lax.rem(row, CAP).astype(F32)
    for copy in loads[:2]:
        copy.wait()
    scale = gs_ref[...]
    combine = scale / jnp.sum(scale, axis=0, keepdims=True)
    routes = rt_ref[...]
    named = jnp.zeros(shape, F32)
    weight = jnp.zeros(shape, F32)
    for s in range(6):
        same = routes[s:s + 1, :] == row_e
        named = jnp.where(same, 1.0, named)
        weight = jnp.where(same, combine[s:s + 1, :], weight)
    earlier = (
        lax.broadcasted_iota(jnp.int32, (TOK, TOK), 0)
        < lax.broadcasted_iota(jnp.int32, (TOK, TOK), 1)
    ).astype(F32).astype(BF16)
    position = jnp.dot(named.astype(BF16), earlier, preferred_element_type=F32)
    chosen = jnp.where(position == row_s, named, 0.0)
    weight = weight * chosen
    slot_weight = jnp.sum(weight, axis=1, keepdims=True)
    select = chosen.astype(BF16)
    SEL[0] = select
    rest = weight
    for n in range(1, 4):
        part = rest.astype(BF16)
        SEL[n] = part
        rest = rest - part.astype(F32)

    def columns(ref, yy):
        return jnp.concatenate(
            [ref[:, (zz * 4 + yy) * SH:(zz * 4 + yy + 1) * SH] for zz in range(NZ)], axis=1
        )

    for copy in loads[2:]:
        copy.wait()
    for yy in range(NY):
        rows = jnp.dot(select, columns(tok_ref, yy), preferred_element_type=F32)
        SX[yy] = rows.astype(BF16).reshape(NE, CAP, YB)
        rows = jnp.dot(select, columns(do_ref, yy), preferred_element_type=F32)
        SD[yy] = (rows * slot_weight).astype(BF16).reshape(NE, CAP, YB)

    mine = c * NE + j
    rows_out = ((SX, X, "x"), (SD, D, "d"))

    def exchange(crossing):
        for src, dst, what in rows_out:
            for q in range(4):
                for rows, to, _, device in partners(q)[crossing]:
                    which = 0 if rows is near else 1
                    send(src.at[:, to, rows], dst.at[:, mine, rows],
                         ("to", what, crossing, q, which), device)

    exchange(0)
    local = []
    for src, dst, what in rows_out:
        copy = pltpu.make_async_copy(src.at[:, j], dst.at[:, mine], rs.at[number("keep", what)])
        copy.start()
        local.append(copy)

    def spread_y(step, zz, piece, kind):
        along(y, zz, piece, ("gy", step, kind, "up"), up_y)
        along(y, zz, piece, ("gy", step, kind, "down"), down_y)

    def onward_f(step, zz):
        here(ym, zz, f, "gy", step, "f", "up")
        along(ym, zz, f, ("gy", step, "f", "on"), up_y)

    def onward_g(step, zz):
        here(yp, zz, g, "gy", step, "g", "down")
        along(yp, zz, g, ("gy", step, "g", "on"), down_y)

    here(y, zm, f, "gz", "f", "up")
    along(y, zm, f, ("gz", "f", "on"), up_z)
    spread_y(1, zm, f, "f")
    here(y, zp, g, "gz", "g", "down")
    along(y, zp, g, ("gz", "g", "on"), down_z)
    spread_y(2, zp, g, "g")
    exchange(1)
    onward_f(0, z)
    onward_g(0, z)
    here(y, zm, g, "gz", "g", "up")
    spread_y(1, zm, g, "g")
    here(y, zp, f, "gz", "f", "down")
    spread_y(2, zp, f, "f")
    onward_f(1, zm)
    onward_g(2, zp)
    here(y, z2, f, "gz", "f", "on")
    spread_y(3, z2, f, "f")
    here(y, z2, g, "gz", "g", "on")
    spread_y(3, z2, g, "g")
    onward_g(1, zm)
    onward_f(2, zp)
    for n, (_, dst, what) in enumerate(rows_out):
        local[n].wait()
        for q in range(4):
            for crossing in range(2):
                for rows, _, fro, _ in partners(q)[crossing]:
                    which = 0 if rows is near else 1
                    arrived(dst.at[:, c * NE + fro, rows], "to", what, crossing, q, which)
        own = dst.at[:, pl.ds(c * NE, NE)]
        send(own, own, ("rows", what), sib)
    onward_f(3, z2)
    onward_g(3, z2)
    def turn(m):
        def body(yy, carry):
            cols = pl.ds(pl.multiple_of(m * ROWS, ROWS), ROWS)
            blocks = pl.ds(m * NE, NE)
            XT[yy, :, cols] = X[yy, blocks].reshape(ROWS, YB).T
            DT[yy, :, cols] = D[yy, blocks].reshape(ROWS, YB).T
            return carry

        lax.fori_loop(0, NY, body, 0)

    def accumulate(yy, m, first):
        rows = pl.ds(pl.multiple_of(m * ROWS, ROWS), ROWS)
        blocks = pl.ds(m * NE, NE)
        for ref, lo, hi in ((X, 0, 256), (X, 256, 512), (X, 512, 768), (D, 768, 1152)):
            got = jnp.dot(
                ref[yy, blocks].reshape(ROWS, YB),
                W[yy, :, :, lo:hi].reshape(YB, hi - lo),
                preferred_element_type=F32,
            )
            if first:
                ACC[rows, lo:hi] = got
            else:
                ACC[rows, lo:hi] += got

    steps = ((0, z), (1, zm), (2, zp), (3, z2))
    turn(c)
    accumulate(y, c, True)
    for step, zz in steps:
        here(ym, zz, g, "gy", step, "g", "up")
    accumulate(ym, c, False)
    for step, zz in steps:
        here(yp, zz, f, "gy", step, "f", "down")
    accumulate(yp, c, False)
    arrived(X.at[:, pl.ds(o * NE, NE)], "rows", "x")
    arrived(D.at[:, pl.ds(o * NE, NE)], "rows", "d")
    turn(o)
    accumulate(y, o, True)
    accumulate(ym, o, False)
    accumulate(yp, o, False)
    for step, zz in steps:
        here(y2, zz, f, "gy", step, "f", "on")
        here(y2, zz, g, "gy", step, "g", "on")
    accumulate(y2, c, False)
    accumulate(y2, o, False)

    def activate(m, carry):
        rows = pl.ds(pl.multiple_of(m * 64, 64), 64)
        gate, up, d_hidden = ACC[rows, 0:HH], ACC[rows, HH:2 * HH], ACC[rows, 2 * HH:HC]
        sig = jax.nn.sigmoid(gate)
        act = gate * sig
        CAT[rows, 0:HH] = (d_hidden * up * sig * (1.0 + gate * (1.0 - sig))).astype(BF16)
        CAT[rows, HH:2 * HH] = (d_hidden * act).astype(BF16)
        CAT[rows, 2 * HH:HC] = (act * up).astype(BF16)
        return carry

    lax.fori_loop(0, 2 * ROWS // 64, activate, 0)

    def partials(yy):
        for ref, lo, hi in ((XT, 0, 256), (XT, 256, 512), (XT, 512, 768), (DT, 768, 1152)):
            got = jnp.dot(ref[yy], CAT[:, lo:hi], preferred_element_type=F32)
            T[yy, :, :, lo:hi] = got.astype(BF16).reshape(NZ, SH, hi - lo)

    nt = (((1,), (1,)), ((), ()))

    def outputs(side, n, write):
        rows = pl.ds(pl.multiple_of(side * ROWS, ROWS), ROWS)
        lo, hi = ((2 * HH, HC), (0, 2 * HH))[n]

        def tile(yy, carry):
            write(n, yy, lax.dot_general(
                CAT[rows, lo:hi], W[yy, :, :, lo:hi].reshape(YB, hi - lo), nt,
                preferred_element_type=F32,
            ))
            return carry

        lax.fori_loop(0, NY, tile, 0)

    def first_f(step, zz):
        send(T.at[y2, zz, f], R1.at[0, step], ("r1", step, "f"), up_y)

    def first_g(step, zz):
        send(T.at[y2, zz, g], R1.at[1, step], ("r1", step, "g"), down_y)

    def plain_g(step, zz):
        send(T.at[yp, zz, g], R2.at[0, step, g], ("r2", step, "g", "up"), up_y)

    def plain_f(step, zz):
        send(T.at[ym, zz, f], R2.at[1, step, f], ("r2", step, "f", "down"), down_y)

    def joined_f(step, zz):
        arrived(R1.at[0, step], "r1", step, "f")
        T[yp, zz, f] = (T[yp, zz, f].astype(F32) + R1[0, step].astype(F32)).astype(BF16)
        send(T.at[yp, zz, f], R2.at[0, step, f], ("r2", step, "f", "up"), up_y)

    def joined_g(step, zz):
        arrived(R1.at[1, step], "r1", step, "g")
        T[ym, zz, g] = (T[ym, zz, g].astype(F32) + R1[1, step].astype(F32)).astype(BF16)
        send(T.at[ym, zz, g], R2.at[1, step, g], ("r2", step, "g", "down"), down_y)

    def partial(yy, zz):
        rows = pl.ds(pl.multiple_of(zz * SH, SH), SH)
        for ref, lo, hi in ((XT, 0, 256), (XT, 256, 512), (XT, 512, 768), (DT, 768, 1152)):
            got = jnp.dot(ref[yy, rows], CAT[:, lo:hi], preferred_element_type=F32)
            T[yy, zz, :, lo:hi] = got.astype(BF16)

    partial(y2, z2)
    first_f(0, z2)
    first_g(0, z2)
    partials(yp)
    plain_g(0, z2)
    partials(ym)
    plain_f(0, z2)
    partial(y2, zm)
    partial(y2, zp)
    partial(y2, z)
    first_f(2, zm)
    first_g(1, zp)

    def write_sibling(n, yy, value):
        OS[n, yy] = value.astype(BF16).reshape(NE, CAP, YB)

    for n in range(2):
        outputs(o, n, write_sibling)
        send(OS.at[n], OR.at[n], ("part", n), sib)
    joined_f(0, z2)
    joined_g(0, z2)
    plain_g(1, zp)
    plain_f(2, zm)

    def write_own(n, yy, value):
        value = value + OR[n, yy].reshape(ROWS, YB).astype(F32)
        BS[n, yy] = value.astype(BF16).reshape(NE, CAP, YB)

    def give_back(n, crossing):
        for q in range(4):
            for rows, to, _, device in partners(q)[crossing]:
                which = 0 if rows is near else 1
                send(BS.at[n, :, to, rows], BK.at[n, :, j, rows],
                     ("back", n, crossing, q, which), device)

    local = []
    for n in range(2):
        arrived(OR.at[n], "part", n)
        outputs(c, n, write_own)
        give_back(n, 1)
        copy = pltpu.make_async_copy(BS.at[n, :, j], BK.at[n, :, j], rs.at[number("stay", n)])
        copy.start()
        local.append(copy)

    partials(y)
    joined_f(2, zm)
    joined_g(1, zp)
    first_f(1, zp)
    first_g(2, zm)
    plain_g(2, zm)
    plain_f(1, zp)

    def summed_y(step, zz, piece, kind):
        for d in range(2):
            arrived(R2.at[d, step, piece], "r2", step, kind, ("up", "down")[d])
        return (
            T[y, zz, piece].astype(F32)
            + R2[0, step, piece].astype(F32)
            + R2[1, step, piece].astype(F32)
        )

    ZS[0, f] = summed_y(0, z2, f, "f").astype(BF16)
    send(ZS.at[0, f], Z1.at[0], ("z1", "f"), up_z)
    ZS[0, g] = summed_y(0, z2, g, "g").astype(BF16)
    send(ZS.at[0, g], Z1.at[1], ("z1", "g"), down_z)
    ZS[2, f] = summed_y(2, zm, f, "f").astype(BF16)
    send(ZS.at[2, f], Z2.at[1, f], ("z2", "f", "down"), down_z)
    ZS[1, g] = summed_y(1, zp, g, "g").astype(BF16)
    send(ZS.at[1, g], Z2.at[0, g], ("z2", "g", "up"), up_z)
    give_back(0, 0)
    give_back(1, 0)
    joined_f(1, zp)
    joined_g(2, zm)
    first_f(3, z)
    first_g(3, z)
    plain_g(3, z)
    plain_f(3, z)
    total = summed_y(1, zp, f, "f")
    arrived(Z1.at[0], "z1", "f")
    ZS[1, f] = (total + Z1[0].astype(F32)).astype(BF16)
    send(ZS.at[1, f], Z2.at[0, f], ("z2", "f", "up"), up_z)
    total = summed_y(2, zm, g, "g")
    arrived(Z1.at[1], "z1", "g")
    ZS[2, g] = (total + Z1[1].astype(F32)).astype(BF16)
    send(ZS.at[2, g], Z2.at[1, g], ("z2", "g", "down"), down_z)
    joined_f(3, z)
    joined_g(3, z)

    for n in range(2):
        local[n].wait()
        for q in range(4):
            for crossing in range(2):
                for rows, _, fro, _ in partners(q)[crossing]:
                    which = 0 if rows is near else 1
                    arrived(BK.at[n, :, fro, rows], "back", n, crossing, q, which)
    tn = (((0,), (0,)), ((), ()))
    for yy in range(NY):
        back = BK[0, yy].reshape(ROWS, YB)
        out = sum(
            lax.dot_general(SEL[n], back, tn, preferred_element_type=F32) for n in (3, 2, 1)
        )
        back = BK[1, yy].reshape(ROWS, YB)
        d_in = lax.dot_general(SEL[0], back, tn, preferred_element_type=F32)
        for zz in range(NZ):
            cols = slice((zz * 4 + yy) * SH, (zz * 4 + yy + 1) * SH)
            lo_ref[:, cols] = out[:, zz * SH:(zz + 1) * SH].astype(BF16)
            dt_ref[:, cols] = d_in[:, zz * SH:(zz + 1) * SH].astype(BF16)

    def total_z(piece, kind):
        total = summed_y(3, z, piece, kind)
        arrived(Z2.at[0, piece], "z2", kind, "up")
        arrived(Z2.at[1, piece], "z2", kind, "down")
        return total + Z2[0, piece].astype(F32) + Z2[1, piece].astype(F32)

    FS[...] = total_z(g, "g")
    send(FS, FR, ("fin",), sib)
    total = total_z(f, "f")
    for n, ref in enumerate((gg_ref, gu_ref, gd_ref)):
        ref[0, :, half_c] = total[:, n * HH:(n + 1) * HH]
    arrived(FR, "fin")
    for n, ref in enumerate((gg_ref, gu_ref, gd_ref)):
        ref[0, :, half_o] = FR[:, n * HH:(n + 1) * HH]

    for copy in sent:
        copy.wait_send()
    assert len(numbers) <= N_SEM


def hand_out(*refs):
    count = len(refs) // 2
    done = refs[-1]
    copies = [
        pltpu.make_async_copy(refs[n], refs[count + n], done.at[n]) for n in range(count)
    ]
    for copy in copies:
        copy.start()
    for copy in copies:
        copy.wait()


def shards(tokens, routes, gate_scale, w_gate, w_up, w_down, d_out):
    vm = pl.BlockSpec(memory_space=pltpu.VMEM)
    hbm = pl.BlockSpec(memory_space=pltpu.HBM)
    grad = jax.ShapeDtypeStruct(w_gate.shape, F32)
    rows = jax.ShapeDtypeStruct(tokens.shape, BF16)
    results = (rows, rows, grad, grad, grad)
    found = pl.pallas_call(
        kernel,
        out_shape=results,
        in_specs=[hbm] * 7,
        out_specs=(vm,) * 5,
        scratch_shapes=[
            pltpu.VMEM((NY, NZ, SH, HC), BF16),
            pltpu.VMEM((NY, 2 * NE, CAP, YB), BF16),
            pltpu.VMEM((NY, 2 * NE, CAP, YB), BF16),
            pltpu.VMEM((NY, YB, 2 * ROWS), BF16),
            pltpu.VMEM((NY, YB, 2 * ROWS), BF16),
            pltpu.VMEM((NY, NE, CAP, YB), BF16),
            pltpu.VMEM((NY, NE, CAP, YB), BF16),
            pltpu.VMEM((4, ROWS, TOK), BF16),
            pltpu.VMEM((2 * ROWS, HC), F32),
            pltpu.VMEM((2 * ROWS, HC), BF16),
            pltpu.VMEM((NY, NZ, SH, HC), BF16),
            pltpu.VMEM((2, NZ, 64, HC), BF16),
            pltpu.VMEM((2, NZ, SH, HC), BF16),
            pltpu.VMEM((2, 64, HC), BF16),
            pltpu.VMEM((2, SH, HC), BF16),
            pltpu.VMEM((3, SH, HC), BF16),
            pltpu.VMEM((64, HC), F32),
            pltpu.VMEM((64, HC), F32),
            pltpu.VMEM((2, NY, NE, CAP, YB), BF16),
            pltpu.VMEM((2, NY, NE, CAP, YB), BF16),
            pltpu.VMEM((2, NY, NE, CAP, YB), BF16),
            pltpu.VMEM((2, NY, NE, CAP, YB), BF16),
            pltpu.VMEM(tokens.shape, BF16),
            pltpu.VMEM(tokens.shape, BF16),
            pltpu.VMEM(routes.shape[::-1], jnp.int32),
            pltpu.VMEM(routes.shape[::-1], F32),
            pltpu.SemaphoreType.DMA((N_SEM,)),
            pltpu.SemaphoreType.DMA((N_SEM,)),
        ],
        compiler_params=pltpu.CompilerParams(
            collective_id=0, has_side_effects=True, vmem_limit_bytes=VMEM_MB * 1024 * 1024
        ),
    )(*(
        pltpu.with_memory_space_constraint(value, pltpu.HBM)
        for value in (tokens, routes.T, gate_scale.T, w_gate, w_up, w_down, d_out)
    ))
    return pl.pallas_call(
        hand_out,
        out_shape=results,
        in_specs=[vm] * 5,
        out_specs=(hbm,) * 5,
        scratch_shapes=[pltpu.SemaphoreType.DMA((5,))],
        compiler_params=pltpu.CompilerParams(vmem_limit_bytes=8 * 1024 * 1024),
    )(*found)


def solution(mesh):
    tok = P(("dp", "expert"), None)
    wei = P("expert", "dp", None)
    return jax.shard_map(
        shards,
        mesh=mesh,
        in_specs=(tok, tok, tok, wei, wei, wei, tok),
        out_specs=(tok, tok, wei, wei, wei),
        check_vma=False,
    )
```

```python
import jax
import jax.numpy as jnp
from jax import lax
from jax.experimental import pallas as pl
from jax.experimental.pallas import tpu as pltpu
from jax.sharding import PartitionSpec as P

CAP = 32
MESH = pl.DeviceIdType.MESH
F32 = jnp.float32
BF16 = jnp.bfloat16

NY, NZ, SH = 4, 4, 128
HH = 384
CW = (256, 128)
CO = (0, 256)
YB = NZ * SH
NE = 8
TOK = 192
ROWS = NE * CAP
N_SEM = 208
VMEM_MB = 50


def kernel(
    tok_hbm, rt_hbm, gs_hbm, wg_ref, wu_ref, wd_ref, do_hbm,
    lo_ref, dt_ref, gg_ref, gu_ref, gd_ref,
    W0, W1, WO0, WO1, X, D, XT, DT, SX, SD, SEL, A0, A1, C0, C1, T0, T1,
    RF0, RF1, RS0, RS1, ZF0, ZF1, Z20, Z21, ZS0, ZS1, FS0, FS1, FR0, FR1,
    OS, OR, BS, BK, tok_ref, do_ref, rt_ref, gs_ref, ss, rs,
):
    W, WO, ACC, CAT, T = (W0, W1), (WO0, WO1), (A0, A1), (C0, C1), (T0, T1)
    R1, R2, Z1, Z2, ZS = (RF0, RF1), (RS0, RS1), (ZF0, ZF1), (Z20, Z21), (ZS0, ZS1)
    FS, FR = (FS0, FS1), (FR0, FR1)
    i = lax.axis_index("dp")
    j = lax.axis_index("expert")
    c = lax.rem(i, 2)
    o = 1 - c
    p = lax.div(i, 2)
    y = lax.rem(p, 4)
    z = lax.div(p, 4)
    x = lax.div(j, 2)
    side = lax.rem(j, 2)
    yp, ym, y2 = lax.rem(y + 1, 4), lax.rem(y + 3, 4), lax.rem(y + 2, 4)
    zp, zm, z2 = lax.rem(z + 1, 4), lax.rem(z + 3, 4), lax.rem(z + 2, 4)
    zn = lax.rem(z + 3 + 2 * side, 4)

    def place(yy, zz, cc):
        return {"dp": (zz * 4 + yy) * 2 + cc}

    sib = place(y, z, o)
    up_y, down_y = place(yp, z, c), place(ym, z, c)
    up_z, down_z = place(y, zp, c), place(y, zm, c)

    near, far = pl.ds(0, 16), pl.ds(16, 16)

    def partners(q):
        to, fro = lax.rem(x + q, 4), lax.rem(x + 4 - q, 4)
        across = [
            (near, to * 2 + 1 - side, fro * 2 + 1 - side, {"expert": to * 2 + 1 - side}),
            (far, to * 2 + 1 - side, fro * 2 + 1 - side,
             {"dp": (zn * 4 + y) * 2 + c, "expert": to * 2 + 1 - side}),
        ]
        same = [(pl.ds(0, CAP), to * 2 + side, fro * 2 + side, {"expert": to * 2 + side})]
        return same if q else [], across

    numbers = {}

    def number(*name):
        return numbers.setdefault(name, len(numbers))

    sent = []

    def send(src, dst, name, to):
        k = number(*name)
        copy = pltpu.make_async_remote_copy(
            src_ref=src, dst_ref=dst, send_sem=ss.at[k], recv_sem=rs.at[k],
            device_id=to, device_id_type=MESH,
        )
        copy.start()
        sent.append(copy)

    def arrived(ref, *name):
        k = number(*name)
        pltpu.make_async_remote_copy(
            src_ref=ref, dst_ref=ref, send_sem=ss.at[k], recv_sem=rs.at[k],
            device_id=sib, device_id_type=MESH,
        ).wait_recv()

    def fetch(src, dst, *name):
        copy = pltpu.make_async_copy(src, dst, rs.at[number(*name)])
        copy.start()
        return copy

    f = pl.ds(pl.multiple_of(c * 64, 64), 64)
    g = pl.ds(pl.multiple_of(o * 64, 64), 64)

    def units(core, k):
        return pl.ds(pl.multiple_of(core * HH + CO[k], 128), CW[k])

    own, other = [[], []], [[], []]
    for k in range(2):
        for n, w_ref in enumerate((wg_ref, wu_ref, wd_ref)):
            cols = pl.ds(n * CW[k], CW[k])
            other[k].append(
                fetch(w_ref.at[0, :, units(o, k)], WO[k].at[:, cols], "other", k, n)
            )
            own[k].append(
                fetch(w_ref.at[0, :, units(c, k)], W[k].at[y, z, f, cols], "own", k, n)
            )
    loads = [
        fetch(rt_hbm, rt_ref, "load", "r"),
        fetch(gs_hbm, gs_ref, "load", "s"),
        fetch(tok_hbm, tok_ref, "load", "x"),
        fetch(do_hbm, do_ref, "load", "d"),
    ]
    barrier = pltpu.get_barrier_semaphore()
    greet = [sib, up_y, down_y, up_z, down_z]
    for q in range(4):
        same, across = partners(q)
        greet += [to for _, _, _, to in same + across]
    for to in greet:
        pl.semaphore_signal(barrier, inc=1, device_id=to, device_id_type=MESH)
    for k in range(2):
        for copy in other[k] + own[k]:
            copy.wait()
    pl.semaphore_wait(barrier, len(greet))

    def along(k, yy, zz, piece, name, to):
        send(W[k].at[yy, zz, piece], W[k].at[yy, zz, piece], (k,) + name, to)

    def here(k, yy, zz, piece, *name):
        arrived(W[k].at[yy, zz, piece], k, *name)

    def leave(k, kind, piece, way):
        to_z, to_y = (up_z, up_y) if way == "up" else (down_z, down_y)
        along(k, y, z, piece, ("gz", kind, way), to_z)
        along(k, y, z, piece, ("gy", 0, kind, way), to_y)

    for k in range(2):
        send(WO[k], W[k].at[y, z, f], ("sib", k), sib)
    leave(0, "f", f, "up")
    arrived(W[0].at[y, z, g], "sib", 0)
    leave(0, "g", g, "down")
    leave(0, "g", g, "up")
    leave(0, "f", f, "down")
    leave(1, "f", f, "up")
    arrived(W[1].at[y, z, g], "sib", 1)
    leave(1, "g", g, "down")
    leave(1, "g", g, "up")
    leave(1, "f", f, "down")

    shape = (ROWS, TOK)
    row = lax.broadcasted_iota(jnp.int32, shape, 0)
    row_e = lax.div(row, CAP)
    row_s = lax.rem(row, CAP).astype(F32)
    for copy in loads[:2]:
        copy.wait()
    scale = gs_ref[...]
    combine = scale / jnp.sum(scale, axis=0, keepdims=True)
    routes = rt_ref[...]
    named = jnp.zeros(shape, F32)
    weight = jnp.zeros(shape, F32)
    for s in range(6):
        same = routes[s:s + 1, :] == row_e
        named = jnp.where(same, 1.0, named)
        weight = jnp.where(same, combine[s:s + 1, :], weight)
    earlier = (
        lax.broadcasted_iota(jnp.int32, (TOK, TOK), 0)
        < lax.broadcasted_iota(jnp.int32, (TOK, TOK), 1)
    ).astype(F32).astype(BF16)
    position = jnp.dot(named.astype(BF16), earlier, preferred_element_type=F32)
    chosen = jnp.where(position == row_s, named, 0.0)
    weight = weight * chosen
    slot_weight = jnp.sum(weight, axis=1, keepdims=True)
    select = chosen.astype(BF16)
    SEL[0] = select
    rest = weight
    for n in range(1, 4):
        part = rest.astype(BF16)
        SEL[n] = part
        rest = rest - part.astype(F32)

    def columns(ref, yy):
        return jnp.concatenate(
            [ref[:, (zz * 4 + yy) * SH:(zz * 4 + yy + 1) * SH] for zz in range(NZ)], axis=1
        )

    for copy in loads[2:]:
        copy.wait()
    for yy in range(NY):
        rows = jnp.dot(select, columns(tok_ref, yy), preferred_element_type=F32)
        SX[yy] = rows.astype(BF16).reshape(NE, CAP, YB)
        rows = jnp.dot(select, columns(do_ref, yy), preferred_element_type=F32)
        SD[yy] = (rows * slot_weight).astype(BF16).reshape(NE, CAP, YB)

    mine = c * NE + j
    rows_out = ((SX, X, "x"), (SD, D, "d"))

    def exchange(crossing):
        for src, dst, what in rows_out:
            for q in range(4):
                for rows, to, _, device in partners(q)[crossing]:
                    which = 0 if rows is near else 1
                    send(src.at[:, to, rows], dst.at[:, mine, rows],
                         ("to", what, crossing, q, which), device)

    exchange(0)
    local = [fetch(src.at[:, j], dst.at[:, mine], "keep", what) for src, dst, what in rows_out]

    def spread_y(k, step, zz, piece, kind):
        along(k, y, zz, piece, ("gy", step, kind, "up"), up_y)
        along(k, y, zz, piece, ("gy", step, kind, "down"), down_y)

    def onward_f(k, step, zz):
        here(k, ym, zz, f, "gy", step, "f", "up")
        along(k, ym, zz, f, ("gy", step, "f", "on"), up_y)

    def onward_g(k, step, zz):
        here(k, yp, zz, g, "gy", step, "g", "down")
        along(k, yp, zz, g, ("gy", step, "g", "on"), down_y)

    def onward_z(k):
        here(k, y, zm, f, "gz", "f", "up")
        along(k, y, zm, f, ("gz", "f", "on"), up_z)
        here(k, y, zp, g, "gz", "g", "down")
        along(k, y, zp, g, ("gz", "g", "on"), down_z)

    onward_f(0, 0, z)
    onward_g(0, 0, z)
    onward_z(0)
    spread_y(0, 1, zm, f, "f")
    spread_y(0, 2, zp, g, "g")
    exchange(1)
    onward_f(1, 0, z)
    onward_g(1, 0, z)
    here(0, y, zm, g, "gz", "g", "up")
    spread_y(0, 1, zm, g, "g")
    here(0, y, zp, f, "gz", "f", "down")
    spread_y(0, 2, zp, f, "f")
    onward_z(1)
    onward_f(0, 1, zm)
    onward_g(0, 2, zp)
    here(0, y, z2, f, "gz", "f", "on")
    spread_y(0, 3, z2, f, "f")
    here(0, y, z2, g, "gz", "g", "on")
    spread_y(0, 3, z2, g, "g")
    here(1, y, zm, g, "gz", "g", "up")
    here(1, y, zp, f, "gz", "f", "down")
    for step, zz in ((1, zm), (2, zp)):
        spread_y(1, step, zz, f, "f")
        spread_y(1, step, zz, g, "g")
    onward_g(0, 1, zm)
    onward_f(0, 2, zp)
    onward_f(0, 3, z2)
    onward_g(0, 3, z2)
    for step, zz in ((1, zm), (2, zp)):
        onward_f(1, step, zz)
        onward_g(1, step, zz)
    for n, (_, dst, what) in enumerate(rows_out):
        local[n].wait()
        for q in range(4):
            for crossing in range(2):
                for rows, _, fro, _ in partners(q)[crossing]:
                    which = 0 if rows is near else 1
                    arrived(dst.at[:, c * NE + fro, rows], "to", what, crossing, q, which)
        block = dst.at[:, pl.ds(c * NE, NE)]
        send(block, block, ("rows", what), sib)

    def turn(m):
        def body(yy, carry):
            cols = pl.ds(pl.multiple_of(m * ROWS, ROWS), ROWS)
            blocks = pl.ds(m * NE, NE)
            XT[yy, :, cols] = X[yy, blocks].reshape(ROWS, YB).T
            DT[yy, :, cols] = D[yy, blocks].reshape(ROWS, YB).T
            return carry

        lax.fori_loop(0, NY, body, 0)

    tiles = (
        ((0, 0, 256), (0, 256, 512), (1, 512, 768)),
        ((0, 0, 256), (1, 256, 384)),
    )

    def accumulate(k, yy, m, first=False):
        rows = pl.ds(pl.multiple_of(m * ROWS, ROWS), ROWS)
        blocks = pl.ds(m * NE, NE)
        for which, lo, hi in tiles[k]:
            got = jnp.dot(
                (X, D)[which][yy, blocks].reshape(ROWS, YB),
                W[k][yy, :, :, lo:hi].reshape(YB, hi - lo),
                preferred_element_type=F32,
            )
            if first:
                ACC[k][rows, lo:hi] = got
            else:
                ACC[k][rows, lo:hi] += got

    steps = ((0, z), (1, zm), (2, zp), (3, z2))

    def wait_m(k):
        for step, zz in steps:
            here(k, ym, zz, g, "gy", step, "g", "up")

    def wait_p(k):
        for step, zz in steps:
            here(k, yp, zz, f, "gy", step, "f", "down")

    def wait_2(k):
        for step, zz in steps:
            here(k, y2, zz, f, "gy", step, "f", "on")
            here(k, y2, zz, g, "gy", step, "g", "on")

    turn(c)
    accumulate(0, y, c, True)
    wait_m(0)
    accumulate(0, ym, c)
    wait_p(0)
    accumulate(0, yp, c)
    wait_2(0)
    accumulate(0, y2, c)
    here(1, y, z2, f, "gz", "f", "on")
    spread_y(1, 3, z2, f, "f")
    here(1, y, z2, g, "gz", "g", "on")
    spread_y(1, 3, z2, g, "g")
    arrived(X.at[:, pl.ds(o * NE, NE)], "rows", "x")
    arrived(D.at[:, pl.ds(o * NE, NE)], "rows", "d")
    turn(o)
    accumulate(0, y, o, True)
    accumulate(0, ym, o)
    accumulate(0, yp, o)
    accumulate(0, y2, o)

    def activate(k):
        w = CW[k]

        def body(m, carry):
            rows = pl.ds(pl.multiple_of(m * 64, 64), 64)
            gate, up, d_hidden = (ACC[k][rows, n * w:(n + 1) * w] for n in range(3))
            sig = jax.nn.sigmoid(gate)
            act = gate * sig
            CAT[k][rows, 0:w] = (
                d_hidden * up * sig * (1.0 + gate * (1.0 - sig))
            ).astype(BF16)
            CAT[k][rows, w:2 * w] = (d_hidden * act).astype(BF16)
            CAT[k][rows, 2 * w:3 * w] = (act * up).astype(BF16)
            return carry

        lax.fori_loop(0, 2 * ROWS // 64, body, 0)

    def partials(k, yy):
        for which, lo, hi in tiles[k]:
            got = jnp.dot(
                (XT, DT)[which][yy], CAT[k][:, lo:hi], preferred_element_type=F32
            )
            T[k][yy, :, :, lo:hi] = got.astype(BF16).reshape(NZ, SH, hi - lo)

    def partial(k, yy, zz):
        rows = pl.ds(pl.multiple_of(zz * SH, SH), SH)
        for which, lo, hi in tiles[k]:
            got = jnp.dot(
                (XT, DT)[which][yy, rows], CAT[k][:, lo:hi], preferred_element_type=F32
            )
            T[k][yy, zz, :, lo:hi] = got.astype(BF16)

    nt = (((1,), (1,)), ((), ()))

    def outputs(side_, n, write):
        rows = pl.ds(pl.multiple_of(side_ * ROWS, ROWS), ROWS)

        def tile(yy, carry):
            total = None
            for k in range(2):
                lo, hi = ((2 * CW[k], 3 * CW[k]), (0, 2 * CW[k]))[n]
                got = lax.dot_general(
                    CAT[k][rows, lo:hi], W[k][yy, :, :, lo:hi].reshape(YB, hi - lo), nt,
                    preferred_element_type=F32,
                )
                total = got if total is None else total + got
            write(n, yy, total)
            return carry

        lax.fori_loop(0, NY, tile, 0)

    def first_f(k, step, zz):
        send(T[k].at[y2, zz, f], R1[k].at[0, step], ("r1", k, step, "f"), up_y)

    def first_g(k, step, zz):
        send(T[k].at[y2, zz, g], R1[k].at[1, step], ("r1", k, step, "g"), down_y)

    def plain_g(k, step, zz):
        send(T[k].at[yp, zz, g], R2[k].at[0, step, g], ("r2", k, step, "g", "up"), up_y)

    def plain_f(k, step, zz):
        send(T[k].at[ym, zz, f], R2[k].at[1, step, f], ("r2", k, step, "f", "down"), down_y)

    def joined_f(k, step, zz):
        arrived(R1[k].at[0, step], "r1", k, step, "f")
        T[k][yp, zz, f] = (
            T[k][yp, zz, f].astype(F32) + R1[k][0, step].astype(F32)
        ).astype(BF16)
        send(T[k].at[yp, zz, f], R2[k].at[0, step, f], ("r2", k, step, "f", "up"), up_y)

    def joined_g(k, step, zz):
        arrived(R1[k].at[1, step], "r1", k, step, "g")
        T[k][ym, zz, g] = (
            T[k][ym, zz, g].astype(F32) + R1[k][1, step].astype(F32)
        ).astype(BF16)
        send(T[k].at[ym, zz, g], R2[k].at[1, step, g], ("r2", k, step, "g", "down"), down_y)

    def summed_y(k, step, zz, piece, kind):
        for d in range(2):
            arrived(R2[k].at[d, step, piece], "r2", k, step, kind, ("up", "down")[d])
        return (
            T[k][y, zz, piece].astype(F32)
            + R2[k][0, step, piece].astype(F32)
            + R2[k][1, step, piece].astype(F32)
        )

    def far_z(k):
        ZS[k][0, f] = summed_y(k, 0, z2, f, "f").astype(BF16)
        send(ZS[k].at[0, f], Z1[k].at[0], ("z1", k, "f"), up_z)
        ZS[k][0, g] = summed_y(k, 0, z2, g, "g").astype(BF16)
        send(ZS[k].at[0, g], Z1[k].at[1], ("z1", k, "g"), down_z)

    def plain_z(k):
        ZS[k][2, f] = summed_y(k, 2, zm, f, "f").astype(BF16)
        send(ZS[k].at[2, f], Z2[k].at[1, f], ("z2", k, "f", "down"), down_z)
        ZS[k][1, g] = summed_y(k, 1, zp, g, "g").astype(BF16)
        send(ZS[k].at[1, g], Z2[k].at[0, g], ("z2", k, "g", "up"), up_z)

    def joined_z(k):
        total = summed_y(k, 1, zp, f, "f")
        arrived(Z1[k].at[0], "z1", k, "f")
        ZS[k][1, f] = (total + Z1[k][0].astype(F32)).astype(BF16)
        send(ZS[k].at[1, f], Z2[k].at[0, f], ("z2", k, "f", "up"), up_z)
        total = summed_y(k, 2, zm, g, "g")
        arrived(Z1[k].at[1], "z1", k, "g")
        ZS[k][2, g] = (total + Z1[k][1].astype(F32)).astype(BF16)
        send(ZS[k].at[2, g], Z2[k].at[1, g], ("z2", k, "g", "down"), down_z)

    def total_z(k, piece, kind):
        total = summed_y(k, 3, z, piece, kind)
        arrived(Z2[k].at[0, piece], "z2", k, kind, "up")
        arrived(Z2[k].at[1, piece], "z2", k, kind, "down")
        return total + Z2[k][0, piece].astype(F32) + Z2[k][1, piece].astype(F32)

    grads = (gg_ref, gu_ref, gd_ref)

    def finish(k):
        w = CW[k]
        FS[k][...] = total_z(k, g, "g")
        send(FS[k], FR[k], ("fin", k), sib)
        total = total_z(k, f, "f")
        for n, ref in enumerate(grads):
            ref[0, :, units(c, k)] = total[:, n * w:(n + 1) * w]

    def close(k):
        w = CW[k]
        arrived(FR[k], "fin", k)
        for n, ref in enumerate(grads):
            ref[0, :, units(o, k)] = FR[k][:, n * w:(n + 1) * w]

    activate(0)
    onward_f(1, 3, z2)
    onward_g(1, 3, z2)
    partial(0, y2, z2)
    first_f(0, 0, z2)
    first_g(0, 0, z2)
    partials(0, yp)
    plain_g(0, 0, z2)
    partials(0, ym)
    plain_f(0, 0, z2)
    partial(0, y2, zm)
    partial(0, y2, zp)
    partial(0, y2, z)
    first_f(0, 2, zm)
    first_g(0, 1, zp)
    for m, first in ((c, True), (o, True)):
        accumulate(1, y, m, first)
    wait_m(1)
    wait_p(1)
    for m in (c, o):
        accumulate(1, ym, m)
        accumulate(1, yp, m)
    wait_2(1)
    for m in (c, o):
        accumulate(1, y2, m)
    activate(1)
    for yy in (y2, yp, ym):
        partial(1, yy, z2)
    first_f(1, 0, z2)
    first_g(1, 0, z2)
    plain_g(1, 0, z2)
    plain_f(1, 0, z2)

    def write_sibling(n, yy, value):
        OS[n, yy] = value.astype(BF16).reshape(NE, CAP, YB)

    outputs(o, 0, write_sibling)
    send(OS.at[0], OR.at[0], ("part", 0), sib)
    joined_f(0, 0, z2)
    joined_g(0, 0, z2)
    plain_g(0, 1, zp)
    plain_f(0, 2, zm)
    outputs(o, 1, write_sibling)
    send(OS.at[1], OR.at[1], ("part", 1), sib)

    def write_own(n, yy, value):
        value = value + OR[n, yy].reshape(ROWS, YB).astype(F32)
        BS[n, yy] = value.astype(BF16).reshape(NE, CAP, YB)

    def give_back(n, crossing):
        for q in range(4):
            for rows, to, _, device in partners(q)[crossing]:
                which = 0 if rows is near else 1
                send(BS.at[n, :, to, rows], BK.at[n, :, j, rows],
                     ("back", n, crossing, q, which), device)

    local = []
    for n in range(2):
        arrived(OR.at[n], "part", n)
        outputs(c, n, write_own)
        if n == 0:
            give_back(0, 1)
        local.append(fetch(BS.at[n, :, j], BK.at[n, :, j], "stay", n))

    joined_f(1, 0, z2)
    joined_g(1, 0, z2)
    joined_f(0, 2, zm)
    joined_g(0, 1, zp)
    first_f(0, 1, zp)
    first_g(0, 2, zm)
    plain_g(0, 2, zm)
    plain_f(0, 1, zp)
    partials(0, y)
    far_z(0)
    give_back(0, 0)
    for yy in (y2, yp, ym):
        for zz in (zm, zp, z):
            partial(1, yy, zz)
    partials(1, y)
    far_z(1)
    plain_z(0)
    give_back(1, 1)
    joined_f(0, 1, zp)
    joined_g(0, 2, zm)
    first_f(0, 3, z)
    first_g(0, 3, z)
    first_f(1, 2, zm)
    first_g(1, 1, zp)
    first_f(1, 1, zp)
    first_g(1, 2, zm)
    plain_g(0, 3, z)
    plain_f(0, 3, z)
    plain_g(1, 1, zp)
    plain_f(1, 2, zm)
    joined_z(0)
    give_back(1, 0)
    joined_f(1, 2, zm)
    joined_g(1, 1, zp)
    first_f(1, 3, z)
    first_g(1, 3, z)
    plain_g(1, 2, zm)
    plain_f(1, 1, zp)
    joined_f(1, 1, zp)
    joined_g(1, 2, zm)
    joined_f(0, 3, z)
    joined_g(0, 3, z)
    plain_g(1, 3, z)
    plain_f(1, 3, z)
    plain_z(1)
    joined_f(1, 3, z)
    joined_g(1, 3, z)
    joined_z(1)

    for n in range(2):
        local[n].wait()
        for q in range(4):
            for crossing in range(2):
                for rows, _, fro, _ in partners(q)[crossing]:
                    which = 0 if rows is near else 1
                    arrived(BK.at[n, :, fro, rows], "back", n, crossing, q, which)
    tn = (((0,), (0,)), ((), ()))
    for yy in range(NY):
        back = BK[0, yy].reshape(ROWS, YB)
        out = sum(
            lax.dot_general(SEL[n], back, tn, preferred_element_type=F32) for n in (3, 2, 1)
        )
        back = BK[1, yy].reshape(ROWS, YB)
        d_in = lax.dot_general(SEL[0], back, tn, preferred_element_type=F32)
        for zz in range(NZ):
            cols = slice((zz * 4 + yy) * SH, (zz * 4 + yy + 1) * SH)
            lo_ref[:, cols] = out[:, zz * SH:(zz + 1) * SH].astype(BF16)
            dt_ref[:, cols] = d_in[:, zz * SH:(zz + 1) * SH].astype(BF16)

    finish(0)
    finish(1)
    close(0)
    close(1)

    for copy in sent:
        copy.wait_send()
    assert len(numbers) <= N_SEM


def hand_out(*refs):
    count = len(refs) // 2
    done = refs[-1]
    copies = [
        pltpu.make_async_copy(refs[n], refs[count + n], done.at[n]) for n in range(count)
    ]
    for copy in copies:
        copy.start()
    for copy in copies:
        copy.wait()


def shards(tokens, routes, gate_scale, w_gate, w_up, w_down, d_out):
    vm = pl.BlockSpec(memory_space=pltpu.VMEM)
    hbm = pl.BlockSpec(memory_space=pltpu.HBM)
    grad = jax.ShapeDtypeStruct(w_gate.shape, F32)
    rows = jax.ShapeDtypeStruct(tokens.shape, BF16)
    results = (rows, rows, grad, grad, grad)

    def chunks(kind, *lead):
        return [pltpu.VMEM((*lead, 3 * w), kind) for w in CW]

    found = pl.pallas_call(
        kernel,
        out_shape=results,
        in_specs=[hbm] * 7,
        out_specs=(vm,) * 5,
        scratch_shapes=[
            *chunks(BF16, NY, NZ, SH),
            *chunks(BF16, 64),
            pltpu.VMEM((NY, 2 * NE, CAP, YB), BF16),
            pltpu.VMEM((NY, 2 * NE, CAP, YB), BF16),
            pltpu.VMEM((NY, YB, 2 * ROWS), BF16),
            pltpu.VMEM((NY, YB, 2 * ROWS), BF16),
            pltpu.VMEM((NY, NE, CAP, YB), BF16),
            pltpu.VMEM((NY, NE, CAP, YB), BF16),
            pltpu.VMEM((4, ROWS, TOK), BF16),
            *chunks(F32, 2 * ROWS),
            *chunks(BF16, 2 * ROWS),
            *chunks(BF16, NY, NZ, SH),
            *chunks(BF16, 2, NZ, 64),
            *chunks(BF16, 2, NZ, SH),
            *chunks(BF16, 2, 64),
            *chunks(BF16, 2, SH),
            *chunks(BF16, 3, SH),
            *chunks(F32, 64),
            *chunks(F32, 64),
            pltpu.VMEM((2, NY, NE, CAP, YB), BF16),
            pltpu.VMEM((2, NY, NE, CAP, YB), BF16),
            pltpu.VMEM((2, NY, NE, CAP, YB), BF16),
            pltpu.VMEM((2, NY, NE, CAP, YB), BF16),
            pltpu.VMEM(tokens.shape, BF16),
            pltpu.VMEM(tokens.shape, BF16),
            pltpu.VMEM(routes.shape[::-1], jnp.int32),
            pltpu.VMEM(routes.shape[::-1], F32),
            pltpu.SemaphoreType.DMA((N_SEM,)),
            pltpu.SemaphoreType.DMA((N_SEM,)),
        ],
        compiler_params=pltpu.CompilerParams(
            collective_id=0, has_side_effects=True, vmem_limit_bytes=VMEM_MB * 1024 * 1024
        ),
    )(*(
        pltpu.with_memory_space_constraint(value, pltpu.HBM)
        for value in (tokens, routes.T, gate_scale.T, w_gate, w_up, w_down, d_out)
    ))
    return pl.pallas_call(
        hand_out,
        out_shape=results,
        in_specs=[vm] * 5,
        out_specs=(hbm,) * 5,
        scratch_shapes=[pltpu.SemaphoreType.DMA((5,))],
        compiler_params=pltpu.CompilerParams(vmem_limit_bytes=8 * 1024 * 1024),
    )(*found)


def solution(mesh):
    tok = P(("dp", "expert"), None)
    wei = P("expert", "dp", None)
    return jax.shard_map(
        shards,
        mesh=mesh,
        in_specs=(tok, tok, tok, wei, wei, wei, tok),
        out_specs=(tok, tok, wei, wei, wei),
        check_vma=False,
    )
```

```python
import jax
import jax.numpy as jnp
from jax import lax
from jax.experimental import pallas as pl
from jax.experimental.pallas import tpu as pltpu
from jax.sharding import PartitionSpec as P

CAP = 32
MESH = pl.DeviceIdType.MESH
F32 = jnp.float32
BF16 = jnp.bfloat16

NY, NZ, SH = 4, 4, 128
HH = 384
CW = (256, 128)
CO = (0, 256)
YB = NZ * SH
NE = 8
TOK = 192
ROWS = NE * CAP
N_SEM = 240
VMEM_MB = 50


def kernel(
    tok_hbm, rt_hbm, gs_hbm, wg_ref, wu_ref, wd_ref, do_hbm,
    lo_ref, dt_ref, gg_ref, gu_ref, gd_ref,
    W0, W1, WO0, WO1, X, D, XT, DT, SX, SD, SEL, A0, A1, C0, C1, T0, T1,
    RF0, RF1, RS0, RS1, ZF0, ZF1, Z20, Z21, ZS0, ZS1, FS0, FS1, FR0, FR1,
    OS, OR, BS, BK, tok_ref, do_ref, rt_ref, gs_ref, ss, rs,
):
    W, WO, ACC, CAT, T = (W0, W1), (WO0, WO1), (A0, A1), (C0, C1), (T0, T1)
    R1, R2, Z1, Z2, ZS = (RF0, RF1), (RS0, RS1), (ZF0, ZF1), (Z20, Z21), (ZS0, ZS1)
    FS, FR = (FS0, FS1), (FR0, FR1)
    i = lax.axis_index("dp")
    j = lax.axis_index("expert")
    c = lax.rem(i, 2)
    o = 1 - c
    p = lax.div(i, 2)
    y = lax.rem(p, 4)
    z = lax.div(p, 4)
    x = lax.div(j, 2)
    side = lax.rem(j, 2)
    yp, ym, y2 = lax.rem(y + 1, 4), lax.rem(y + 3, 4), lax.rem(y + 2, 4)
    zp, zm, z2 = lax.rem(z + 1, 4), lax.rem(z + 3, 4), lax.rem(z + 2, 4)
    zn = lax.rem(z + 3 + 2 * side, 4)

    def place(yy, zz, cc):
        return {"dp": (zz * 4 + yy) * 2 + cc}

    sib = place(y, z, o)
    up_y, down_y = place(yp, z, c), place(ym, z, c)
    up_z, down_z = place(y, zp, c), place(y, zm, c)

    near, far = pl.ds(0, 16), pl.ds(16, 16)

    def partners(q):
        to, fro = lax.rem(x + q, 4), lax.rem(x + 4 - q, 4)
        across = [
            (near, to * 2 + 1 - side, fro * 2 + 1 - side, {"expert": to * 2 + 1 - side}),
            (far, to * 2 + 1 - side, fro * 2 + 1 - side,
             {"dp": (zn * 4 + y) * 2 + c, "expert": to * 2 + 1 - side}),
        ]
        same = [(pl.ds(0, CAP), to * 2 + side, fro * 2 + side, {"expert": to * 2 + side})]
        return same if q else [], across

    numbers = {}

    def number(*name):
        return numbers.setdefault(name, len(numbers))

    sent = []

    def send(src, dst, name, to):
        k = number(*name)
        copy = pltpu.make_async_remote_copy(
            src_ref=src, dst_ref=dst, send_sem=ss.at[k], recv_sem=rs.at[k],
            device_id=to, device_id_type=MESH,
        )
        copy.start()
        sent.append(copy)

    def arrived(ref, *name):
        k = number(*name)
        pltpu.make_async_remote_copy(
            src_ref=ref, dst_ref=ref, send_sem=ss.at[k], recv_sem=rs.at[k],
            device_id=sib, device_id_type=MESH,
        ).wait_recv()

    def fetch(src, dst, *name):
        copy = pltpu.make_async_copy(src, dst, rs.at[number(*name)])
        copy.start()
        return copy

    f = pl.ds(pl.multiple_of(c * 64, 64), 64)
    g = pl.ds(pl.multiple_of(o * 64, 64), 64)

    def units(core, k):
        return pl.ds(pl.multiple_of(core * HH + CO[k], 128), CW[k])

    own, other = [[], []], [[], []]
    for k in range(2):
        for n, w_ref in enumerate((wg_ref, wu_ref, wd_ref)):
            cols = pl.ds(n * CW[k], CW[k])
            other[k].append(
                fetch(w_ref.at[0, :, units(o, k)], WO[k].at[:, cols], "other", k, n)
            )
            own[k].append(
                fetch(w_ref.at[0, :, units(c, k)], W[k].at[y, z, f, cols], "own", k, n)
            )
    loads = [
        fetch(rt_hbm, rt_ref, "load", "r"),
        fetch(gs_hbm, gs_ref, "load", "s"),
        fetch(tok_hbm, tok_ref, "load", "x"),
        fetch(do_hbm, do_ref, "load", "d"),
    ]
    barrier = pltpu.get_barrier_semaphore()
    greet = [sib, up_y, down_y, up_z, down_z]
    for q in range(4):
        same, across = partners(q)
        greet += [to for _, _, _, to in same + across]
    for to in greet:
        pl.semaphore_signal(barrier, inc=1, device_id=to, device_id_type=MESH)
    for k in range(2):
        for copy in other[k] + own[k]:
            copy.wait()
    pl.semaphore_wait(barrier, len(greet))

    def along(k, yy, zz, piece, name, to):
        send(W[k].at[yy, zz, piece], W[k].at[yy, zz, piece], (k,) + name, to)

    def here(k, yy, zz, piece, *name):
        arrived(W[k].at[yy, zz, piece], k, *name)

    def leave(k, kind, piece, way):
        to_z, to_y = (up_z, up_y) if way == "up" else (down_z, down_y)
        along(k, y, z, piece, ("gz", kind, way), to_z)
        along(k, y, z, piece, ("gy", 0, kind, way), to_y)

    for k in range(2):
        send(WO[k], W[k].at[y, z, f], ("sib", k), sib)
    leave(0, "f", f, "up")
    arrived(W[0].at[y, z, g], "sib", 0)
    leave(0, "g", g, "down")
    leave(0, "g", g, "up")
    leave(0, "f", f, "down")
    leave(1, "f", f, "up")
    arrived(W[1].at[y, z, g], "sib", 1)
    leave(1, "g", g, "down")
    leave(1, "g", g, "up")
    leave(1, "f", f, "down")

    shape = (ROWS, TOK)
    row = lax.broadcasted_iota(jnp.int32, shape, 0)
    row_e = lax.div(row, CAP)
    row_s = lax.rem(row, CAP).astype(F32)
    for copy in loads[:2]:
        copy.wait()
    scale = gs_ref[...]
    combine = scale / jnp.sum(scale, axis=0, keepdims=True)
    routes = rt_ref[...]
    named = jnp.zeros(shape, F32)
    weight = jnp.zeros(shape, F32)
    for s in range(6):
        same = routes[s:s + 1, :] == row_e
        named = jnp.where(same, 1.0, named)
        weight = jnp.where(same, combine[s:s + 1, :], weight)
    earlier = (
        lax.broadcasted_iota(jnp.int32, (TOK, TOK), 0)
        < lax.broadcasted_iota(jnp.int32, (TOK, TOK), 1)
    ).astype(F32).astype(BF16)
    position = jnp.dot(named.astype(BF16), earlier, preferred_element_type=F32)
    chosen = jnp.where(position == row_s, named, 0.0)
    weight = weight * chosen
    slot_weight = jnp.sum(weight, axis=1, keepdims=True)
    select = chosen.astype(BF16)
    SEL[0] = select
    rest = weight
    for n in range(1, 4):
        part = rest.astype(BF16)
        SEL[n] = part
        rest = rest - part.astype(F32)

    def columns(ref, yy):
        return jnp.concatenate(
            [ref[:, (zz * 4 + yy) * SH:(zz * 4 + yy + 1) * SH] for zz in range(NZ)], axis=1
        )

    for copy in loads[2:]:
        copy.wait()
    for yy in range(NY):
        rows = jnp.dot(select, columns(tok_ref, yy), preferred_element_type=F32)
        SX[yy] = rows.astype(BF16).reshape(NE, CAP, YB)
        rows = jnp.dot(select, columns(do_ref, yy), preferred_element_type=F32)
        SD[yy] = (rows * slot_weight).astype(BF16).reshape(NE, CAP, YB)

    mine = c * NE + j
    rows_out = ((SX, X, "x"), (SD, D, "d"))

    def exchange(crossing):
        for src, dst, what in rows_out:
            for q in range(4):
                for rows, to, _, device in partners(q)[crossing]:
                    which = 0 if rows is near else 1
                    send(src.at[:, to, rows], dst.at[:, mine, rows],
                         ("to", what, crossing, q, which), device)

    exchange(0)
    local = [fetch(src.at[:, j], dst.at[:, mine], "keep", what) for src, dst, what in rows_out]

    def spread_y(k, step, zz, piece, kind):
        along(k, y, zz, piece, ("gy", step, kind, "up"), up_y)
        along(k, y, zz, piece, ("gy", step, kind, "down"), down_y)

    def onward_f(k, step, zz):
        here(k, ym, zz, f, "gy", step, "f", "up")
        along(k, ym, zz, f, ("gy", step, "f", "on"), up_y)

    def onward_g(k, step, zz):
        here(k, yp, zz, g, "gy", step, "g", "down")
        along(k, yp, zz, g, ("gy", step, "g", "on"), down_y)

    def onward_z(k):
        here(k, y, zm, f, "gz", "f", "up")
        along(k, y, zm, f, ("gz", "f", "on"), up_z)
        here(k, y, zp, g, "gz", "g", "down")
        along(k, y, zp, g, ("gz", "g", "on"), down_z)

    onward_f(0, 0, z)
    onward_g(0, 0, z)
    onward_z(0)
    spread_y(0, 1, zm, f, "f")
    spread_y(0, 2, zp, g, "g")
    exchange(1)
    onward_f(1, 0, z)
    onward_g(1, 0, z)
    here(0, y, zm, g, "gz", "g", "up")
    spread_y(0, 1, zm, g, "g")
    here(0, y, zp, f, "gz", "f", "down")
    spread_y(0, 2, zp, f, "f")
    onward_z(1)
    onward_f(0, 1, zm)
    onward_g(0, 2, zp)
    here(0, y, z2, f, "gz", "f", "on")
    spread_y(0, 3, z2, f, "f")
    here(0, y, z2, g, "gz", "g", "on")
    spread_y(0, 3, z2, g, "g")
    here(1, y, zm, g, "gz", "g", "up")
    here(1, y, zp, f, "gz", "f", "down")
    for step, zz in ((1, zm), (2, zp)):
        spread_y(1, step, zz, f, "f")
        spread_y(1, step, zz, g, "g")
    onward_g(0, 1, zm)
    onward_f(0, 2, zp)
    onward_f(0, 3, z2)
    onward_g(0, 3, z2)
    for step, zz in ((1, zm), (2, zp)):
        onward_f(1, step, zz)
        onward_g(1, step, zz)
    for n, (_, dst, what) in enumerate(rows_out):
        local[n].wait()
        for q in range(4):
            for crossing in range(2):
                for rows, _, fro, _ in partners(q)[crossing]:
                    which = 0 if rows is near else 1
                    arrived(dst.at[:, c * NE + fro, rows], "to", what, crossing, q, which)
        block = dst.at[:, pl.ds(c * NE, NE)]
        send(block, block, ("rows", what), sib)

    def turn(m, first, last):
        def body(step, carry):
            yy = lax.rem(y2 + step, NY)
            cols = pl.ds(pl.multiple_of(m * ROWS, ROWS), ROWS)
            blocks = pl.ds(m * NE, NE)
            XT[yy, :, cols] = X[yy, blocks].reshape(ROWS, YB).T
            DT[yy, :, cols] = D[yy, blocks].reshape(ROWS, YB).T
            return carry

        lax.fori_loop(first, last, body, 0)

    tiles = (
        ((0, 0, 256), (0, 256, 512), (1, 512, 768)),
        ((0, 0, 256), (1, 256, 384)),
    )

    def accumulate(k, yy, m, first=False):
        rows = pl.ds(pl.multiple_of(m * ROWS, ROWS), ROWS)
        blocks = pl.ds(m * NE, NE)
        for which, lo, hi in tiles[k]:
            got = jnp.dot(
                (X, D)[which][yy, blocks].reshape(ROWS, YB),
                W[k][yy, :, :, lo:hi].reshape(YB, hi - lo),
                preferred_element_type=F32,
            )
            if first:
                ACC[k][rows, lo:hi] = got
            else:
                ACC[k][rows, lo:hi] += got

    steps = ((0, z), (1, zm), (2, zp), (3, z2))

    def wait_m(k):
        for step, zz in steps:
            here(k, ym, zz, g, "gy", step, "g", "up")

    def wait_p(k):
        for step, zz in steps:
            here(k, yp, zz, f, "gy", step, "f", "down")

    def wait_2(k):
        for step, zz in steps:
            here(k, y2, zz, f, "gy", step, "f", "on")
            here(k, y2, zz, g, "gy", step, "g", "on")

    turn(c, 0, NY)
    here(1, y, z2, f, "gz", "f", "on")
    spread_y(1, 3, z2, f, "f")
    here(1, y, z2, g, "gz", "g", "on")
    spread_y(1, 3, z2, g, "g")
    accumulate(0, y, c, True)
    wait_m(0)
    accumulate(0, ym, c)
    wait_p(0)
    accumulate(0, yp, c)
    wait_2(0)
    accumulate(0, y2, c)
    arrived(X.at[:, pl.ds(o * NE, NE)], "rows", "x")
    arrived(D.at[:, pl.ds(o * NE, NE)], "rows", "d")
    turn(o, 0, 1)
    accumulate(0, y, o, True)
    accumulate(0, ym, o)
    accumulate(0, yp, o)
    accumulate(0, y2, o)

    def activate(k):
        w = CW[k]

        def body(m, carry):
            rows = pl.ds(pl.multiple_of(m * 64, 64), 64)
            gate, up, d_hidden = (ACC[k][rows, n * w:(n + 1) * w] for n in range(3))
            sig = jax.nn.sigmoid(gate)
            act = gate * sig
            CAT[k][rows, 0:w] = (
                d_hidden * up * sig * (1.0 + gate * (1.0 - sig))
            ).astype(BF16)
            CAT[k][rows, w:2 * w] = (d_hidden * act).astype(BF16)
            CAT[k][rows, 2 * w:3 * w] = (act * up).astype(BF16)
            return carry

        lax.fori_loop(0, 2 * ROWS // 64, body, 0)

    def partials(k, yy):
        for which, lo, hi in tiles[k]:
            got = jnp.dot(
                (XT, DT)[which][yy], CAT[k][:, lo:hi], preferred_element_type=F32
            )
            T[k][yy, :, :, lo:hi] = got.astype(BF16).reshape(NZ, SH, hi - lo)

    def partial(k, yy, zz):
        rows = pl.ds(pl.multiple_of(zz * SH, SH), SH)
        for which, lo, hi in tiles[k]:
            got = jnp.dot(
                (XT, DT)[which][yy, rows], CAT[k][:, lo:hi], preferred_element_type=F32
            )
            T[k][yy, zz, :, lo:hi] = got.astype(BF16)

    nt = (((1,), (1,)), ((), ()))

    def output(side_, n, yy):
        rows = pl.ds(pl.multiple_of(side_ * ROWS, ROWS), ROWS)
        total = None
        for k in range(2):
            lo, hi = ((2 * CW[k], 3 * CW[k]), (0, 2 * CW[k]))[n]
            got = lax.dot_general(
                CAT[k][rows, lo:hi], W[k][yy, :, :, lo:hi].reshape(YB, hi - lo), nt,
                preferred_element_type=F32,
            )
            total = got if total is None else total + got
        return total

    def output_sibling(n):
        for yy in range(NY):
            OS[n, yy] = output(o, n, yy).astype(BF16).reshape(NE, CAP, YB)
            send(OS.at[n, yy], OR.at[n, yy], ("part", n, yy), sib)

    def output_own(n):
        for yy in range(NY):
            value = output(c, n, yy)
            arrived(OR.at[n, yy], "part", n, yy)
            value = value + OR[n, yy].reshape(ROWS, YB).astype(F32)
            BS[n, yy] = value.astype(BF16).reshape(NE, CAP, YB)

    def give_back(n, crossing):
        for q in range(4):
            for rows, to, _, device in partners(q)[crossing]:
                which = 0 if rows is near else 1
                send(BS.at[n, :, to, rows], BK.at[n, :, j, rows],
                     ("back", n, crossing, q, which), device)

    def first_f(k, step, zz):
        send(T[k].at[y2, zz, f], R1[k].at[0, step], ("r1", k, step, "f"), up_y)

    def first_g(k, step, zz):
        send(T[k].at[y2, zz, g], R1[k].at[1, step], ("r1", k, step, "g"), down_y)

    def plain_g(k, step, zz):
        send(T[k].at[yp, zz, g], R2[k].at[0, step, g], ("r2", k, step, "g", "up"), up_y)

    def plain_f(k, step, zz):
        send(T[k].at[ym, zz, f], R2[k].at[1, step, f], ("r2", k, step, "f", "down"), down_y)

    def joined_f(k, step, zz):
        arrived(R1[k].at[0, step], "r1", k, step, "f")
        T[k][yp, zz, f] = (
            T[k][yp, zz, f].astype(F32) + R1[k][0, step].astype(F32)
        ).astype(BF16)
        send(T[k].at[yp, zz, f], R2[k].at[0, step, f], ("r2", k, step, "f", "up"), up_y)

    def joined_g(k, step, zz):
        arrived(R1[k].at[1, step], "r1", k, step, "g")
        T[k][ym, zz, g] = (
            T[k][ym, zz, g].astype(F32) + R1[k][1, step].astype(F32)
        ).astype(BF16)
        send(T[k].at[ym, zz, g], R2[k].at[1, step, g], ("r2", k, step, "g", "down"), down_y)

    def summed_y(k, step, zz, piece, kind):
        for d in range(2):
            arrived(R2[k].at[d, step, piece], "r2", k, step, kind, ("up", "down")[d])
        return (
            T[k][y, zz, piece].astype(F32)
            + R2[k][0, step, piece].astype(F32)
            + R2[k][1, step, piece].astype(F32)
        )

    def far_z(k):
        ZS[k][0, f] = summed_y(k, 0, z2, f, "f").astype(BF16)
        send(ZS[k].at[0, f], Z1[k].at[0], ("z1", k, "f"), up_z)
        ZS[k][0, g] = summed_y(k, 0, z2, g, "g").astype(BF16)
        send(ZS[k].at[0, g], Z1[k].at[1], ("z1", k, "g"), down_z)

    def plain_z(k):
        ZS[k][2, f] = summed_y(k, 2, zm, f, "f").astype(BF16)
        send(ZS[k].at[2, f], Z2[k].at[1, f], ("z2", k, "f", "down"), down_z)
        ZS[k][1, g] = summed_y(k, 1, zp, g, "g").astype(BF16)
        send(ZS[k].at[1, g], Z2[k].at[0, g], ("z2", k, "g", "up"), up_z)

    def joined_z(k):
        total = summed_y(k, 1, zp, f, "f")
        arrived(Z1[k].at[0], "z1", k, "f")
        ZS[k][1, f] = (total + Z1[k][0].astype(F32)).astype(BF16)
        send(ZS[k].at[1, f], Z2[k].at[0, f], ("z2", k, "f", "up"), up_z)
        total = summed_y(k, 2, zm, g, "g")
        arrived(Z1[k].at[1], "z1", k, "g")
        ZS[k][2, g] = (total + Z1[k][1].astype(F32)).astype(BF16)
        send(ZS[k].at[2, g], Z2[k].at[1, g], ("z2", k, "g", "down"), down_z)

    def total_z(k, piece, kind):
        total = summed_y(k, 3, z, piece, kind)
        arrived(Z2[k].at[0, piece], "z2", k, kind, "up")
        arrived(Z2[k].at[1, piece], "z2", k, kind, "down")
        return total + Z2[k][0, piece].astype(F32) + Z2[k][1, piece].astype(F32)

    grads = (gg_ref, gu_ref, gd_ref)

    def finish(k):
        w = CW[k]
        FS[k][...] = total_z(k, g, "g")
        send(FS[k], FR[k], ("fin", k), sib)
        total = total_z(k, f, "f")
        for n, ref in enumerate(grads):
            ref[0, :, units(c, k)] = total[:, n * w:(n + 1) * w]

    def close(k):
        w = CW[k]
        arrived(FR[k], "fin", k)
        for n, ref in enumerate(grads):
            ref[0, :, units(o, k)] = FR[k][:, n * w:(n + 1) * w]

    activate(0)
    onward_f(1, 3, z2)
    onward_g(1, 3, z2)
    partial(0, y2, z2)
    first_f(0, 0, z2)
    first_g(0, 0, z2)
    turn(o, 1, NY)
    partial(0, yp, z2)
    plain_g(0, 0, z2)
    partial(0, ym, z2)
    plain_f(0, 0, z2)
    partial(0, y2, zm)
    first_f(0, 2, zm)
    partial(0, y2, zp)
    first_g(0, 1, zp)
    for m, first in ((c, True), (o, True)):
        accumulate(1, y, m, first)
    wait_m(1)
    wait_p(1)
    for m in (c, o):
        accumulate(1, ym, m)
        accumulate(1, yp, m)
    wait_2(1)
    for m in (c, o):
        accumulate(1, y2, m)
    activate(1)
    output_sibling(0)
    joined_f(0, 0, z2)
    joined_g(0, 0, z2)
    partial(0, yp, zp)
    plain_g(0, 1, zp)
    partial(0, ym, zm)
    plain_f(0, 2, zm)
    output_own(0)
    give_back(0, 1)
    local = [fetch(BS.at[0, :, j], BK.at[0, :, j], "stay", 0)]
    for yy in (y2, yp, ym):
        partial(1, yy, z2)
    first_f(1, 0, z2)
    first_g(1, 0, z2)
    plain_g(1, 0, z2)
    plain_f(1, 0, z2)
    partial(0, yp, zm)
    partial(0, ym, zp)
    joined_f(0, 2, zm)
    joined_g(0, 1, zp)
    first_f(0, 1, zp)
    first_g(0, 2, zm)
    plain_g(0, 2, zm)
    plain_f(0, 1, zp)
    output_sibling(1)
    partial(0, y, z2)
    far_z(0)
    output_own(1)
    local.append(fetch(BS.at[1, :, j], BK.at[1, :, j], "stay", 1))
    joined_f(1, 0, z2)
    joined_g(1, 0, z2)
    for zz in (zm, zp, z):
        partial(0, y, zz)
    for yy in (y2, yp, ym):
        partial(0, yy, z)
    give_back(0, 0)
    for yy in (y2, yp, ym):
        for zz in (zm, zp, z):
            partial(1, yy, zz)
    partials(1, y)
    plain_z(0)
    give_back(1, 1)
    joined_f(0, 1, zp)
    joined_g(0, 2, zm)
    first_f(0, 3, z)
    first_g(0, 3, z)
    first_f(1, 2, zm)
    first_g(1, 1, zp)
    first_f(1, 1, zp)
    first_g(1, 2, zm)
    plain_g(0, 3, z)
    plain_f(0, 3, z)
    plain_g(1, 1, zp)
    plain_f(1, 2, zm)
    far_z(1)
    joined_z(0)
    give_back(1, 0)
    joined_f(1, 2, zm)
    joined_g(1, 1, zp)
    first_f(1, 3, z)
    first_g(1, 3, z)
    plain_g(1, 2, zm)
    plain_f(1, 1, zp)
    joined_f(1, 1, zp)
    joined_g(1, 2, zm)
    joined_f(0, 3, z)
    joined_g(0, 3, z)
    plain_g(1, 3, z)
    plain_f(1, 3, z)
    plain_z(1)
    joined_f(1, 3, z)
    joined_g(1, 3, z)
    joined_z(1)

    for n in range(2):
        local[n].wait()
        for q in range(4):
            for crossing in range(2):
                for rows, _, fro, _ in partners(q)[crossing]:
                    which = 0 if rows is near else 1
                    arrived(BK.at[n, :, fro, rows], "back", n, crossing, q, which)
    tn = (((0,), (0,)), ((), ()))
    for yy in range(NY):
        back = BK[0, yy].reshape(ROWS, YB)
        out = sum(
            lax.dot_general(SEL[n], back, tn, preferred_element_type=F32) for n in (3, 2, 1)
        )
        back = BK[1, yy].reshape(ROWS, YB)
        d_in = lax.dot_general(SEL[0], back, tn, preferred_element_type=F32)
        for zz in range(NZ):
            cols = slice((zz * 4 + yy) * SH, (zz * 4 + yy + 1) * SH)
            lo_ref[:, cols] = out[:, zz * SH:(zz + 1) * SH].astype(BF16)
            dt_ref[:, cols] = d_in[:, zz * SH:(zz + 1) * SH].astype(BF16)

    finish(0)
    finish(1)
    close(0)
    close(1)

    for copy in sent:
        copy.wait_send()
    assert len(numbers) <= N_SEM


def hand_out(*refs):
    count = len(refs) // 2
    done = refs[-1]
    copies = [
        pltpu.make_async_copy(refs[n], refs[count + n], done.at[n]) for n in range(count)
    ]
    for copy in copies:
        copy.start()
    for copy in copies:
        copy.wait()


def shards(tokens, routes, gate_scale, w_gate, w_up, w_down, d_out):
    vm = pl.BlockSpec(memory_space=pltpu.VMEM)
    hbm = pl.BlockSpec(memory_space=pltpu.HBM)
    grad = jax.ShapeDtypeStruct(w_gate.shape, F32)
    rows = jax.ShapeDtypeStruct(tokens.shape, BF16)
    results = (rows, rows, grad, grad, grad)

    def chunks(kind, *lead):
        return [pltpu.VMEM((*lead, 3 * w), kind) for w in CW]

    found = pl.pallas_call(
        kernel,
        out_shape=results,
        in_specs=[hbm] * 7,
        out_specs=(vm,) * 5,
        scratch_shapes=[
            *chunks(BF16, NY, NZ, SH),
            *chunks(BF16, 64),
            pltpu.VMEM((NY, 2 * NE, CAP, YB), BF16),
            pltpu.VMEM((NY, 2 * NE, CAP, YB), BF16),
            pltpu.VMEM((NY, YB, 2 * ROWS), BF16),
            pltpu.VMEM((NY, YB, 2 * ROWS), BF16),
            pltpu.VMEM((NY, NE, CAP, YB), BF16),
            pltpu.VMEM((NY, NE, CAP, YB), BF16),
            pltpu.VMEM((4, ROWS, TOK), BF16),
            *chunks(F32, 2 * ROWS),
            *chunks(BF16, 2 * ROWS),
            *chunks(BF16, NY, NZ, SH),
            *chunks(BF16, 2, NZ, 64),
            *chunks(BF16, 2, NZ, SH),
            *chunks(BF16, 2, 64),
            *chunks(BF16, 2, SH),
            *chunks(BF16, 3, SH),
            *chunks(F32, 64),
            *chunks(F32, 64),
            pltpu.VMEM((2, NY, NE, CAP, YB), BF16),
            pltpu.VMEM((2, NY, NE, CAP, YB), BF16),
            pltpu.VMEM((2, NY, NE, CAP, YB), BF16),
            pltpu.VMEM((2, NY, NE, CAP, YB), BF16),
            pltpu.VMEM(tokens.shape, BF16),
            pltpu.VMEM(tokens.shape, BF16),
            pltpu.VMEM(routes.shape[::-1], jnp.int32),
            pltpu.VMEM(routes.shape[::-1], F32),
            pltpu.SemaphoreType.DMA((N_SEM,)),
            pltpu.SemaphoreType.DMA((N_SEM,)),
        ],
        compiler_params=pltpu.CompilerParams(
            collective_id=0, has_side_effects=True, vmem_limit_bytes=VMEM_MB * 1024 * 1024
        ),
    )(*(
        pltpu.with_memory_space_constraint(value, pltpu.HBM)
        for value in (tokens, routes.T, gate_scale.T, w_gate, w_up, w_down, d_out)
    ))
    return pl.pallas_call(
        hand_out,
        out_shape=results,
        in_specs=[vm] * 5,
        out_specs=(hbm,) * 5,
        scratch_shapes=[pltpu.SemaphoreType.DMA((5,))],
        compiler_params=pltpu.CompilerParams(vmem_limit_bytes=8 * 1024 * 1024),
    )(*found)


def solution(mesh):
    tok = P(("dp", "expert"), None)
    wei = P("expert", "dp", None)
    return jax.shard_map(
        shards,
        mesh=mesh,
        in_specs=(tok, tok, tok, wei, wei, wei, tok),
        out_specs=(tok, tok, wei, wei, wei),
        check_vma=False,
    )
```

```python
import jax
import jax.numpy as jnp
from jax import lax
from jax.experimental import pallas as pl
from jax.experimental.pallas import tpu as pltpu
from jax.sharding import PartitionSpec as P

CAP = 32
MESH = pl.DeviceIdType.MESH
F32 = jnp.float32
BF16 = jnp.bfloat16

NY, NZ, SH = 4, 4, 128
HH = 384
CW = (256, 128)
CO = (0, 256)
YB = NZ * SH
NE = 8
TOK = 192
ROWS = NE * CAP
N_SEM = 240
VMEM_MB = 50


def kernel(
    tok_hbm, rt_hbm, gs_hbm, wg_ref, wu_ref, wd_ref, do_hbm,
    lo_ref, dt_ref, gg_ref, gu_ref, gd_ref,
    W0, W1, WO0, WO1, X, D, XT, DT, SX, SD, SEL, A0, A1, C0, C1, T0, T1,
    RF0, RF1, RS0, RS1, ZF0, ZF1, Z20, Z21, ZS0, ZS1, FS0, FS1, FR0, FR1,
    OS, OR, BS, BK, tok_ref, do_ref, rt_ref, gs_ref, ss, rs,
):
    W, WO, ACC, CAT, T = (W0, W1), (WO0, WO1), (A0, A1), (C0, C1), (T0, T1)
    R1, R2, Z1, Z2, ZS = (RF0, RF1), (RS0, RS1), (ZF0, ZF1), (Z20, Z21), (ZS0, ZS1)
    FS, FR = (FS0, FS1), (FR0, FR1)
    i = lax.axis_index("dp")
    j = lax.axis_index("expert")
    c = lax.rem(i, 2)
    o = 1 - c
    p = lax.div(i, 2)
    y = lax.rem(p, 4)
    z = lax.div(p, 4)
    x = lax.div(j, 2)
    side = lax.rem(j, 2)
    yp, ym, y2 = lax.rem(y + 1, 4), lax.rem(y + 3, 4), lax.rem(y + 2, 4)
    zp, zm, z2 = lax.rem(z + 1, 4), lax.rem(z + 3, 4), lax.rem(z + 2, 4)
    zn = lax.rem(z + 3 + 2 * side, 4)

    def place(yy, zz, cc):
        return {"dp": (zz * 4 + yy) * 2 + cc}

    sib = place(y, z, o)
    up_y, down_y = place(yp, z, c), place(ym, z, c)
    up_z, down_z = place(y, zp, c), place(y, zm, c)

    near, far = pl.ds(0, 16), pl.ds(16, 16)

    def partners(q):
        to, fro = lax.rem(x + q, 4), lax.rem(x + 4 - q, 4)
        across = [
            (near, to * 2 + 1 - side, fro * 2 + 1 - side, {"expert": to * 2 + 1 - side}),
            (far, to * 2 + 1 - side, fro * 2 + 1 - side,
             {"dp": (zn * 4 + y) * 2 + c, "expert": to * 2 + 1 - side}),
        ]
        same = [(pl.ds(0, CAP), to * 2 + side, fro * 2 + side, {"expert": to * 2 + side})]
        return same if q else [], across

    numbers = {}

    def number(*name):
        return numbers.setdefault(name, len(numbers))

    sent = []

    def send(src, dst, name, to):
        k = number(*name)
        copy = pltpu.make_async_remote_copy(
            src_ref=src, dst_ref=dst, send_sem=ss.at[k], recv_sem=rs.at[k],
            device_id=to, device_id_type=MESH,
        )
        copy.start()
        sent.append(copy)

    def arrived(ref, *name):
        k = number(*name)
        pltpu.make_async_remote_copy(
            src_ref=ref, dst_ref=ref, send_sem=ss.at[k], recv_sem=rs.at[k],
            device_id=sib, device_id_type=MESH,
        ).wait_recv()

    def fetch(src, dst, *name):
        copy = pltpu.make_async_copy(src, dst, rs.at[number(*name)])
        copy.start()
        return copy

    f = pl.ds(pl.multiple_of(c * 64, 64), 64)
    g = pl.ds(pl.multiple_of(o * 64, 64), 64)

    def units(core, k):
        return pl.ds(pl.multiple_of(core * HH + CO[k], 128), CW[k])

    own, other = [[], []], [[], []]
    for k in range(2):
        for n, w_ref in enumerate((wg_ref, wu_ref, wd_ref)):
            cols = pl.ds(n * CW[k], CW[k])
            other[k].append(
                fetch(w_ref.at[0, :, units(o, k)], WO[k].at[:, cols], "other", k, n)
            )
            own[k].append(
                fetch(w_ref.at[0, :, units(c, k)], W[k].at[y, z, f, cols], "own", k, n)
            )
    loads = [
        fetch(rt_hbm, rt_ref, "load", "r"),
        fetch(gs_hbm, gs_ref, "load", "s"),
        fetch(tok_hbm, tok_ref, "load", "x"),
        fetch(do_hbm, do_ref, "load", "d"),
    ]
    barrier = pltpu.get_barrier_semaphore()
    greet = [sib, up_y, down_y, up_z, down_z]
    for q in range(4):
        same, across = partners(q)
        greet += [to for _, _, _, to in same + across]
    for to in greet:
        pl.semaphore_signal(barrier, inc=1, device_id=to, device_id_type=MESH)
    for k in range(2):
        for copy in other[k] + own[k]:
            copy.wait()
    pl.semaphore_wait(barrier, len(greet))

    def along(k, yy, zz, piece, name, to):
        send(W[k].at[yy, zz, piece], W[k].at[yy, zz, piece], (k,) + name, to)

    def here(k, yy, zz, piece, *name):
        arrived(W[k].at[yy, zz, piece], k, *name)

    def leave(k, kind, piece, way):
        to_z, to_y = (up_z, up_y) if way == "up" else (down_z, down_y)
        along(k, y, z, piece, ("gz", kind, way), to_z)
        along(k, y, z, piece, ("gy", 0, kind, way), to_y)

    for k in range(2):
        send(WO[k], W[k].at[y, z, f], ("sib", k), sib)
    leave(0, "f", f, "up")
    arrived(W[0].at[y, z, g], "sib", 0)
    leave(0, "g", g, "down")
    leave(0, "g", g, "up")
    leave(0, "f", f, "down")
    leave(1, "f", f, "up")
    arrived(W[1].at[y, z, g], "sib", 1)
    leave(1, "g", g, "down")
    leave(1, "g", g, "up")
    leave(1, "f", f, "down")

    shape = (ROWS, TOK)
    row = lax.broadcasted_iota(jnp.int32, shape, 0)
    row_e = lax.div(row, CAP)
    row_s = lax.rem(row, CAP).astype(F32)
    for copy in loads[:2]:
        copy.wait()
    scale = gs_ref[...]
    combine = scale / jnp.sum(scale, axis=0, keepdims=True)
    routes = rt_ref[...]
    named = jnp.zeros(shape, F32)
    weight = jnp.zeros(shape, F32)
    for s in range(6):
        same = routes[s:s + 1, :] == row_e
        named = jnp.where(same, 1.0, named)
        weight = jnp.where(same, combine[s:s + 1, :], weight)
    earlier = (
        lax.broadcasted_iota(jnp.int32, (TOK, TOK), 0)
        < lax.broadcasted_iota(jnp.int32, (TOK, TOK), 1)
    ).astype(F32).astype(BF16)
    position = jnp.dot(named.astype(BF16), earlier, preferred_element_type=F32)
    chosen = jnp.where(position == row_s, named, 0.0)
    weight = weight * chosen
    slot_weight = jnp.sum(weight, axis=1, keepdims=True)
    select = chosen.astype(BF16)
    SEL[0] = select
    rest = weight
    for n in range(1, 4):
        part = rest.astype(BF16)
        SEL[n] = part
        rest = rest - part.astype(F32)

    def columns(ref, yy):
        return jnp.concatenate(
            [ref[:, (zz * 4 + yy) * SH:(zz * 4 + yy + 1) * SH] for zz in range(NZ)], axis=1
        )

    for copy in loads[2:]:
        copy.wait()
    for yy in range(NY):
        rows = jnp.dot(select, columns(tok_ref, yy), preferred_element_type=F32)
        SX[yy] = rows.astype(BF16).reshape(NE, CAP, YB)
        rows = jnp.dot(select, columns(do_ref, yy), preferred_element_type=F32)
        SD[yy] = (rows * slot_weight).astype(BF16).reshape(NE, CAP, YB)

    mine = c * NE + j
    rows_out = ((SX, X, "x"), (SD, D, "d"))

    def exchange(crossing):
        for src, dst, what in rows_out:
            for q in range(4):
                for rows, to, _, device in partners(q)[crossing]:
                    which = 0 if rows is near else 1
                    send(src.at[:, to, rows], dst.at[:, mine, rows],
                         ("to", what, crossing, q, which), device)

    exchange(0)
    local = [fetch(src.at[:, j], dst.at[:, mine], "keep", what) for src, dst, what in rows_out]

    def spread_y(k, step, zz, piece, kind):
        along(k, y, zz, piece, ("gy", step, kind, "up"), up_y)
        along(k, y, zz, piece, ("gy", step, kind, "down"), down_y)

    def onward_f(k, step, zz):
        here(k, ym, zz, f, "gy", step, "f", "up")
        along(k, ym, zz, f, ("gy", step, "f", "on"), up_y)

    def onward_g(k, step, zz):
        here(k, yp, zz, g, "gy", step, "g", "down")
        along(k, yp, zz, g, ("gy", step, "g", "on"), down_y)

    def onward_z(k):
        here(k, y, zm, f, "gz", "f", "up")
        along(k, y, zm, f, ("gz", "f", "on"), up_z)
        here(k, y, zp, g, "gz", "g", "down")
        along(k, y, zp, g, ("gz", "g", "on"), down_z)

    onward_f(0, 0, z)
    onward_g(0, 0, z)
    onward_z(0)
    spread_y(0, 1, zm, f, "f")
    spread_y(0, 2, zp, g, "g")
    exchange(1)
    onward_f(1, 0, z)
    onward_g(1, 0, z)
    here(0, y, zm, g, "gz", "g", "up")
    spread_y(0, 1, zm, g, "g")
    here(0, y, zp, f, "gz", "f", "down")
    spread_y(0, 2, zp, f, "f")
    onward_z(1)
    onward_f(0, 1, zm)
    onward_g(0, 2, zp)
    here(0, y, z2, f, "gz", "f", "on")
    spread_y(0, 3, z2, f, "f")
    here(0, y, z2, g, "gz", "g", "on")
    spread_y(0, 3, z2, g, "g")
    here(1, y, zm, g, "gz", "g", "up")
    here(1, y, zp, f, "gz", "f", "down")
    for step, zz in ((1, zm), (2, zp)):
        spread_y(1, step, zz, f, "f")
        spread_y(1, step, zz, g, "g")
    onward_g(0, 1, zm)
    onward_f(0, 2, zp)
    def fro(q, crossing):
        return lax.rem(x + 4 - q, 4) * 2 + (1 - side if crossing else side)

    def pass_on(crossing):
        for n, (_, dst, what) in enumerate(rows_out):
            for q in range(4):
                if q == 0 and not crossing:
                    local[n].wait()
                for rows, _, block, _ in partners(q)[crossing]:
                    which = 0 if rows is near else 1
                    arrived(dst.at[:, c * NE + block, rows], "to", what, crossing, q, which)
                ready = dst.at[:, c * NE + fro(q, crossing)]
                send(ready, ready, ("rows", what, crossing, q), sib)

    pass_on(0)
    onward_f(0, 3, z2)
    onward_g(0, 3, z2)
    for step, zz in ((1, zm), (2, zp)):
        onward_f(1, step, zz)
        onward_g(1, step, zz)
    pass_on(1)

    def turn(m, first, last):
        def body(step, carry):
            yy = lax.rem(y2 + step, NY)
            cols = pl.ds(pl.multiple_of(m * ROWS, ROWS), ROWS)
            blocks = pl.ds(m * NE, NE)
            XT[yy, :, cols] = X[yy, blocks].reshape(ROWS, YB).T
            DT[yy, :, cols] = D[yy, blocks].reshape(ROWS, YB).T
            return carry

        lax.fori_loop(first, last, body, 0)

    tiles = (
        ((0, 0, 256), (0, 256, 512), (1, 512, 768)),
        ((0, 0, 256), (1, 256, 384)),
    )

    def accumulate(k, yy, m, first=False):
        rows = pl.ds(pl.multiple_of(m * ROWS, ROWS), ROWS)
        blocks = pl.ds(m * NE, NE)
        for which, lo, hi in tiles[k]:
            got = jnp.dot(
                (X, D)[which][yy, blocks].reshape(ROWS, YB),
                W[k][yy, :, :, lo:hi].reshape(YB, hi - lo),
                preferred_element_type=F32,
            )
            if first:
                ACC[k][rows, lo:hi] = got
            else:
                ACC[k][rows, lo:hi] += got

    steps = ((0, z), (1, zm), (2, zp), (3, z2))

    def wait_m(k):
        for step, zz in steps:
            here(k, ym, zz, g, "gy", step, "g", "up")

    def wait_p(k):
        for step, zz in steps:
            here(k, yp, zz, f, "gy", step, "f", "down")

    def wait_2(k):
        for step, zz in steps:
            here(k, y2, zz, f, "gy", step, "f", "on")
            here(k, y2, zz, g, "gy", step, "g", "on")

    turn(c, 0, 1)
    accumulate(0, y, c, True)
    wait_m(0)
    accumulate(0, ym, c)
    wait_p(0)
    accumulate(0, yp, c)
    here(1, y, z2, f, "gz", "f", "on")
    spread_y(1, 3, z2, f, "f")
    here(1, y, z2, g, "gz", "g", "on")
    spread_y(1, 3, z2, g, "g")
    for _, dst, what in rows_out:
        for crossing in range(2):
            for q in range(4):
                arrived(dst.at[:, o * NE + fro(q, crossing)], "rows", what, crossing, q)
    turn(o, 0, 1)
    accumulate(0, y, o, True)
    accumulate(0, ym, o)
    accumulate(0, yp, o)
    wait_2(0)
    accumulate(0, y2, c)
    accumulate(0, y2, o)

    def activate(k):
        w = CW[k]

        def body(m, carry):
            rows = pl.ds(pl.multiple_of(m * 64, 64), 64)
            gate, up, d_hidden = (ACC[k][rows, n * w:(n + 1) * w] for n in range(3))
            sig = jax.nn.sigmoid(gate)
            act = gate * sig
            CAT[k][rows, 0:w] = (
                d_hidden * up * sig * (1.0 + gate * (1.0 - sig))
            ).astype(BF16)
            CAT[k][rows, w:2 * w] = (d_hidden * act).astype(BF16)
            CAT[k][rows, 2 * w:3 * w] = (act * up).astype(BF16)
            return carry

        lax.fori_loop(0, 2 * ROWS // 64, body, 0)

    def partials(k, yy):
        for which, lo, hi in tiles[k]:
            got = jnp.dot(
                (XT, DT)[which][yy], CAT[k][:, lo:hi], preferred_element_type=F32
            )
            T[k][yy, :, :, lo:hi] = got.astype(BF16).reshape(NZ, SH, hi - lo)

    def partial(k, yy, zz):
        rows = pl.ds(pl.multiple_of(zz * SH, SH), SH)
        for which, lo, hi in tiles[k]:
            got = jnp.dot(
                (XT, DT)[which][yy, rows], CAT[k][:, lo:hi], preferred_element_type=F32
            )
            T[k][yy, zz, :, lo:hi] = got.astype(BF16)

    nt = (((1,), (1,)), ((), ()))

    def output(side_, n, yy):
        rows = pl.ds(pl.multiple_of(side_ * ROWS, ROWS), ROWS)
        total = None
        for k in range(2):
            lo, hi = ((2 * CW[k], 3 * CW[k]), (0, 2 * CW[k]))[n]
            got = lax.dot_general(
                CAT[k][rows, lo:hi], W[k][yy, :, :, lo:hi].reshape(YB, hi - lo), nt,
                preferred_element_type=F32,
            )
            total = got if total is None else total + got
        return total

    def output_sibling(n):
        for yy in range(NY):
            OS[n, yy] = output(o, n, yy).astype(BF16).reshape(NE, CAP, YB)
            send(OS.at[n, yy], OR.at[n, yy], ("part", n, yy), sib)

    def output_own(n):
        for yy in range(NY):
            value = output(c, n, yy)
            arrived(OR.at[n, yy], "part", n, yy)
            value = value + OR[n, yy].reshape(ROWS, YB).astype(F32)
            BS[n, yy] = value.astype(BF16).reshape(NE, CAP, YB)

    def give_back(n, crossing):
        for q in range(4):
            for rows, to, _, device in partners(q)[crossing]:
                which = 0 if rows is near else 1
                send(BS.at[n, :, to, rows], BK.at[n, :, j, rows],
                     ("back", n, crossing, q, which), device)

    def first_f(k, step, zz):
        send(T[k].at[y2, zz, f], R1[k].at[0, step], ("r1", k, step, "f"), up_y)

    def first_g(k, step, zz):
        send(T[k].at[y2, zz, g], R1[k].at[1, step], ("r1", k, step, "g"), down_y)

    def plain_g(k, step, zz):
        send(T[k].at[yp, zz, g], R2[k].at[0, step, g], ("r2", k, step, "g", "up"), up_y)

    def plain_f(k, step, zz):
        send(T[k].at[ym, zz, f], R2[k].at[1, step, f], ("r2", k, step, "f", "down"), down_y)

    def joined_f(k, step, zz):
        arrived(R1[k].at[0, step], "r1", k, step, "f")
        T[k][yp, zz, f] = (
            T[k][yp, zz, f].astype(F32) + R1[k][0, step].astype(F32)
        ).astype(BF16)
        send(T[k].at[yp, zz, f], R2[k].at[0, step, f], ("r2", k, step, "f", "up"), up_y)

    def joined_g(k, step, zz):
        arrived(R1[k].at[1, step], "r1", k, step, "g")
        T[k][ym, zz, g] = (
            T[k][ym, zz, g].astype(F32) + R1[k][1, step].astype(F32)
        ).astype(BF16)
        send(T[k].at[ym, zz, g], R2[k].at[1, step, g], ("r2", k, step, "g", "down"), down_y)

    def summed_y(k, step, zz, piece, kind):
        for d in range(2):
            arrived(R2[k].at[d, step, piece], "r2", k, step, kind, ("up", "down")[d])
        return (
            T[k][y, zz, piece].astype(F32)
            + R2[k][0, step, piece].astype(F32)
            + R2[k][1, step, piece].astype(F32)
        )

    def far_z(k):
        ZS[k][0, f] = summed_y(k, 0, z2, f, "f").astype(BF16)
        send(ZS[k].at[0, f], Z1[k].at[0], ("z1", k, "f"), up_z)
        ZS[k][0, g] = summed_y(k, 0, z2, g, "g").astype(BF16)
        send(ZS[k].at[0, g], Z1[k].at[1], ("z1", k, "g"), down_z)

    def plain_z(k):
        ZS[k][2, f] = summed_y(k, 2, zm, f, "f").astype(BF16)
        send(ZS[k].at[2, f], Z2[k].at[1, f], ("z2", k, "f", "down"), down_z)
        ZS[k][1, g] = summed_y(k, 1, zp, g, "g").astype(BF16)
        send(ZS[k].at[1, g], Z2[k].at[0, g], ("z2", k, "g", "up"), up_z)

    def joined_z(k):
        total = summed_y(k, 1, zp, f, "f")
        arrived(Z1[k].at[0], "z1", k, "f")
        ZS[k][1, f] = (total + Z1[k][0].astype(F32)).astype(BF16)
        send(ZS[k].at[1, f], Z2[k].at[0, f], ("z2", k, "f", "up"), up_z)
        total = summed_y(k, 2, zm, g, "g")
        arrived(Z1[k].at[1], "z1", k, "g")
        ZS[k][2, g] = (total + Z1[k][1].astype(F32)).astype(BF16)
        send(ZS[k].at[2, g], Z2[k].at[1, g], ("z2", k, "g", "down"), down_z)

    def total_z(k, piece, kind):
        total = summed_y(k, 3, z, piece, kind)
        arrived(Z2[k].at[0, piece], "z2", k, kind, "up")
        arrived(Z2[k].at[1, piece], "z2", k, kind, "down")
        return total + Z2[k][0, piece].astype(F32) + Z2[k][1, piece].astype(F32)

    grads = (gg_ref, gu_ref, gd_ref)

    def finish(k):
        w = CW[k]
        FS[k][...] = total_z(k, g, "g")
        send(FS[k], FR[k], ("fin", k), sib)
        total = total_z(k, f, "f")
        for n, ref in enumerate(grads):
            ref[0, :, units(c, k)] = total[:, n * w:(n + 1) * w]

    def close(k):
        w = CW[k]
        arrived(FR[k], "fin", k)
        for n, ref in enumerate(grads):
            ref[0, :, units(o, k)] = FR[k][:, n * w:(n + 1) * w]

    activate(0)
    onward_f(1, 3, z2)
    onward_g(1, 3, z2)
    partial(0, y2, z2)
    first_f(0, 0, z2)
    first_g(0, 0, z2)
    turn(c, 1, NY)
    turn(o, 1, NY)
    partial(0, yp, z2)
    plain_g(0, 0, z2)
    partial(0, ym, z2)
    plain_f(0, 0, z2)
    partial(0, y2, zm)
    first_f(0, 2, zm)
    partial(0, y2, zp)
    first_g(0, 1, zp)
    for m, first in ((c, True), (o, True)):
        accumulate(1, y, m, first)
    wait_m(1)
    wait_p(1)
    for m in (c, o):
        accumulate(1, ym, m)
        accumulate(1, yp, m)
    wait_2(1)
    for m in (c, o):
        accumulate(1, y2, m)
    activate(1)
    output_sibling(0)
    joined_f(0, 0, z2)
    joined_g(0, 0, z2)
    partial(0, yp, zp)
    plain_g(0, 1, zp)
    partial(0, ym, zm)
    plain_f(0, 2, zm)
    output_own(0)
    give_back(0, 1)
    local = [fetch(BS.at[0, :, j], BK.at[0, :, j], "stay", 0)]
    for yy in (y2, yp, ym):
        partial(1, yy, z2)
    first_f(1, 0, z2)
    first_g(1, 0, z2)
    plain_g(1, 0, z2)
    plain_f(1, 0, z2)
    partial(0, yp, zm)
    partial(0, ym, zp)
    joined_f(0, 2, zm)
    joined_g(0, 1, zp)
    first_f(0, 1, zp)
    first_g(0, 2, zm)
    plain_g(0, 2, zm)
    plain_f(0, 1, zp)
    output_sibling(1)
    partial(0, y, z2)
    far_z(0)
    output_own(1)
    local.append(fetch(BS.at[1, :, j], BK.at[1, :, j], "stay", 1))
    joined_f(1, 0, z2)
    joined_g(1, 0, z2)
    for zz in (zm, zp, z):
        partial(0, y, zz)
    for yy in (y2, yp, ym):
        partial(0, yy, z)
    give_back(0, 0)
    for yy in (y2, yp, ym):
        for zz in (zm, zp, z):
            partial(1, yy, zz)
    partials(1, y)
    plain_z(0)
    give_back(1, 1)
    joined_f(0, 1, zp)
    joined_g(0, 2, zm)
    first_f(1, 2, zm)
    first_g(1, 1, zp)
    first_f(1, 1, zp)
    first_g(1, 2, zm)
    first_f(0, 3, z)
    first_g(0, 3, z)
    plain_g(1, 1, zp)
    plain_f(1, 2, zm)
    far_z(1)
    joined_z(0)
    give_back(1, 0)
    joined_f(1, 2, zm)
    joined_g(1, 1, zp)
    plain_g(1, 2, zm)
    plain_f(1, 1, zp)
    joined_f(1, 1, zp)
    joined_g(1, 2, zm)
    first_f(1, 3, z)
    first_g(1, 3, z)
    plain_g(0, 3, z)
    plain_f(0, 3, z)
    joined_f(0, 3, z)
    joined_g(0, 3, z)
    plain_g(1, 3, z)
    plain_f(1, 3, z)
    plain_z(1)
    joined_z(1)
    joined_f(1, 3, z)
    joined_g(1, 3, z)

    for n in range(2):
        local[n].wait()
        for q in range(4):
            for crossing in range(2):
                for rows, _, fro, _ in partners(q)[crossing]:
                    which = 0 if rows is near else 1
                    arrived(BK.at[n, :, fro, rows], "back", n, crossing, q, which)
    tn = (((0,), (0,)), ((), ()))
    for yy in range(NY):
        back = BK[0, yy].reshape(ROWS, YB)
        out = sum(
            lax.dot_general(SEL[n], back, tn, preferred_element_type=F32) for n in (3, 2, 1)
        )
        back = BK[1, yy].reshape(ROWS, YB)
        d_in = lax.dot_general(SEL[0], back, tn, preferred_element_type=F32)
        for zz in range(NZ):
            cols = slice((zz * 4 + yy) * SH, (zz * 4 + yy + 1) * SH)
            lo_ref[:, cols] = out[:, zz * SH:(zz + 1) * SH].astype(BF16)
            dt_ref[:, cols] = d_in[:, zz * SH:(zz + 1) * SH].astype(BF16)

    finish(0)
    finish(1)
    close(0)
    close(1)

    for copy in sent:
        copy.wait_send()
    assert len(numbers) <= N_SEM


def hand_out(*refs):
    count = len(refs) // 2
    done = refs[-1]
    copies = [
        pltpu.make_async_copy(refs[n], refs[count + n], done.at[n]) for n in range(count)
    ]
    for copy in copies:
        copy.start()
    for copy in copies:
        copy.wait()


def shards(tokens, routes, gate_scale, w_gate, w_up, w_down, d_out):
    vm = pl.BlockSpec(memory_space=pltpu.VMEM)
    hbm = pl.BlockSpec(memory_space=pltpu.HBM)
    grad = jax.ShapeDtypeStruct(w_gate.shape, F32)
    rows = jax.ShapeDtypeStruct(tokens.shape, BF16)
    results = (rows, rows, grad, grad, grad)

    def chunks(kind, *lead):
        return [pltpu.VMEM((*lead, 3 * w), kind) for w in CW]

    found = pl.pallas_call(
        kernel,
        out_shape=results,
        in_specs=[hbm] * 7,
        out_specs=(vm,) * 5,
        scratch_shapes=[
            *chunks(BF16, NY, NZ, SH),
            *chunks(BF16, 64),
            pltpu.VMEM((NY, 2 * NE, CAP, YB), BF16),
            pltpu.VMEM((NY, 2 * NE, CAP, YB), BF16),
            pltpu.VMEM((NY, YB, 2 * ROWS), BF16),
            pltpu.VMEM((NY, YB, 2 * ROWS), BF16),
            pltpu.VMEM((NY, NE, CAP, YB), BF16),
            pltpu.VMEM((NY, NE, CAP, YB), BF16),
            pltpu.VMEM((4, ROWS, TOK), BF16),
            *chunks(F32, 2 * ROWS),
            *chunks(BF16, 2 * ROWS),
            *chunks(BF16, NY, NZ, SH),
            *chunks(BF16, 2, NZ, 64),
            *chunks(BF16, 2, NZ, SH),
            *chunks(BF16, 2, 64),
            *chunks(BF16, 2, SH),
            *chunks(BF16, 3, SH),
            *chunks(F32, 64),
            *chunks(F32, 64),
            pltpu.VMEM((2, NY, NE, CAP, YB), BF16),
            pltpu.VMEM((2, NY, NE, CAP, YB), BF16),
            pltpu.VMEM((2, NY, NE, CAP, YB), BF16),
            pltpu.VMEM((2, NY, NE, CAP, YB), BF16),
            pltpu.VMEM(tokens.shape, BF16),
            pltpu.VMEM(tokens.shape, BF16),
            pltpu.VMEM(routes.shape[::-1], jnp.int32),
            pltpu.VMEM(routes.shape[::-1], F32),
            pltpu.SemaphoreType.DMA((N_SEM,)),
            pltpu.SemaphoreType.DMA((N_SEM,)),
        ],
        compiler_params=pltpu.CompilerParams(
            collective_id=0, has_side_effects=True, vmem_limit_bytes=VMEM_MB * 1024 * 1024
        ),
    )(*(
        pltpu.with_memory_space_constraint(value, pltpu.HBM)
        for value in (tokens, routes.T, gate_scale.T, w_gate, w_up, w_down, d_out)
    ))
    return pl.pallas_call(
        hand_out,
        out_shape=results,
        in_specs=[vm] * 5,
        out_specs=(hbm,) * 5,
        scratch_shapes=[pltpu.SemaphoreType.DMA((5,))],
        compiler_params=pltpu.CompilerParams(vmem_limit_bytes=8 * 1024 * 1024),
    )(*found)


def solution(mesh):
    tok = P(("dp", "expert"), None)
    wei = P("expert", "dp", None)
    return jax.shard_map(
        shards,
        mesh=mesh,
        in_specs=(tok, tok, tok, wei, wei, wei, tok),
        out_specs=(tok, tok, wei, wei, wei),
        check_vma=False,
    )
```

```python
import jax
import jax.numpy as jnp
from jax import lax
from jax.experimental import pallas as pl
from jax.experimental.pallas import tpu as pltpu
from jax.sharding import PartitionSpec as P

CAP = 32
MESH = pl.DeviceIdType.MESH
F32 = jnp.float32
BF16 = jnp.bfloat16

NY, NZ, SH = 4, 4, 128
HH = 384
CW = (256, 128)
CO = (0, 256)
YB = NZ * SH
NE = 8
TOK = 192
ROWS = NE * CAP
N_SEM = 240
VMEM_MB = 50


def kernel(
    tok_hbm, rt_hbm, gs_hbm, wg_ref, wu_ref, wd_ref, do_hbm,
    lo_ref, dt_ref, gg_ref, gu_ref, gd_ref,
    W0, W1, WO0, WO1, X, D, XT, DT, SX, SD, SEL, A0, A1, C0, C1, T0, T1,
    RF0, RF1, RS0, RS1, ZF0, ZF1, Z20, Z21, ZS0, ZS1, FS0, FS1, FR0, FR1,
    OS, OR, BS, BK, tok_ref, do_ref, rt_ref, gs_ref, ss, rs,
):
    W, WO, ACC, CAT, T = (W0, W1), (WO0, WO1), (A0, A1), (C0, C1), (T0, T1)
    R1, R2, Z1, Z2, ZS = (RF0, RF1), (RS0, RS1), (ZF0, ZF1), (Z20, Z21), (ZS0, ZS1)
    FS, FR = (FS0, FS1), (FR0, FR1)
    i = lax.axis_index("dp")
    j = lax.axis_index("expert")
    c = lax.rem(i, 2)
    o = 1 - c
    p = lax.div(i, 2)
    y = lax.rem(p, 4)
    z = lax.div(p, 4)
    x = lax.div(j, 2)
    side = lax.rem(j, 2)
    yp, ym, y2 = lax.rem(y + 1, 4), lax.rem(y + 3, 4), lax.rem(y + 2, 4)
    zp, zm, z2 = lax.rem(z + 1, 4), lax.rem(z + 3, 4), lax.rem(z + 2, 4)
    zn = lax.rem(z + 3 + 2 * side, 4)

    def place(yy, zz, cc):
        return {"dp": (zz * 4 + yy) * 2 + cc}

    sib = place(y, z, o)
    up_y, down_y = place(yp, z, c), place(ym, z, c)
    up_z, down_z = place(y, zp, c), place(y, zm, c)

    near, far = pl.ds(0, 16), pl.ds(16, 16)

    def partners(q):
        to, fro = lax.rem(x + q, 4), lax.rem(x + 4 - q, 4)
        across = [
            (near, to * 2 + 1 - side, fro * 2 + 1 - side, {"expert": to * 2 + 1 - side}),
            (far, to * 2 + 1 - side, fro * 2 + 1 - side,
             {"dp": (zn * 4 + y) * 2 + c, "expert": to * 2 + 1 - side}),
        ]
        same = [(pl.ds(0, CAP), to * 2 + side, fro * 2 + side, {"expert": to * 2 + side})]
        return same if q else [], across

    numbers = {}

    def number(*name):
        return numbers.setdefault(name, len(numbers))

    sent = []

    def send(src, dst, name, to):
        k = number(*name)
        copy = pltpu.make_async_remote_copy(
            src_ref=src, dst_ref=dst, send_sem=ss.at[k], recv_sem=rs.at[k],
            device_id=to, device_id_type=MESH,
        )
        copy.start()
        sent.append(copy)

    def arrived(ref, *name):
        k = number(*name)
        pltpu.make_async_remote_copy(
            src_ref=ref, dst_ref=ref, send_sem=ss.at[k], recv_sem=rs.at[k],
            device_id=sib, device_id_type=MESH,
        ).wait_recv()

    def fetch(src, dst, *name):
        copy = pltpu.make_async_copy(src, dst, rs.at[number(*name)])
        copy.start()
        return copy

    f = pl.ds(pl.multiple_of(c * 64, 64), 64)
    g = pl.ds(pl.multiple_of(o * 64, 64), 64)

    def units(core, k):
        return pl.ds(pl.multiple_of(core * HH + CO[k], 128), CW[k])

    own, other = [[], []], [[], []]
    for k in range(2):
        for n, w_ref in enumerate((wg_ref, wu_ref, wd_ref)):
            cols = pl.ds(n * CW[k], CW[k])
            other[k].append(
                fetch(w_ref.at[0, :, units(o, k)], WO[k].at[:, cols], "other", k, n)
            )
            own[k].append(
                fetch(w_ref.at[0, :, units(c, k)], W[k].at[y, z, f, cols], "own", k, n)
            )
    loads = [
        fetch(rt_hbm, rt_ref, "load", "r"),
        fetch(gs_hbm, gs_ref, "load", "s"),
        fetch(tok_hbm, tok_ref, "load", "x"),
        fetch(do_hbm, do_ref, "load", "d"),
    ]
    barrier = pltpu.get_barrier_semaphore()
    greet = [sib, up_y, down_y, up_z, down_z]
    for q in range(4):
        same, across = partners(q)
        greet += [to for _, _, _, to in same + across]
    for to in greet:
        pl.semaphore_signal(barrier, inc=1, device_id=to, device_id_type=MESH)
    for k in range(2):
        for copy in other[k] + own[k]:
            copy.wait()
    pl.semaphore_wait(barrier, len(greet))

    def along(k, yy, zz, piece, name, to):
        send(W[k].at[yy, zz, piece], W[k].at[yy, zz, piece], (k,) + name, to)

    def here(k, yy, zz, piece, *name):
        arrived(W[k].at[yy, zz, piece], k, *name)

    def leave(k, kind, piece, way):
        to_z, to_y = (up_z, up_y) if way == "up" else (down_z, down_y)
        along(k, y, z, piece, ("gz", kind, way), to_z)
        along(k, y, z, piece, ("gy", 0, kind, way), to_y)

    for k in range(2):
        send(WO[k], W[k].at[y, z, f], ("sib", k), sib)
    leave(0, "f", f, "up")
    arrived(W[0].at[y, z, g], "sib", 0)
    leave(0, "g", g, "down")
    leave(0, "g", g, "up")
    leave(0, "f", f, "down")
    leave(1, "f", f, "up")
    arrived(W[1].at[y, z, g], "sib", 1)
    leave(1, "g", g, "down")
    leave(1, "g", g, "up")
    leave(1, "f", f, "down")

    shape = (ROWS, TOK)
    row = lax.broadcasted_iota(jnp.int32, shape, 0)
    row_e = lax.div(row, CAP)
    row_s = lax.rem(row, CAP).astype(F32)
    for copy in loads[:2]:
        copy.wait()
    scale = gs_ref[...]
    combine = scale / jnp.sum(scale, axis=0, keepdims=True)
    routes = rt_ref[...]
    named = jnp.zeros(shape, F32)
    weight = jnp.zeros(shape, F32)
    for s in range(6):
        same = routes[s:s + 1, :] == row_e
        named = jnp.where(same, 1.0, named)
        weight = jnp.where(same, combine[s:s + 1, :], weight)
    earlier = (
        lax.broadcasted_iota(jnp.int32, (TOK, TOK), 0)
        < lax.broadcasted_iota(jnp.int32, (TOK, TOK), 1)
    ).astype(F32).astype(BF16)
    position = jnp.dot(named.astype(BF16), earlier, preferred_element_type=F32)
    chosen = jnp.where(position == row_s, named, 0.0)
    weight = weight * chosen
    slot_weight = jnp.sum(weight, axis=1, keepdims=True)
    select = chosen.astype(BF16)
    SEL[0] = select
    rest = weight
    for n in range(1, 4):
        part = rest.astype(BF16)
        SEL[n] = part
        rest = rest - part.astype(F32)

    def columns(ref, yy):
        return jnp.concatenate(
            [ref[:, (zz * 4 + yy) * SH:(zz * 4 + yy + 1) * SH] for zz in range(NZ)], axis=1
        )

    for copy in loads[2:]:
        copy.wait()
    for yy in range(NY):
        rows = jnp.dot(select, columns(tok_ref, yy), preferred_element_type=F32)
        SX[yy] = rows.astype(BF16).reshape(NE, CAP, YB)
        rows = jnp.dot(select, columns(do_ref, yy), preferred_element_type=F32)
        SD[yy] = (rows * slot_weight).astype(BF16).reshape(NE, CAP, YB)

    mine = c * NE + j
    rows_out = ((SX, X, "x"), (SD, D, "d"))

    def exchange(crossing):
        for src, dst, what in rows_out:
            for q in range(4):
                for rows, to, _, device in partners(q)[crossing]:
                    which = 0 if rows is near else 1
                    send(src.at[:, to, rows], dst.at[:, mine, rows],
                         ("to", what, crossing, q, which), device)

    exchange(0)
    local = [fetch(src.at[:, j], dst.at[:, mine], "keep", what) for src, dst, what in rows_out]

    def spread_y(k, step, zz, piece, kind):
        along(k, y, zz, piece, ("gy", step, kind, "up"), up_y)
        along(k, y, zz, piece, ("gy", step, kind, "down"), down_y)

    def onward_f(k, step, zz):
        here(k, ym, zz, f, "gy", step, "f", "up")
        along(k, ym, zz, f, ("gy", step, "f", "on"), up_y)

    def onward_g(k, step, zz):
        here(k, yp, zz, g, "gy", step, "g", "down")
        along(k, yp, zz, g, ("gy", step, "g", "on"), down_y)

    def onward_z(k):
        here(k, y, zm, f, "gz", "f", "up")
        along(k, y, zm, f, ("gz", "f", "on"), up_z)
        here(k, y, zp, g, "gz", "g", "down")
        along(k, y, zp, g, ("gz", "g", "on"), down_z)

    onward_f(0, 0, z)
    onward_g(0, 0, z)
    onward_z(0)
    spread_y(0, 1, zm, f, "f")
    spread_y(0, 2, zp, g, "g")
    exchange(1)
    onward_f(1, 0, z)
    onward_g(1, 0, z)
    here(0, y, zm, g, "gz", "g", "up")
    spread_y(0, 1, zm, g, "g")
    here(0, y, zp, f, "gz", "f", "down")
    spread_y(0, 2, zp, f, "f")
    onward_z(1)
    onward_f(0, 1, zm)
    onward_g(0, 2, zp)
    here(0, y, z2, f, "gz", "f", "on")
    spread_y(0, 3, z2, f, "f")
    here(0, y, z2, g, "gz", "g", "on")
    spread_y(0, 3, z2, g, "g")
    here(1, y, zm, g, "gz", "g", "up")
    here(1, y, zp, f, "gz", "f", "down")
    for step, zz in ((1, zm), (2, zp)):
        spread_y(1, step, zz, f, "f")
        spread_y(1, step, zz, g, "g")
    onward_g(0, 1, zm)
    onward_f(0, 2, zp)
    onward_f(0, 3, z2)
    onward_g(0, 3, z2)
    for step, zz in ((1, zm), (2, zp)):
        onward_f(1, step, zz)
        onward_g(1, step, zz)
    for n, (_, dst, what) in enumerate(rows_out):
        local[n].wait()
        for q in range(4):
            for crossing in range(2):
                for rows, _, fro, _ in partners(q)[crossing]:
                    which = 0 if rows is near else 1
                    arrived(dst.at[:, c * NE + fro, rows], "to", what, crossing, q, which)
        block = dst.at[:, pl.ds(c * NE, NE)]
        send(block, block, ("rows", what), sib)

    def turn(m, first, last):
        def body(step, carry):
            yy = lax.rem(y2 + step, NY)
            cols = pl.ds(pl.multiple_of(m * ROWS, ROWS), ROWS)
            blocks = pl.ds(m * NE, NE)
            XT[yy, :, cols] = X[yy, blocks].reshape(ROWS, YB).T
            DT[yy, :, cols] = D[yy, blocks].reshape(ROWS, YB).T
            return carry

        lax.fori_loop(first, last, body, 0)

    tiles = (
        ((0, 0, 256), (0, 256, 512), (1, 512, 768)),
        ((0, 0, 256), (1, 256, 384)),
    )

    def accumulate(k, yy, m, first=False):
        rows = pl.ds(pl.multiple_of(m * ROWS, ROWS), ROWS)
        blocks = pl.ds(m * NE, NE)
        for which, lo, hi in tiles[k]:
            got = jnp.dot(
                (X, D)[which][yy, blocks].reshape(ROWS, YB),
                W[k][yy, :, :, lo:hi].reshape(YB, hi - lo),
                preferred_element_type=F32,
            )
            if first:
                ACC[k][rows, lo:hi] = got
            else:
                ACC[k][rows, lo:hi] += got

    steps = ((0, z), (1, zm), (2, zp), (3, z2))

    def wait_m(k):
        for step, zz in steps:
            here(k, ym, zz, g, "gy", step, "g", "up")

    def wait_p(k):
        for step, zz in steps:
            here(k, yp, zz, f, "gy", step, "f", "down")

    def wait_2(k):
        for step, zz in steps:
            here(k, y2, zz, f, "gy", step, "f", "on")
            here(k, y2, zz, g, "gy", step, "g", "on")

    turn(c, 0, NY)
    here(1, y, z2, f, "gz", "f", "on")
    spread_y(1, 3, z2, f, "f")
    here(1, y, z2, g, "gz", "g", "on")
    spread_y(1, 3, z2, g, "g")
    accumulate(0, y, c, True)
    wait_m(0)
    accumulate(0, ym, c)
    wait_p(0)
    accumulate(0, yp, c)
    wait_2(0)
    accumulate(0, y2, c)
    arrived(X.at[:, pl.ds(o * NE, NE)], "rows", "x")
    arrived(D.at[:, pl.ds(o * NE, NE)], "rows", "d")
    turn(o, 0, 1)
    accumulate(0, y, o, True)
    accumulate(0, ym, o)
    accumulate(0, yp, o)
    accumulate(0, y2, o)

    def activate(k):
        w = CW[k]

        def body(m, carry):
            rows = pl.ds(pl.multiple_of(m * 64, 64), 64)
            gate, up, d_hidden = (ACC[k][rows, n * w:(n + 1) * w] for n in range(3))
            sig = jax.nn.sigmoid(gate)
            act = gate * sig
            CAT[k][rows, 0:w] = (
                d_hidden * up * sig * (1.0 + gate * (1.0 - sig))
            ).astype(BF16)
            CAT[k][rows, w:2 * w] = (d_hidden * act).astype(BF16)
            CAT[k][rows, 2 * w:3 * w] = (act * up).astype(BF16)
            return carry

        lax.fori_loop(0, 2 * ROWS // 64, body, 0)

    def partials(k, yy):
        for which, lo, hi in tiles[k]:
            got = jnp.dot(
                (XT, DT)[which][yy], CAT[k][:, lo:hi], preferred_element_type=F32
            )
            T[k][yy, :, :, lo:hi] = got.astype(BF16).reshape(NZ, SH, hi - lo)

    def partial(k, yy, zz):
        rows = pl.ds(pl.multiple_of(zz * SH, SH), SH)
        for which, lo, hi in tiles[k]:
            got = jnp.dot(
                (XT, DT)[which][yy, rows], CAT[k][:, lo:hi], preferred_element_type=F32
            )
            T[k][yy, zz, :, lo:hi] = got.astype(BF16)

    nt = (((1,), (1,)), ((), ()))

    def output(side_, n, yy):
        rows = pl.ds(pl.multiple_of(side_ * ROWS, ROWS), ROWS)
        total = None
        for k in range(2):
            lo, hi = ((2 * CW[k], 3 * CW[k]), (0, 2 * CW[k]))[n]
            got = lax.dot_general(
                CAT[k][rows, lo:hi], W[k][yy, :, :, lo:hi].reshape(YB, hi - lo), nt,
                preferred_element_type=F32,
            )
            total = got if total is None else total + got
        return total

    def output_sibling(n):
        for yy in range(NY):
            OS[n, yy] = output(o, n, yy).astype(BF16).reshape(NE, CAP, YB)
            send(OS.at[n, yy], OR.at[n, yy], ("part", n, yy), sib)

    def output_own(n):
        for yy in range(NY):
            value = output(c, n, yy)
            arrived(OR.at[n, yy], "part", n, yy)
            value = value + OR[n, yy].reshape(ROWS, YB).astype(F32)
            BS[n, yy] = value.astype(BF16).reshape(NE, CAP, YB)

    def give_back(n, crossing):
        for q in range(4):
            for rows, to, _, device in partners(q)[crossing]:
                which = 0 if rows is near else 1
                send(BS.at[n, :, to, rows], BK.at[n, :, j, rows],
                     ("back", n, crossing, q, which), device)

    def first_f(k, step, zz):
        send(T[k].at[y2, zz, f], R1[k].at[0, step], ("r1", k, step, "f"), up_y)

    def first_g(k, step, zz):
        send(T[k].at[y2, zz, g], R1[k].at[1, step], ("r1", k, step, "g"), down_y)

    def plain_g(k, step, zz):
        send(T[k].at[yp, zz, g], R2[k].at[0, step, g], ("r2", k, step, "g", "up"), up_y)

    def plain_f(k, step, zz):
        send(T[k].at[ym, zz, f], R2[k].at[1, step, f], ("r2", k, step, "f", "down"), down_y)

    def joined_f(k, step, zz):
        arrived(R1[k].at[0, step], "r1", k, step, "f")
        T[k][yp, zz, f] = (
            T[k][yp, zz, f].astype(F32) + R1[k][0, step].astype(F32)
        ).astype(BF16)
        send(T[k].at[yp, zz, f], R2[k].at[0, step, f], ("r2", k, step, "f", "up"), up_y)

    def joined_g(k, step, zz):
        arrived(R1[k].at[1, step], "r1", k, step, "g")
        T[k][ym, zz, g] = (
            T[k][ym, zz, g].astype(F32) + R1[k][1, step].astype(F32)
        ).astype(BF16)
        send(T[k].at[ym, zz, g], R2[k].at[1, step, g], ("r2", k, step, "g", "down"), down_y)

    def summed_y(k, step, zz, piece, kind):
        for d in range(2):
            arrived(R2[k].at[d, step, piece], "r2", k, step, kind, ("up", "down")[d])
        return (
            T[k][y, zz, piece].astype(F32)
            + R2[k][0, step, piece].astype(F32)
            + R2[k][1, step, piece].astype(F32)
        )

    def far_z(k):
        ZS[k][0, f] = summed_y(k, 0, z2, f, "f").astype(BF16)
        send(ZS[k].at[0, f], Z1[k].at[0], ("z1", k, "f"), up_z)
        ZS[k][0, g] = summed_y(k, 0, z2, g, "g").astype(BF16)
        send(ZS[k].at[0, g], Z1[k].at[1], ("z1", k, "g"), down_z)

    def plain_z(k):
        ZS[k][2, f] = summed_y(k, 2, zm, f, "f").astype(BF16)
        send(ZS[k].at[2, f], Z2[k].at[1, f], ("z2", k, "f", "down"), down_z)
        ZS[k][1, g] = summed_y(k, 1, zp, g, "g").astype(BF16)
        send(ZS[k].at[1, g], Z2[k].at[0, g], ("z2", k, "g", "up"), up_z)

    def joined_z(k):
        total = summed_y(k, 1, zp, f, "f")
        arrived(Z1[k].at[0], "z1", k, "f")
        ZS[k][1, f] = (total + Z1[k][0].astype(F32)).astype(BF16)
        send(ZS[k].at[1, f], Z2[k].at[0, f], ("z2", k, "f", "up"), up_z)
        total = summed_y(k, 2, zm, g, "g")
        arrived(Z1[k].at[1], "z1", k, "g")
        ZS[k][2, g] = (total + Z1[k][1].astype(F32)).astype(BF16)
        send(ZS[k].at[2, g], Z2[k].at[1, g], ("z2", k, "g", "down"), down_z)

    def total_z(k, piece, kind):
        total = summed_y(k, 3, z, piece, kind)
        arrived(Z2[k].at[0, piece], "z2", k, kind, "up")
        arrived(Z2[k].at[1, piece], "z2", k, kind, "down")
        return total + Z2[k][0, piece].astype(F32) + Z2[k][1, piece].astype(F32)

    grads = (gg_ref, gu_ref, gd_ref)

    def finish(k):
        w = CW[k]
        FS[k][...] = total_z(k, g, "g")
        send(FS[k], FR[k], ("fin", k), sib)
        total = total_z(k, f, "f")
        for n, ref in enumerate(grads):
            ref[0, :, units(c, k)] = total[:, n * w:(n + 1) * w]

    def close(k):
        w = CW[k]
        arrived(FR[k], "fin", k)
        for n, ref in enumerate(grads):
            ref[0, :, units(o, k)] = FR[k][:, n * w:(n + 1) * w]

    activate(0)
    onward_f(1, 3, z2)
    onward_g(1, 3, z2)
    partial(0, y2, z2)
    first_f(0, 0, z2)
    first_g(0, 0, z2)
    turn(o, 1, NY)
    partial(0, yp, z2)
    plain_g(0, 0, z2)
    partial(0, ym, z2)
    plain_f(0, 0, z2)
    partial(0, y2, zm)
    first_f(0, 2, zm)
    partial(0, y2, zp)
    first_g(0, 1, zp)
    for m, first in ((c, True), (o, True)):
        accumulate(1, y, m, first)
    wait_m(1)
    wait_p(1)
    for m in (c, o):
        accumulate(1, ym, m)
        accumulate(1, yp, m)
    wait_2(1)
    for m in (c, o):
        accumulate(1, y2, m)
    activate(1)
    output_sibling(0)
    joined_f(0, 0, z2)
    joined_g(0, 0, z2)
    partial(0, yp, zp)
    plain_g(0, 1, zp)
    partial(0, ym, zm)
    plain_f(0, 2, zm)
    output_own(0)
    give_back(0, 1)
    local = [fetch(BS.at[0, :, j], BK.at[0, :, j], "stay", 0)]
    for yy in (y2, yp, ym):
        partial(1, yy, z2)
    first_f(1, 0, z2)
    first_g(1, 0, z2)
    plain_g(1, 0, z2)
    plain_f(1, 0, z2)
    partial(0, yp, zm)
    partial(0, ym, zp)
    joined_f(0, 2, zm)
    joined_g(0, 1, zp)
    first_f(0, 1, zp)
    first_g(0, 2, zm)
    plain_g(0, 2, zm)
    plain_f(0, 1, zp)
    output_sibling(1)
    partial(0, y, z2)
    far_z(0)
    output_own(1)
    local.append(fetch(BS.at[1, :, j], BK.at[1, :, j], "stay", 1))
    joined_f(1, 0, z2)
    joined_g(1, 0, z2)
    for zz in (zm, zp, z):
        partial(0, y, zz)
    for yy in (y2, yp, ym):
        partial(0, yy, z)
    give_back(0, 0)
    for yy in (y2, yp, ym):
        for zz in (zm, zp, z):
            partial(1, yy, zz)
    partials(1, y)
    plain_z(0)
    give_back(1, 1)
    joined_f(0, 1, zp)
    joined_g(0, 2, zm)
    first_f(1, 2, zm)
    first_g(1, 1, zp)
    first_f(1, 1, zp)
    first_g(1, 2, zm)
    first_f(0, 3, z)
    first_g(0, 3, z)
    plain_g(1, 1, zp)
    plain_f(1, 2, zm)
    far_z(1)
    joined_z(0)
    give_back(1, 0)
    joined_f(1, 2, zm)
    joined_g(1, 1, zp)
    plain_g(1, 2, zm)
    plain_f(1, 1, zp)
    joined_f(1, 1, zp)
    joined_g(1, 2, zm)
    plain_g(0, 3, z)
    plain_f(0, 3, z)
    first_f(1, 3, z)
    first_g(1, 3, z)
    joined_f(0, 3, z)
    joined_g(0, 3, z)
    plain_g(1, 3, z)
    plain_f(1, 3, z)
    plain_z(1)
    joined_z(1)
    joined_f(1, 3, z)
    joined_g(1, 3, z)

    for n in range(2):
        local[n].wait()
        for q in range(4):
            for crossing in range(2):
                for rows, _, fro, _ in partners(q)[crossing]:
                    which = 0 if rows is near else 1
                    arrived(BK.at[n, :, fro, rows], "back", n, crossing, q, which)
    tn = (((0,), (0,)), ((), ()))
    for yy in range(NY):
        back = BK[0, yy].reshape(ROWS, YB)
        out = sum(
            lax.dot_general(SEL[n], back, tn, preferred_element_type=F32) for n in (3, 2, 1)
        )
        back = BK[1, yy].reshape(ROWS, YB)
        d_in = lax.dot_general(SEL[0], back, tn, preferred_element_type=F32)
        for zz in range(NZ):
            cols = slice((zz * 4 + yy) * SH, (zz * 4 + yy + 1) * SH)
            lo_ref[:, cols] = out[:, zz * SH:(zz + 1) * SH].astype(BF16)
            dt_ref[:, cols] = d_in[:, zz * SH:(zz + 1) * SH].astype(BF16)

    finish(0)
    finish(1)
    close(0)
    close(1)

    for copy in sent:
        copy.wait_send()
    assert len(numbers) <= N_SEM


def hand_out(*refs):
    count = len(refs) // 2
    done = refs[-1]
    copies = [
        pltpu.make_async_copy(refs[n], refs[count + n], done.at[n]) for n in range(count)
    ]
    for copy in copies:
        copy.start()
    for copy in copies:
        copy.wait()


def shards(tokens, routes, gate_scale, w_gate, w_up, w_down, d_out):
    vm = pl.BlockSpec(memory_space=pltpu.VMEM)
    hbm = pl.BlockSpec(memory_space=pltpu.HBM)
    grad = jax.ShapeDtypeStruct(w_gate.shape, F32)
    rows = jax.ShapeDtypeStruct(tokens.shape, BF16)
    results = (rows, rows, grad, grad, grad)

    def chunks(kind, *lead):
        return [pltpu.VMEM((*lead, 3 * w), kind) for w in CW]

    found = pl.pallas_call(
        kernel,
        out_shape=results,
        in_specs=[hbm] * 7,
        out_specs=(vm,) * 5,
        scratch_shapes=[
            *chunks(BF16, NY, NZ, SH),
            *chunks(BF16, 64),
            pltpu.VMEM((NY, 2 * NE, CAP, YB), BF16),
            pltpu.VMEM((NY, 2 * NE, CAP, YB), BF16),
            pltpu.VMEM((NY, YB, 2 * ROWS), BF16),
            pltpu.VMEM((NY, YB, 2 * ROWS), BF16),
            pltpu.VMEM((NY, NE, CAP, YB), BF16),
            pltpu.VMEM((NY, NE, CAP, YB), BF16),
            pltpu.VMEM((4, ROWS, TOK), BF16),
            *chunks(F32, 2 * ROWS),
            *chunks(BF16, 2 * ROWS),
            *chunks(BF16, NY, NZ, SH),
            *chunks(BF16, 2, NZ, 64),
            *chunks(BF16, 2, NZ, SH),
            *chunks(BF16, 2, 64),
            *chunks(BF16, 2, SH),
            *chunks(BF16, 3, SH),
            *chunks(F32, 64),
            *chunks(F32, 64),
            pltpu.VMEM((2, NY, NE, CAP, YB), BF16),
            pltpu.VMEM((2, NY, NE, CAP, YB), BF16),
            pltpu.VMEM((2, NY, NE, CAP, YB), BF16),
            pltpu.VMEM((2, NY, NE, CAP, YB), BF16),
            pltpu.VMEM(tokens.shape, BF16),
            pltpu.VMEM(tokens.shape, BF16),
            pltpu.VMEM(routes.shape[::-1], jnp.int32),
            pltpu.VMEM(routes.shape[::-1], F32),
            pltpu.SemaphoreType.DMA((N_SEM,)),
            pltpu.SemaphoreType.DMA((N_SEM,)),
        ],
        compiler_params=pltpu.CompilerParams(
            collective_id=0, has_side_effects=True, vmem_limit_bytes=VMEM_MB * 1024 * 1024
        ),
    )(*(
        pltpu.with_memory_space_constraint(value, pltpu.HBM)
        for value in (tokens, routes.T, gate_scale.T, w_gate, w_up, w_down, d_out)
    ))
    return pl.pallas_call(
        hand_out,
        out_shape=results,
        in_specs=[vm] * 5,
        out_specs=(hbm,) * 5,
        scratch_shapes=[pltpu.SemaphoreType.DMA((5,))],
        compiler_params=pltpu.CompilerParams(vmem_limit_bytes=8 * 1024 * 1024),
    )(*found)


def solution(mesh):
    tok = P(("dp", "expert"), None)
    wei = P("expert", "dp", None)
    return jax.shard_map(
        shards,
        mesh=mesh,
        in_specs=(tok, tok, tok, wei, wei, wei, tok),
        out_specs=(tok, tok, wei, wei, wei),
        check_vma=False,
    )
```

```python
import jax
import jax.numpy as jnp
from jax import lax
from jax.experimental import pallas as pl
from jax.experimental.pallas import tpu as pltpu
from jax.sharding import PartitionSpec as P

CAP = 32
MESH = pl.DeviceIdType.MESH
F32 = jnp.float32
BF16 = jnp.bfloat16

NY, NZ, SH = 4, 4, 128
HH = 384
CW = (256, 128)
CO = (0, 256)
YB = NZ * SH
NE = 8
TOK = 192
ROWS = NE * CAP
N_SEM = 240
VMEM_MB = 50


def kernel(
    tok_hbm, rt_hbm, gs_hbm, wg_ref, wu_ref, wd_ref, do_hbm,
    lo_ref, dt_ref, gg_ref, gu_ref, gd_ref,
    W0, W1, WO0, WO1, X, D, XT, DT, SX, SD, SEL, A0, A1, C0, C1, T0, T1,
    RF0, RF1, RS0, RS1, ZF0, ZF1, Z20, Z21, ZS0, ZS1, FS0, FS1, FR0, FR1,
    OS, OR, BS, BK, tok_ref, do_ref, rt_ref, gs_ref, ss, rs,
):
    W, WO, ACC, CAT, T = (W0, W1), (WO0, WO1), (A0, A1), (C0, C1), (T0, T1)
    R1, R2, Z1, Z2, ZS = (RF0, RF1), (RS0, RS1), (ZF0, ZF1), (Z20, Z21), (ZS0, ZS1)
    FS, FR = (FS0, FS1), (FR0, FR1)
    i = lax.axis_index("dp")
    j = lax.axis_index("expert")
    c = lax.rem(i, 2)
    o = 1 - c
    p = lax.div(i, 2)
    y = lax.rem(p, 4)
    z = lax.div(p, 4)
    x = lax.div(j, 2)
    side = lax.rem(j, 2)
    yp, ym, y2 = lax.rem(y + 1, 4), lax.rem(y + 3, 4), lax.rem(y + 2, 4)
    zp, zm, z2 = lax.rem(z + 1, 4), lax.rem(z + 3, 4), lax.rem(z + 2, 4)
    zn = lax.rem(z + 3 + 2 * side, 4)

    def place(yy, zz, cc):
        return {"dp": (zz * 4 + yy) * 2 + cc}

    sib = place(y, z, o)
    up_y, down_y = place(yp, z, c), place(ym, z, c)
    up_z, down_z = place(y, zp, c), place(y, zm, c)

    near, far = pl.ds(0, 16), pl.ds(16, 16)

    def partners(q):
        to, fro = lax.rem(x + q, 4), lax.rem(x + 4 - q, 4)
        across = [
            (near, to * 2 + 1 - side, fro * 2 + 1 - side, {"expert": to * 2 + 1 - side}),
            (far, to * 2 + 1 - side, fro * 2 + 1 - side,
             {"dp": (zn * 4 + y) * 2 + c, "expert": to * 2 + 1 - side}),
        ]
        same = [(pl.ds(0, CAP), to * 2 + side, fro * 2 + side, {"expert": to * 2 + side})]
        return same if q else [], across

    numbers = {}

    def number(*name):
        return numbers.setdefault(name, len(numbers))

    sent = []

    def send(src, dst, name, to):
        k = number(*name)
        copy = pltpu.make_async_remote_copy(
            src_ref=src, dst_ref=dst, send_sem=ss.at[k], recv_sem=rs.at[k],
            device_id=to, device_id_type=MESH,
        )
        copy.start()
        sent.append(copy)

    def arrived(ref, *name):
        k = number(*name)
        pltpu.make_async_remote_copy(
            src_ref=ref, dst_ref=ref, send_sem=ss.at[k], recv_sem=rs.at[k],
            device_id=sib, device_id_type=MESH,
        ).wait_recv()

    def fetch(src, dst, *name):
        copy = pltpu.make_async_copy(src, dst, rs.at[number(*name)])
        copy.start()
        return copy

    f = pl.ds(pl.multiple_of(c * 64, 64), 64)
    g = pl.ds(pl.multiple_of(o * 64, 64), 64)

    def units(core, k):
        return pl.ds(pl.multiple_of(core * HH + CO[k], 128), CW[k])

    own, other = [[], []], [[], []]
    for k in range(2):
        for n, w_ref in enumerate((wg_ref, wu_ref, wd_ref)):
            cols = pl.ds(n * CW[k], CW[k])
            other[k].append(
                fetch(w_ref.at[0, :, units(o, k)], WO[k].at[:, cols], "other", k, n)
            )
            own[k].append(
                fetch(w_ref.at[0, :, units(c, k)], W[k].at[y, z, f, cols], "own", k, n)
            )
    loads = [
        fetch(rt_hbm, rt_ref, "load", "r"),
        fetch(gs_hbm, gs_ref, "load", "s"),
        fetch(tok_hbm, tok_ref, "load", "x"),
        fetch(do_hbm, do_ref, "load", "d"),
    ]
    barrier = pltpu.get_barrier_semaphore()
    greet = [sib, up_y, down_y, up_z, down_z]
    for q in range(4):
        same, across = partners(q)
        greet += [to for _, _, _, to in same + across]
    for to in greet:
        pl.semaphore_signal(barrier, inc=1, device_id=to, device_id_type=MESH)
    for k in range(2):
        for copy in other[k] + own[k]:
            copy.wait()
    pl.semaphore_wait(barrier, len(greet))

    def along(k, yy, zz, piece, name, to):
        send(W[k].at[yy, zz, piece], W[k].at[yy, zz, piece], (k,) + name, to)

    def here(k, yy, zz, piece, *name):
        arrived(W[k].at[yy, zz, piece], k, *name)

    def leave(k, kind, piece, way):
        to_z, to_y = (up_z, up_y) if way == "up" else (down_z, down_y)
        along(k, y, z, piece, ("gz", kind, way), to_z)
        along(k, y, z, piece, ("gy", 0, kind, way), to_y)

    for k in range(2):
        send(WO[k], W[k].at[y, z, f], ("sib", k), sib)
    leave(0, "f", f, "up")
    arrived(W[0].at[y, z, g], "sib", 0)
    leave(0, "g", g, "down")
    leave(0, "g", g, "up")
    leave(0, "f", f, "down")
    leave(1, "f", f, "up")
    arrived(W[1].at[y, z, g], "sib", 1)
    leave(1, "g", g, "down")
    leave(1, "g", g, "up")
    leave(1, "f", f, "down")

    shape = (ROWS, TOK)
    row = lax.broadcasted_iota(jnp.int32, shape, 0)
    row_e = lax.div(row, CAP)
    row_s = lax.rem(row, CAP).astype(F32)
    for copy in loads[:2]:
        copy.wait()
    scale = gs_ref[...]
    combine = scale / jnp.sum(scale, axis=0, keepdims=True)
    routes = rt_ref[...]
    named = jnp.zeros(shape, F32)
    weight = jnp.zeros(shape, F32)
    for s in range(6):
        same = routes[s:s + 1, :] == row_e
        named = jnp.where(same, 1.0, named)
        weight = jnp.where(same, combine[s:s + 1, :], weight)
    earlier = (
        lax.broadcasted_iota(jnp.int32, (TOK, TOK), 0)
        < lax.broadcasted_iota(jnp.int32, (TOK, TOK), 1)
    ).astype(F32).astype(BF16)
    position = jnp.dot(named.astype(BF16), earlier, preferred_element_type=F32)
    chosen = jnp.where(position == row_s, named, 0.0)
    weight = weight * chosen
    slot_weight = jnp.sum(weight, axis=1, keepdims=True)
    select = chosen.astype(BF16)
    SEL[0] = select
    rest = weight
    for n in range(1, 4):
        part = rest.astype(BF16)
        SEL[n] = part
        rest = rest - part.astype(F32)

    def columns(ref, yy):
        return jnp.concatenate(
            [ref[:, (zz * 4 + yy) * SH:(zz * 4 + yy + 1) * SH] for zz in range(NZ)], axis=1
        )

    for copy in loads[2:]:
        copy.wait()
    for yy in range(NY):
        rows = jnp.dot(select, columns(tok_ref, yy), preferred_element_type=F32)
        SX[yy] = rows.astype(BF16).reshape(NE, CAP, YB)
        rows = jnp.dot(select, columns(do_ref, yy), preferred_element_type=F32)
        SD[yy] = (rows * slot_weight).astype(BF16).reshape(NE, CAP, YB)

    mine = c * NE + j
    rows_out = ((SX, X, "x"), (SD, D, "d"))

    def exchange(crossing):
        for src, dst, what in rows_out:
            for q in range(4):
                for rows, to, _, device in partners(q)[crossing]:
                    which = 0 if rows is near else 1
                    send(src.at[:, to, rows], dst.at[:, mine, rows],
                         ("to", what, crossing, q, which), device)

    exchange(0)
    local = [fetch(src.at[:, j], dst.at[:, mine], "keep", what) for src, dst, what in rows_out]

    def spread_y(k, step, zz, piece, kind):
        along(k, y, zz, piece, ("gy", step, kind, "up"), up_y)
        along(k, y, zz, piece, ("gy", step, kind, "down"), down_y)

    def onward_f(k, step, zz):
        here(k, ym, zz, f, "gy", step, "f", "up")
        along(k, ym, zz, f, ("gy", step, "f", "on"), up_y)

    def onward_g(k, step, zz):
        here(k, yp, zz, g, "gy", step, "g", "down")
        along(k, yp, zz, g, ("gy", step, "g", "on"), down_y)

    def onward_z(k):
        here(k, y, zm, f, "gz", "f", "up")
        along(k, y, zm, f, ("gz", "f", "on"), up_z)
        here(k, y, zp, g, "gz", "g", "down")
        along(k, y, zp, g, ("gz", "g", "on"), down_z)

    onward_f(0, 0, z)
    onward_g(0, 0, z)
    onward_z(0)
    spread_y(0, 1, zm, f, "f")
    spread_y(0, 2, zp, g, "g")
    exchange(1)
    onward_f(1, 0, z)
    onward_g(1, 0, z)
    here(0, y, zm, g, "gz", "g", "up")
    spread_y(0, 1, zm, g, "g")
    here(0, y, zp, f, "gz", "f", "down")
    spread_y(0, 2, zp, f, "f")
    onward_z(1)
    onward_f(0, 1, zm)
    onward_g(0, 2, zp)
    here(0, y, z2, f, "gz", "f", "on")
    spread_y(0, 3, z2, f, "f")
    here(0, y, z2, g, "gz", "g", "on")
    spread_y(0, 3, z2, g, "g")
    here(1, y, zm, g, "gz", "g", "up")
    here(1, y, zp, f, "gz", "f", "down")
    for step, zz in ((1, zm), (2, zp)):
        spread_y(1, step, zz, f, "f")
        spread_y(1, step, zz, g, "g")
    onward_g(0, 1, zm)
    onward_f(0, 2, zp)
    onward_f(0, 3, z2)
    onward_g(0, 3, z2)
    for step, zz in ((1, zm), (2, zp)):
        onward_f(1, step, zz)
        onward_g(1, step, zz)
    for n, (_, dst, what) in enumerate(rows_out):
        local[n].wait()
        for q in range(4):
            for crossing in range(2):
                for rows, _, fro, _ in partners(q)[crossing]:
                    which = 0 if rows is near else 1
                    arrived(dst.at[:, c * NE + fro, rows], "to", what, crossing, q, which)
        block = dst.at[:, pl.ds(c * NE, NE)]
        send(block, block, ("rows", what), sib)

    def turn(m, first, last):
        def body(step, carry):
            yy = lax.rem(y2 + step, NY)
            cols = pl.ds(pl.multiple_of(m * ROWS, ROWS), ROWS)
            blocks = pl.ds(m * NE, NE)
            XT[yy, :, cols] = X[yy, blocks].reshape(ROWS, YB).T
            DT[yy, :, cols] = D[yy, blocks].reshape(ROWS, YB).T
            return carry

        lax.fori_loop(first, last, body, 0)

    tiles = (
        ((0, 0, 256), (0, 256, 512), (1, 512, 768)),
        ((0, 0, 256), (1, 256, 384)),
    )

    def accumulate(k, yy, m, first=False):
        rows = pl.ds(pl.multiple_of(m * ROWS, ROWS), ROWS)
        blocks = pl.ds(m * NE, NE)
        for which, lo, hi in tiles[k]:
            got = jnp.dot(
                (X, D)[which][yy, blocks].reshape(ROWS, YB),
                W[k][yy, :, :, lo:hi].reshape(YB, hi - lo),
                preferred_element_type=F32,
            )
            if first:
                ACC[k][rows, lo:hi] = got
            else:
                ACC[k][rows, lo:hi] += got

    steps = ((0, z), (1, zm), (2, zp), (3, z2))

    def wait_m(k):
        for step, zz in steps:
            here(k, ym, zz, g, "gy", step, "g", "up")

    def wait_p(k):
        for step, zz in steps:
            here(k, yp, zz, f, "gy", step, "f", "down")

    def wait_2(k):
        for step, zz in steps:
            here(k, y2, zz, f, "gy", step, "f", "on")
            here(k, y2, zz, g, "gy", step, "g", "on")

    turn(c, 0, NY)
    here(1, y, z2, f, "gz", "f", "on")
    spread_y(1, 3, z2, f, "f")
    here(1, y, z2, g, "gz", "g", "on")
    spread_y(1, 3, z2, g, "g")
    accumulate(0, y, c, True)
    wait_m(0)
    accumulate(0, ym, c)
    wait_p(0)
    accumulate(0, yp, c)
    wait_2(0)
    accumulate(0, y2, c)
    arrived(X.at[:, pl.ds(o * NE, NE)], "rows", "x")
    arrived(D.at[:, pl.ds(o * NE, NE)], "rows", "d")
    turn(o, 0, 1)
    accumulate(0, y, o, True)
    accumulate(0, ym, o)
    accumulate(0, yp, o)
    accumulate(0, y2, o)

    def activate(k):
        w = CW[k]

        def body(m, carry):
            rows = pl.ds(pl.multiple_of(m * 64, 64), 64)
            gate, up, d_hidden = (ACC[k][rows, n * w:(n + 1) * w] for n in range(3))
            sig = jax.nn.sigmoid(gate)
            act = gate * sig
            CAT[k][rows, 0:w] = (
                d_hidden * up * sig * (1.0 + gate * (1.0 - sig))
            ).astype(BF16)
            CAT[k][rows, w:2 * w] = (d_hidden * act).astype(BF16)
            CAT[k][rows, 2 * w:3 * w] = (act * up).astype(BF16)
            return carry

        lax.fori_loop(0, 2 * ROWS // 64, body, 0)

    def partials(k, yy):
        for which, lo, hi in tiles[k]:
            got = jnp.dot(
                (XT, DT)[which][yy], CAT[k][:, lo:hi], preferred_element_type=F32
            )
            T[k][yy, :, :, lo:hi] = got.astype(BF16).reshape(NZ, SH, hi - lo)

    def partial(k, yy, zz):
        rows = pl.ds(pl.multiple_of(zz * SH, SH), SH)
        for which, lo, hi in tiles[k]:
            got = jnp.dot(
                (XT, DT)[which][yy, rows], CAT[k][:, lo:hi], preferred_element_type=F32
            )
            T[k][yy, zz, :, lo:hi] = got.astype(BF16)

    nt = (((1,), (1,)), ((), ()))

    def output(side_, n, yy):
        rows = pl.ds(pl.multiple_of(side_ * ROWS, ROWS), ROWS)
        total = None
        for k in range(2):
            lo, hi = ((2 * CW[k], 3 * CW[k]), (0, 2 * CW[k]))[n]
            got = lax.dot_general(
                CAT[k][rows, lo:hi], W[k][yy, :, :, lo:hi].reshape(YB, hi - lo), nt,
                preferred_element_type=F32,
            )
            total = got if total is None else total + got
        return total

    def output_sibling(n):
        for yy in range(NY):
            OS[n, yy] = output(o, n, yy).astype(BF16).reshape(NE, CAP, YB)
            send(OS.at[n, yy], OR.at[n, yy], ("part", n, yy), sib)

    def output_own(n):
        for yy in range(NY):
            value = output(c, n, yy)
            arrived(OR.at[n, yy], "part", n, yy)
            value = value + OR[n, yy].reshape(ROWS, YB).astype(F32)
            BS[n, yy] = value.astype(BF16).reshape(NE, CAP, YB)

    def give_back(n, crossing):
        for q in range(4):
            for rows, to, _, device in partners(q)[crossing]:
                which = 0 if rows is near else 1
                send(BS.at[n, :, to, rows], BK.at[n, :, j, rows],
                     ("back", n, crossing, q, which), device)

    def first_f(k, step, zz):
        send(T[k].at[y2, zz, f], R1[k].at[0, step], ("r1", k, step, "f"), up_y)

    def first_g(k, step, zz):
        send(T[k].at[y2, zz, g], R1[k].at[1, step], ("r1", k, step, "g"), down_y)

    def plain_g(k, step, zz):
        send(T[k].at[yp, zz, g], R2[k].at[0, step, g], ("r2", k, step, "g", "up"), up_y)

    def plain_f(k, step, zz):
        send(T[k].at[ym, zz, f], R2[k].at[1, step, f], ("r2", k, step, "f", "down"), down_y)

    def joined_f(k, step, zz):
        arrived(R1[k].at[0, step], "r1", k, step, "f")
        T[k][yp, zz, f] = (
            T[k][yp, zz, f].astype(F32) + R1[k][0, step].astype(F32)
        ).astype(BF16)
        send(T[k].at[yp, zz, f], R2[k].at[0, step, f], ("r2", k, step, "f", "up"), up_y)

    def joined_g(k, step, zz):
        arrived(R1[k].at[1, step], "r1", k, step, "g")
        T[k][ym, zz, g] = (
            T[k][ym, zz, g].astype(F32) + R1[k][1, step].astype(F32)
        ).astype(BF16)
        send(T[k].at[ym, zz, g], R2[k].at[1, step, g], ("r2", k, step, "g", "down"), down_y)

    def summed_y(k, step, zz, piece, kind):
        for d in range(2):
            arrived(R2[k].at[d, step, piece], "r2", k, step, kind, ("up", "down")[d])
        return (
            T[k][y, zz, piece].astype(F32)
            + R2[k][0, step, piece].astype(F32)
            + R2[k][1, step, piece].astype(F32)
        )

    def far_z(k):
        ZS[k][0, f] = summed_y(k, 0, z2, f, "f").astype(BF16)
        send(ZS[k].at[0, f], Z1[k].at[0], ("z1", k, "f"), up_z)
        ZS[k][0, g] = summed_y(k, 0, z2, g, "g").astype(BF16)
        send(ZS[k].at[0, g], Z1[k].at[1], ("z1", k, "g"), down_z)

    def plain_z(k):
        ZS[k][2, f] = summed_y(k, 2, zm, f, "f").astype(BF16)
        send(ZS[k].at[2, f], Z2[k].at[1, f], ("z2", k, "f", "down"), down_z)
        ZS[k][1, g] = summed_y(k, 1, zp, g, "g").astype(BF16)
        send(ZS[k].at[1, g], Z2[k].at[0, g], ("z2", k, "g", "up"), up_z)

    def joined_z(k):
        total = summed_y(k, 1, zp, f, "f")
        arrived(Z1[k].at[0], "z1", k, "f")
        ZS[k][1, f] = (total + Z1[k][0].astype(F32)).astype(BF16)
        send(ZS[k].at[1, f], Z2[k].at[0, f], ("z2", k, "f", "up"), up_z)
        total = summed_y(k, 2, zm, g, "g")
        arrived(Z1[k].at[1], "z1", k, "g")
        ZS[k][2, g] = (total + Z1[k][1].astype(F32)).astype(BF16)
        send(ZS[k].at[2, g], Z2[k].at[1, g], ("z2", k, "g", "down"), down_z)

    def total_z(k, piece, kind):
        total = summed_y(k, 3, z, piece, kind)
        arrived(Z2[k].at[0, piece], "z2", k, kind, "up")
        arrived(Z2[k].at[1, piece], "z2", k, kind, "down")
        return total + Z2[k][0, piece].astype(F32) + Z2[k][1, piece].astype(F32)

    grads = (gg_ref, gu_ref, gd_ref)

    def finish(k):
        w = CW[k]
        FS[k][...] = total_z(k, g, "g")
        send(FS[k], FR[k], ("fin", k), sib)
        total = total_z(k, f, "f")
        for n, ref in enumerate(grads):
            ref[0, :, units(c, k)] = total[:, n * w:(n + 1) * w]

    def close(k):
        w = CW[k]
        arrived(FR[k], "fin", k)
        for n, ref in enumerate(grads):
            ref[0, :, units(o, k)] = FR[k][:, n * w:(n + 1) * w]

    activate(0)
    onward_f(1, 3, z2)
    onward_g(1, 3, z2)
    partial(0, y2, z2)
    first_f(0, 0, z2)
    first_g(0, 0, z2)
    turn(o, 1, NY)
    partial(0, yp, z2)
    plain_g(0, 0, z2)
    partial(0, ym, z2)
    plain_f(0, 0, z2)
    partial(0, y2, zm)
    first_f(0, 2, zm)
    partial(0, y2, zp)
    first_g(0, 1, zp)
    for m, first in ((c, True), (o, True)):
        accumulate(1, y, m, first)
    wait_m(1)
    wait_p(1)
    for m in (c, o):
        accumulate(1, ym, m)
        accumulate(1, yp, m)
    wait_2(1)
    for m in (c, o):
        accumulate(1, y2, m)
    activate(1)
    output_sibling(0)
    joined_f(0, 0, z2)
    joined_g(0, 0, z2)
    partial(0, yp, zp)
    plain_g(0, 1, zp)
    partial(0, ym, zm)
    plain_f(0, 2, zm)
    output_own(0)
    give_back(0, 1)
    local = [fetch(BS.at[0, :, j], BK.at[0, :, j], "stay", 0)]
    for yy in (y2, yp, ym):
        partial(1, yy, z2)
    first_f(1, 0, z2)
    first_g(1, 0, z2)
    plain_g(1, 0, z2)
    plain_f(1, 0, z2)
    partial(0, yp, zm)
    partial(0, ym, zp)
    joined_f(0, 2, zm)
    joined_g(0, 1, zp)
    first_f(0, 1, zp)
    first_g(0, 2, zm)
    plain_g(0, 2, zm)
    plain_f(0, 1, zp)
    output_sibling(1)
    partial(0, y, z2)
    far_z(0)
    output_own(1)
    local.append(fetch(BS.at[1, :, j], BK.at[1, :, j], "stay", 1))
    joined_f(1, 0, z2)
    joined_g(1, 0, z2)
    for zz in (zm, zp, z):
        partial(0, y, zz)
    for yy in (y2, yp, ym):
        partial(0, yy, z)
    give_back(0, 0)
    for yy in (y2, yp, ym):
        for zz in (zm, zp, z):
            partial(1, yy, zz)
    partials(1, y)
    plain_z(0)
    give_back(1, 1)
    joined_f(0, 1, zp)
    joined_g(0, 2, zm)
    first_f(1, 2, zm)
    first_g(1, 1, zp)
    first_f(1, 1, zp)
    first_g(1, 2, zm)
    first_f(0, 3, z)
    first_g(0, 3, z)
    plain_g(1, 1, zp)
    plain_f(1, 2, zm)
    far_z(1)
    joined_z(0)
    give_back(1, 0)
    joined_f(1, 2, zm)
    joined_g(1, 1, zp)
    plain_g(1, 2, zm)
    plain_f(1, 1, zp)
    joined_f(1, 1, zp)
    joined_g(1, 2, zm)
    first_f(1, 3, z)
    first_g(1, 3, z)
    plain_g(0, 3, z)
    plain_f(0, 3, z)
    joined_f(0, 3, z)
    joined_g(0, 3, z)
    plain_g(1, 3, z)
    plain_f(1, 3, z)
    plain_z(1)
    joined_z(1)
    joined_f(1, 3, z)
    joined_g(1, 3, z)

    for n in range(2):
        local[n].wait()
        for q in range(4):
            for crossing in range(2):
                for rows, _, fro, _ in partners(q)[crossing]:
                    which = 0 if rows is near else 1
                    arrived(BK.at[n, :, fro, rows], "back", n, crossing, q, which)
    tn = (((0,), (0,)), ((), ()))
    for yy in range(NY):
        back = BK[0, yy].reshape(ROWS, YB)
        out = sum(
            lax.dot_general(SEL[n], back, tn, preferred_element_type=F32) for n in (3, 2, 1)
        )
        back = BK[1, yy].reshape(ROWS, YB)
        d_in = lax.dot_general(SEL[0], back, tn, preferred_element_type=F32)
        for zz in range(NZ):
            cols = slice((zz * 4 + yy) * SH, (zz * 4 + yy + 1) * SH)
            lo_ref[:, cols] = out[:, zz * SH:(zz + 1) * SH].astype(BF16)
            dt_ref[:, cols] = d_in[:, zz * SH:(zz + 1) * SH].astype(BF16)

    finish(0)
    finish(1)
    close(0)
    close(1)

    for copy in sent:
        copy.wait_send()
    assert len(numbers) <= N_SEM


def hand_out(*refs):
    count = len(refs) // 2
    done = refs[-1]
    copies = [
        pltpu.make_async_copy(refs[n], refs[count + n], done.at[n]) for n in range(count)
    ]
    for copy in copies:
        copy.start()
    for copy in copies:
        copy.wait()


def shards(tokens, routes, gate_scale, w_gate, w_up, w_down, d_out):
    vm = pl.BlockSpec(memory_space=pltpu.VMEM)
    hbm = pl.BlockSpec(memory_space=pltpu.HBM)
    grad = jax.ShapeDtypeStruct(w_gate.shape, F32)
    rows = jax.ShapeDtypeStruct(tokens.shape, BF16)
    results = (rows, rows, grad, grad, grad)

    def chunks(kind, *lead):
        return [pltpu.VMEM((*lead, 3 * w), kind) for w in CW]

    found = pl.pallas_call(
        kernel,
        out_shape=results,
        in_specs=[hbm] * 7,
        out_specs=(vm,) * 5,
        scratch_shapes=[
            *chunks(BF16, NY, NZ, SH),
            *chunks(BF16, 64),
            pltpu.VMEM((NY, 2 * NE, CAP, YB), BF16),
            pltpu.VMEM((NY, 2 * NE, CAP, YB), BF16),
            pltpu.VMEM((NY, YB, 2 * ROWS), BF16),
            pltpu.VMEM((NY, YB, 2 * ROWS), BF16),
            pltpu.VMEM((NY, NE, CAP, YB), BF16),
            pltpu.VMEM((NY, NE, CAP, YB), BF16),
            pltpu.VMEM((4, ROWS, TOK), BF16),
            *chunks(F32, 2 * ROWS),
            *chunks(BF16, 2 * ROWS),
            *chunks(BF16, NY, NZ, SH),
            *chunks(BF16, 2, NZ, 64),
            *chunks(BF16, 2, NZ, SH),
            *chunks(BF16, 2, 64),
            *chunks(BF16, 2, SH),
            *chunks(BF16, 3, SH),
            *chunks(F32, 64),
            *chunks(F32, 64),
            pltpu.VMEM((2, NY, NE, CAP, YB), BF16),
            pltpu.VMEM((2, NY, NE, CAP, YB), BF16),
            pltpu.VMEM((2, NY, NE, CAP, YB), BF16),
            pltpu.VMEM((2, NY, NE, CAP, YB), BF16),
            pltpu.VMEM(tokens.shape, BF16),
            pltpu.VMEM(tokens.shape, BF16),
            pltpu.VMEM(routes.shape[::-1], jnp.int32),
            pltpu.VMEM(routes.shape[::-1], F32),
            pltpu.SemaphoreType.DMA((N_SEM,)),
            pltpu.SemaphoreType.DMA((N_SEM,)),
        ],
        compiler_params=pltpu.CompilerParams(
            collective_id=0, has_side_effects=True, vmem_limit_bytes=VMEM_MB * 1024 * 1024
        ),
    )(*(
        pltpu.with_memory_space_constraint(value, pltpu.HBM)
        for value in (tokens, routes.T, gate_scale.T, w_gate, w_up, w_down, d_out)
    ))
    return pl.pallas_call(
        hand_out,
        out_shape=results,
        in_specs=[vm] * 5,
        out_specs=(hbm,) * 5,
        scratch_shapes=[pltpu.SemaphoreType.DMA((5,))],
        compiler_params=pltpu.CompilerParams(vmem_limit_bytes=8 * 1024 * 1024),
    )(*found)


def solution(mesh):
    tok = P(("dp", "expert"), None)
    wei = P("expert", "dp", None)
    return jax.shard_map(
        shards,
        mesh=mesh,
        in_specs=(tok, tok, tok, wei, wei, wei, tok),
        out_specs=(tok, tok, wei, wei, wei),
        check_vma=False,
    )
```

```python
import jax
import jax.numpy as jnp
from jax import lax
from jax.experimental import pallas as pl
from jax.experimental.pallas import tpu as pltpu
from jax.sharding import PartitionSpec as P

CAP = 32
MESH = pl.DeviceIdType.MESH
F32 = jnp.float32
BF16 = jnp.bfloat16

NY, NZ, SH = 4, 4, 128
HH = 384
CW = (256, 128)
CO = (0, 256)
YB = NZ * SH
NE = 8
TOK = 192
ROWS = NE * CAP
N_SEM = 240
VMEM_MB = 50


def kernel(
    tok_hbm, rt_hbm, gs_hbm, wg_ref, wu_ref, wd_ref, do_hbm,
    lo_ref, dt_ref, gg_ref, gu_ref, gd_ref,
    W0, W1, WO0, WO1, X, D, XT, DT, SX, SD, SEL, A0, A1, C0, C1, T0, T1,
    RF0, RF1, RS0, RS1, ZF0, ZF1, Z20, Z21, ZS0, ZS1, FS0, FS1, FR0, FR1,
    OS, OR, BS, BK, tok_ref, do_ref, rt_ref, gs_ref, ss, rs,
):
    W, WO, ACC, CAT, T = (W0, W1), (WO0, WO1), (A0, A1), (C0, C1), (T0, T1)
    R1, R2, Z1, Z2, ZS = (RF0, RF1), (RS0, RS1), (ZF0, ZF1), (Z20, Z21), (ZS0, ZS1)
    FS, FR = (FS0, FS1), (FR0, FR1)
    i = lax.axis_index("dp")
    j = lax.axis_index("expert")
    c = lax.rem(i, 2)
    o = 1 - c
    p = lax.div(i, 2)
    y = lax.rem(p, 4)
    z = lax.div(p, 4)
    x = lax.div(j, 2)
    side = lax.rem(j, 2)
    yp, ym, y2 = lax.rem(y + 1, 4), lax.rem(y + 3, 4), lax.rem(y + 2, 4)
    zp, zm, z2 = lax.rem(z + 1, 4), lax.rem(z + 3, 4), lax.rem(z + 2, 4)
    zn = lax.rem(z + 3 + 2 * side, 4)

    def place(yy, zz, cc):
        return {"dp": (zz * 4 + yy) * 2 + cc}

    sib = place(y, z, o)
    up_y, down_y = place(yp, z, c), place(ym, z, c)
    up_z, down_z = place(y, zp, c), place(y, zm, c)

    near, far = pl.ds(0, 16), pl.ds(16, 16)

    def partners(q):
        to, fro = lax.rem(x + q, 4), lax.rem(x + 4 - q, 4)
        across = [
            (near, to * 2 + 1 - side, fro * 2 + 1 - side, {"expert": to * 2 + 1 - side}),
            (far, to * 2 + 1 - side, fro * 2 + 1 - side,
             {"dp": (zn * 4 + y) * 2 + c, "expert": to * 2 + 1 - side}),
        ]
        same = [(pl.ds(0, CAP), to * 2 + side, fro * 2 + side, {"expert": to * 2 + side})]
        return same if q else [], across

    numbers = {}

    def number(*name):
        return numbers.setdefault(name, len(numbers))

    sent = []

    def send(src, dst, name, to):
        k = number(*name)
        copy = pltpu.make_async_remote_copy(
            src_ref=src, dst_ref=dst, send_sem=ss.at[k], recv_sem=rs.at[k],
            device_id=to, device_id_type=MESH,
        )
        copy.start()
        sent.append(copy)

    def arrived(ref, *name):
        k = number(*name)
        pltpu.make_async_remote_copy(
            src_ref=ref, dst_ref=ref, send_sem=ss.at[k], recv_sem=rs.at[k],
            device_id=sib, device_id_type=MESH,
        ).wait_recv()

    def fetch(src, dst, *name):
        copy = pltpu.make_async_copy(src, dst, rs.at[number(*name)])
        copy.start()
        return copy

    f = pl.ds(pl.multiple_of(c * 64, 64), 64)
    g = pl.ds(pl.multiple_of(o * 64, 64), 64)

    def units(core, k):
        return pl.ds(pl.multiple_of(core * HH + CO[k], 128), CW[k])

    own, other = [[], []], [[], []]
    for k in range(2):
        for n, w_ref in enumerate((wg_ref, wu_ref, wd_ref)):
            cols = pl.ds(n * CW[k], CW[k])
            other[k].append(
                fetch(w_ref.at[0, :, units(o, k)], WO[k].at[:, cols], "other", k, n)
            )
            own[k].append(
                fetch(w_ref.at[0, :, units(c, k)], W[k].at[y, z, f, cols], "own", k, n)
            )
    loads = [
        fetch(rt_hbm, rt_ref, "load", "r"),
        fetch(gs_hbm, gs_ref, "load", "s"),
        fetch(tok_hbm, tok_ref, "load", "x"),
        fetch(do_hbm, do_ref, "load", "d"),
    ]
    barrier = pltpu.get_barrier_semaphore()
    greet = [sib, up_y, down_y, up_z, down_z]
    for q in range(4):
        same, across = partners(q)
        greet += [to for _, _, _, to in same + across]
    for to in greet:
        pl.semaphore_signal(barrier, inc=1, device_id=to, device_id_type=MESH)
    for k in range(2):
        for copy in other[k] + own[k]:
            copy.wait()
    pl.semaphore_wait(barrier, len(greet))

    def along(k, yy, zz, piece, name, to):
        send(W[k].at[yy, zz, piece], W[k].at[yy, zz, piece], (k,) + name, to)

    def here(k, yy, zz, piece, *name):
        arrived(W[k].at[yy, zz, piece], k, *name)

    def leave(k, kind, piece, way):
        to_z, to_y = (up_z, up_y) if way == "up" else (down_z, down_y)
        along(k, y, z, piece, ("gz", kind, way), to_z)
        along(k, y, z, piece, ("gy", 0, kind, way), to_y)

    for k in range(2):
        send(WO[k], W[k].at[y, z, f], ("sib", k), sib)
    leave(0, "f", f, "up")
    arrived(W[0].at[y, z, g], "sib", 0)
    leave(0, "g", g, "down")
    leave(0, "g", g, "up")
    leave(0, "f", f, "down")
    leave(1, "f", f, "up")
    arrived(W[1].at[y, z, g], "sib", 1)
    leave(1, "g", g, "down")
    leave(1, "g", g, "up")
    leave(1, "f", f, "down")

    shape = (ROWS, TOK)
    row = lax.broadcasted_iota(jnp.int32, shape, 0)
    row_e = lax.div(row, CAP)
    row_s = lax.rem(row, CAP).astype(F32)
    for copy in loads[:2]:
        copy.wait()
    scale = gs_ref[...]
    combine = scale / jnp.sum(scale, axis=0, keepdims=True)
    routes = rt_ref[...]
    named = jnp.zeros(shape, F32)
    weight = jnp.zeros(shape, F32)
    for s in range(6):
        same = routes[s:s + 1, :] == row_e
        named = jnp.where(same, 1.0, named)
        weight = jnp.where(same, combine[s:s + 1, :], weight)
    earlier = (
        lax.broadcasted_iota(jnp.int32, (TOK, TOK), 0)
        < lax.broadcasted_iota(jnp.int32, (TOK, TOK), 1)
    ).astype(F32).astype(BF16)
    position = jnp.dot(named.astype(BF16), earlier, preferred_element_type=F32)
    chosen = jnp.where(position == row_s, named, 0.0)
    weight = weight * chosen
    slot_weight = jnp.sum(weight, axis=1, keepdims=True)
    select = chosen.astype(BF16)
    SEL[0] = select
    rest = weight
    for n in range(1, 4):
        part = rest.astype(BF16)
        SEL[n] = part
        rest = rest - part.astype(F32)

    def columns(ref, yy):
        return jnp.concatenate(
            [ref[:, (zz * 4 + yy) * SH:(zz * 4 + yy + 1) * SH] for zz in range(NZ)], axis=1
        )

    for copy in loads[2:]:
        copy.wait()
    for yy in range(NY):
        rows = jnp.dot(select, columns(tok_ref, yy), preferred_element_type=F32)
        SX[yy] = rows.astype(BF16).reshape(NE, CAP, YB)
        rows = jnp.dot(select, columns(do_ref, yy), preferred_element_type=F32)
        SD[yy] = (rows * slot_weight).astype(BF16).reshape(NE, CAP, YB)

    mine = c * NE + j
    rows_out = ((SX, X, "x"), (SD, D, "d"))

    def exchange(crossing):
        for src, dst, what in rows_out:
            for q in range(4):
                for rows, to, _, device in partners(q)[crossing]:
                    which = 0 if rows is near else 1
                    send(src.at[:, to, rows], dst.at[:, mine, rows],
                         ("to", what, crossing, q, which), device)

    exchange(0)
    local = [fetch(src.at[:, j], dst.at[:, mine], "keep", what) for src, dst, what in rows_out]

    def spread_y(k, step, zz, piece, kind):
        along(k, y, zz, piece, ("gy", step, kind, "up"), up_y)
        along(k, y, zz, piece, ("gy", step, kind, "down"), down_y)

    def onward_f(k, step, zz):
        here(k, ym, zz, f, "gy", step, "f", "up")
        along(k, ym, zz, f, ("gy", step, "f", "on"), up_y)

    def onward_g(k, step, zz):
        here(k, yp, zz, g, "gy", step, "g", "down")
        along(k, yp, zz, g, ("gy", step, "g", "on"), down_y)

    def onward_z(k):
        here(k, y, zm, f, "gz", "f", "up")
        along(k, y, zm, f, ("gz", "f", "on"), up_z)
        here(k, y, zp, g, "gz", "g", "down")
        along(k, y, zp, g, ("gz", "g", "on"), down_z)

    onward_f(0, 0, z)
    onward_g(0, 0, z)
    onward_z(0)
    spread_y(0, 1, zm, f, "f")
    spread_y(0, 2, zp, g, "g")
    exchange(1)
    onward_f(1, 0, z)
    onward_g(1, 0, z)
    here(0, y, zm, g, "gz", "g", "up")
    spread_y(0, 1, zm, g, "g")
    here(0, y, zp, f, "gz", "f", "down")
    spread_y(0, 2, zp, f, "f")
    onward_z(1)
    onward_f(0, 1, zm)
    onward_g(0, 2, zp)
    here(0, y, z2, f, "gz", "f", "on")
    spread_y(0, 3, z2, f, "f")
    here(0, y, z2, g, "gz", "g", "on")
    spread_y(0, 3, z2, g, "g")
    here(1, y, zm, g, "gz", "g", "up")
    here(1, y, zp, f, "gz", "f", "down")
    for step, zz in ((1, zm), (2, zp)):
        spread_y(1, step, zz, f, "f")
        spread_y(1, step, zz, g, "g")
    onward_g(0, 1, zm)
    onward_f(0, 2, zp)
    onward_f(0, 3, z2)
    onward_g(0, 3, z2)
    for step, zz in ((1, zm), (2, zp)):
        onward_f(1, step, zz)
        onward_g(1, step, zz)
    for n, (_, dst, what) in enumerate(rows_out):
        local[n].wait()
        for q in range(4):
            for crossing in range(2):
                for rows, _, fro, _ in partners(q)[crossing]:
                    which = 0 if rows is near else 1
                    arrived(dst.at[:, c * NE + fro, rows], "to", what, crossing, q, which)
        block = dst.at[:, pl.ds(c * NE, NE)]
        send(block, block, ("rows", what), sib)

    def turn(m, first, last):
        def body(step, carry):
            yy = lax.rem(y2 + step, NY)
            cols = pl.ds(pl.multiple_of(m * ROWS, ROWS), ROWS)
            blocks = pl.ds(m * NE, NE)
            XT[yy, :, cols] = X[yy, blocks].reshape(ROWS, YB).T
            DT[yy, :, cols] = D[yy, blocks].reshape(ROWS, YB).T
            return carry

        lax.fori_loop(first, last, body, 0)

    tiles = (
        ((0, 0, 256), (0, 256, 512), (1, 512, 768)),
        ((0, 0, 256), (1, 256, 384)),
    )

    def accumulate(k, yy, m, first=False):
        rows = pl.ds(pl.multiple_of(m * ROWS, ROWS), ROWS)
        blocks = pl.ds(m * NE, NE)
        for which, lo, hi in tiles[k]:
            got = jnp.dot(
                (X, D)[which][yy, blocks].reshape(ROWS, YB),
                W[k][yy, :, :, lo:hi].reshape(YB, hi - lo),
                preferred_element_type=F32,
            )
            if first:
                ACC[k][rows, lo:hi] = got
            else:
                ACC[k][rows, lo:hi] += got

    steps = ((0, z), (1, zm), (2, zp), (3, z2))

    def wait_m(k):
        for step, zz in steps:
            here(k, ym, zz, g, "gy", step, "g", "up")

    def wait_p(k):
        for step, zz in steps:
            here(k, yp, zz, f, "gy", step, "f", "down")

    def wait_2(k):
        for step, zz in steps:
            here(k, y2, zz, f, "gy", step, "f", "on")
            here(k, y2, zz, g, "gy", step, "g", "on")

    turn(c, 0, NY)
    here(1, y, z2, f, "gz", "f", "on")
    spread_y(1, 3, z2, f, "f")
    here(1, y, z2, g, "gz", "g", "on")
    spread_y(1, 3, z2, g, "g")
    accumulate(0, y, c, True)
    wait_m(0)
    accumulate(0, ym, c)
    wait_p(0)
    accumulate(0, yp, c)
    wait_2(0)
    accumulate(0, y2, c)
    arrived(X.at[:, pl.ds(o * NE, NE)], "rows", "x")
    arrived(D.at[:, pl.ds(o * NE, NE)], "rows", "d")
    turn(o, 0, 1)
    accumulate(0, y, o, True)
    accumulate(0, ym, o)
    accumulate(0, yp, o)
    accumulate(0, y2, o)

    def activate(k):
        w = CW[k]

        def body(m, carry):
            rows = pl.ds(pl.multiple_of(m * 64, 64), 64)
            gate, up, d_hidden = (ACC[k][rows, n * w:(n + 1) * w] for n in range(3))
            sig = jax.nn.sigmoid(gate)
            act = gate * sig
            CAT[k][rows, 0:w] = (
                d_hidden * up * sig * (1.0 + gate * (1.0 - sig))
            ).astype(BF16)
            CAT[k][rows, w:2 * w] = (d_hidden * act).astype(BF16)
            CAT[k][rows, 2 * w:3 * w] = (act * up).astype(BF16)
            return carry

        lax.fori_loop(0, 2 * ROWS // 64, body, 0)

    def partials(k, yy):
        for which, lo, hi in tiles[k]:
            got = jnp.dot(
                (XT, DT)[which][yy], CAT[k][:, lo:hi], preferred_element_type=F32
            )
            T[k][yy, :, :, lo:hi] = got.astype(BF16).reshape(NZ, SH, hi - lo)

    def partial(k, yy, zz):
        rows = pl.ds(pl.multiple_of(zz * SH, SH), SH)
        for which, lo, hi in tiles[k]:
            got = jnp.dot(
                (XT, DT)[which][yy, rows], CAT[k][:, lo:hi], preferred_element_type=F32
            )
            T[k][yy, zz, :, lo:hi] = got.astype(BF16)

    nt = (((1,), (1,)), ((), ()))

    def output(side_, n, yy):
        rows = pl.ds(pl.multiple_of(side_ * ROWS, ROWS), ROWS)
        total = None
        for k in range(2):
            lo, hi = ((2 * CW[k], 3 * CW[k]), (0, 2 * CW[k]))[n]
            got = lax.dot_general(
                CAT[k][rows, lo:hi], W[k][yy, :, :, lo:hi].reshape(YB, hi - lo), nt,
                preferred_element_type=F32,
            )
            total = got if total is None else total + got
        return total

    def output_sibling(n):
        for yy in range(NY):
            OS[n, yy] = output(o, n, yy).astype(BF16).reshape(NE, CAP, YB)
            send(OS.at[n, yy], OR.at[n, yy], ("part", n, yy), sib)

    def output_own(n):
        for yy in range(NY):
            value = output(c, n, yy)
            arrived(OR.at[n, yy], "part", n, yy)
            value = value + OR[n, yy].reshape(ROWS, YB).astype(F32)
            BS[n, yy] = value.astype(BF16).reshape(NE, CAP, YB)

    def give_back(n, crossing):
        for q in range(4):
            for rows, to, _, device in partners(q)[crossing]:
                which = 0 if rows is near else 1
                send(BS.at[n, :, to, rows], BK.at[n, :, j, rows],
                     ("back", n, crossing, q, which), device)

    def first_f(k, step, zz):
        send(T[k].at[y2, zz, f], R1[k].at[0, step], ("r1", k, step, "f"), up_y)

    def first_g(k, step, zz):
        send(T[k].at[y2, zz, g], R1[k].at[1, step], ("r1", k, step, "g"), down_y)

    def plain_g(k, step, zz):
        send(T[k].at[yp, zz, g], R2[k].at[0, step, g], ("r2", k, step, "g", "up"), up_y)

    def plain_f(k, step, zz):
        send(T[k].at[ym, zz, f], R2[k].at[1, step, f], ("r2", k, step, "f", "down"), down_y)

    def joined_f(k, step, zz):
        arrived(R1[k].at[0, step], "r1", k, step, "f")
        T[k][yp, zz, f] = (
            T[k][yp, zz, f].astype(F32) + R1[k][0, step].astype(F32)
        ).astype(BF16)
        send(T[k].at[yp, zz, f], R2[k].at[0, step, f], ("r2", k, step, "f", "up"), up_y)

    def joined_g(k, step, zz):
        arrived(R1[k].at[1, step], "r1", k, step, "g")
        T[k][ym, zz, g] = (
            T[k][ym, zz, g].astype(F32) + R1[k][1, step].astype(F32)
        ).astype(BF16)
        send(T[k].at[ym, zz, g], R2[k].at[1, step, g], ("r2", k, step, "g", "down"), down_y)

    def summed_y(k, step, zz, piece, kind):
        for d in range(2):
            arrived(R2[k].at[d, step, piece], "r2", k, step, kind, ("up", "down")[d])
        return (
            T[k][y, zz, piece].astype(F32)
            + R2[k][0, step, piece].astype(F32)
            + R2[k][1, step, piece].astype(F32)
        )

    def far_z(k):
        ZS[k][0, f] = summed_y(k, 0, z2, f, "f").astype(BF16)
        send(ZS[k].at[0, f], Z1[k].at[0], ("z1", k, "f"), up_z)
        ZS[k][0, g] = summed_y(k, 0, z2, g, "g").astype(BF16)
        send(ZS[k].at[0, g], Z1[k].at[1], ("z1", k, "g"), down_z)

    def plain_z(k):
        ZS[k][2, f] = summed_y(k, 2, zm, f, "f").astype(BF16)
        send(ZS[k].at[2, f], Z2[k].at[1, f], ("z2", k, "f", "down"), down_z)
        ZS[k][1, g] = summed_y(k, 1, zp, g, "g").astype(BF16)
        send(ZS[k].at[1, g], Z2[k].at[0, g], ("z2", k, "g", "up"), up_z)

    def joined_z(k):
        total = summed_y(k, 1, zp, f, "f")
        arrived(Z1[k].at[0], "z1", k, "f")
        ZS[k][1, f] = (total + Z1[k][0].astype(F32)).astype(BF16)
        send(ZS[k].at[1, f], Z2[k].at[0, f], ("z2", k, "f", "up"), up_z)
        total = summed_y(k, 2, zm, g, "g")
        arrived(Z1[k].at[1], "z1", k, "g")
        ZS[k][2, g] = (total + Z1[k][1].astype(F32)).astype(BF16)
        send(ZS[k].at[2, g], Z2[k].at[1, g], ("z2", k, "g", "down"), down_z)

    def total_z(k, piece, kind):
        total = summed_y(k, 3, z, piece, kind)
        arrived(Z2[k].at[0, piece], "z2", k, kind, "up")
        arrived(Z2[k].at[1, piece], "z2", k, kind, "down")
        return total + Z2[k][0, piece].astype(F32) + Z2[k][1, piece].astype(F32)

    grads = (gg_ref, gu_ref, gd_ref)

    def finish(k):
        w = CW[k]
        FS[k][...] = total_z(k, g, "g")
        send(FS[k], FR[k], ("fin", k), sib)
        total = total_z(k, f, "f")
        for n, ref in enumerate(grads):
            ref[0, :, units(c, k)] = total[:, n * w:(n + 1) * w]

    def close(k):
        w = CW[k]
        arrived(FR[k], "fin", k)
        for n, ref in enumerate(grads):
            ref[0, :, units(o, k)] = FR[k][:, n * w:(n + 1) * w]

    activate(0)
    onward_f(1, 3, z2)
    onward_g(1, 3, z2)
    partial(0, y2, z2)
    first_f(0, 0, z2)
    first_g(0, 0, z2)
    turn(o, 1, NY)
    partial(0, yp, z2)
    plain_g(0, 0, z2)
    partial(0, ym, z2)
    plain_f(0, 0, z2)
    partial(0, y2, zm)
    first_f(0, 2, zm)
    partial(0, y2, zp)
    first_g(0, 1, zp)
    for m, first in ((c, True), (o, True)):
        accumulate(1, y, m, first)
    wait_m(1)
    wait_p(1)
    for m in (c, o):
        accumulate(1, ym, m)
        accumulate(1, yp, m)
    wait_2(1)
    for m in (c, o):
        accumulate(1, y2, m)
    activate(1)
    output_sibling(0)
    joined_f(0, 0, z2)
    joined_g(0, 0, z2)
    partial(0, yp, zp)
    plain_g(0, 1, zp)
    partial(0, ym, zm)
    plain_f(0, 2, zm)
    output_own(0)
    give_back(0, 1)
    local = [fetch(BS.at[0, :, j], BK.at[0, :, j], "stay", 0)]
    for yy in (y2, yp, ym):
        partial(1, yy, z2)
    first_f(1, 0, z2)
    first_g(1, 0, z2)
    plain_g(1, 0, z2)
    plain_f(1, 0, z2)
    partial(0, yp, zm)
    partial(0, ym, zp)
    joined_f(0, 2, zm)
    joined_g(0, 1, zp)
    first_f(0, 1, zp)
    first_g(0, 2, zm)
    plain_g(0, 2, zm)
    plain_f(0, 1, zp)
    output_sibling(1)
    partial(0, y, z2)
    far_z(0)
    output_own(1)
    local.append(fetch(BS.at[1, :, j], BK.at[1, :, j], "stay", 1))
    joined_f(1, 0, z2)
    joined_g(1, 0, z2)
    for zz in (zm, zp, z):
        partial(0, y, zz)
    for yy in (y2, yp, ym):
        partial(0, yy, z)
    give_back(0, 0)
    for yy in (y2, yp, ym):
        for zz in (zm, zp, z):
            partial(1, yy, zz)
    partials(1, y)
    give_back(1, 1)
    plain_z(0)
    joined_f(0, 1, zp)
    joined_g(0, 2, zm)
    first_f(1, 2, zm)
    first_g(1, 1, zp)
    first_f(1, 1, zp)
    first_g(1, 2, zm)
    first_f(0, 3, z)
    first_g(0, 3, z)
    plain_g(1, 1, zp)
    plain_f(1, 2, zm)
    far_z(1)
    joined_z(0)
    give_back(1, 0)
    joined_f(1, 2, zm)
    joined_g(1, 1, zp)
    plain_g(1, 2, zm)
    plain_f(1, 1, zp)
    joined_f(1, 1, zp)
    joined_g(1, 2, zm)
    first_f(1, 3, z)
    first_g(1, 3, z)
    plain_g(0, 3, z)
    plain_f(0, 3, z)
    joined_f(0, 3, z)
    joined_g(0, 3, z)
    plain_g(1, 3, z)
    plain_f(1, 3, z)
    plain_z(1)
    joined_z(1)
    joined_f(1, 3, z)
    joined_g(1, 3, z)

    for n in range(2):
        local[n].wait()
        for q in range(4):
            for crossing in range(2):
                for rows, _, fro, _ in partners(q)[crossing]:
                    which = 0 if rows is near else 1
                    arrived(BK.at[n, :, fro, rows], "back", n, crossing, q, which)
    tn = (((0,), (0,)), ((), ()))
    for yy in range(NY):
        back = BK[0, yy].reshape(ROWS, YB)
        out = sum(
            lax.dot_general(SEL[n], back, tn, preferred_element_type=F32) for n in (3, 2, 1)
        )
        back = BK[1, yy].reshape(ROWS, YB)
        d_in = lax.dot_general(SEL[0], back, tn, preferred_element_type=F32)
        for zz in range(NZ):
            cols = slice((zz * 4 + yy) * SH, (zz * 4 + yy + 1) * SH)
            lo_ref[:, cols] = out[:, zz * SH:(zz + 1) * SH].astype(BF16)
            dt_ref[:, cols] = d_in[:, zz * SH:(zz + 1) * SH].astype(BF16)

    finish(0)
    finish(1)
    close(0)
    close(1)

    for copy in sent:
        copy.wait_send()
    assert len(numbers) <= N_SEM


def hand_out(*refs):
    count = len(refs) // 2
    done = refs[-1]
    copies = [
        pltpu.make_async_copy(refs[n], refs[count + n], done.at[n]) for n in range(count)
    ]
    for copy in copies:
        copy.start()
    for copy in copies:
        copy.wait()


def shards(tokens, routes, gate_scale, w_gate, w_up, w_down, d_out):
    vm = pl.BlockSpec(memory_space=pltpu.VMEM)
    hbm = pl.BlockSpec(memory_space=pltpu.HBM)
    grad = jax.ShapeDtypeStruct(w_gate.shape, F32)
    rows = jax.ShapeDtypeStruct(tokens.shape, BF16)
    results = (rows, rows, grad, grad, grad)

    def chunks(kind, *lead):
        return [pltpu.VMEM((*lead, 3 * w), kind) for w in CW]

    found = pl.pallas_call(
        kernel,
        out_shape=results,
        in_specs=[hbm] * 7,
        out_specs=(vm,) * 5,
        scratch_shapes=[
            *chunks(BF16, NY, NZ, SH),
            *chunks(BF16, 64),
            pltpu.VMEM((NY, 2 * NE, CAP, YB), BF16),
            pltpu.VMEM((NY, 2 * NE, CAP, YB), BF16),
            pltpu.VMEM((NY, YB, 2 * ROWS), BF16),
            pltpu.VMEM((NY, YB, 2 * ROWS), BF16),
            pltpu.VMEM((NY, NE, CAP, YB), BF16),
            pltpu.VMEM((NY, NE, CAP, YB), BF16),
            pltpu.VMEM((4, ROWS, TOK), BF16),
            *chunks(F32, 2 * ROWS),
            *chunks(BF16, 2 * ROWS),
            *chunks(BF16, NY, NZ, SH),
            *chunks(BF16, 2, NZ, 64),
            *chunks(BF16, 2, NZ, SH),
            *chunks(BF16, 2, 64),
            *chunks(BF16, 2, SH),
            *chunks(BF16, 3, SH),
            *chunks(F32, 64),
            *chunks(F32, 64),
            pltpu.VMEM((2, NY, NE, CAP, YB), BF16),
            pltpu.VMEM((2, NY, NE, CAP, YB), BF16),
            pltpu.VMEM((2, NY, NE, CAP, YB), BF16),
            pltpu.VMEM((2, NY, NE, CAP, YB), BF16),
            pltpu.VMEM(tokens.shape, BF16),
            pltpu.VMEM(tokens.shape, BF16),
            pltpu.VMEM(routes.shape[::-1], jnp.int32),
            pltpu.VMEM(routes.shape[::-1], F32),
            pltpu.SemaphoreType.DMA((N_SEM,)),
            pltpu.SemaphoreType.DMA((N_SEM,)),
        ],
        compiler_params=pltpu.CompilerParams(
            collective_id=0, has_side_effects=True, vmem_limit_bytes=VMEM_MB * 1024 * 1024
        ),
    )(*(
        pltpu.with_memory_space_constraint(value, pltpu.HBM)
        for value in (tokens, routes.T, gate_scale.T, w_gate, w_up, w_down, d_out)
    ))
    return pl.pallas_call(
        hand_out,
        out_shape=results,
        in_specs=[vm] * 5,
        out_specs=(hbm,) * 5,
        scratch_shapes=[pltpu.SemaphoreType.DMA((5,))],
        compiler_params=pltpu.CompilerParams(vmem_limit_bytes=8 * 1024 * 1024),
    )(*found)


def solution(mesh):
    tok = P(("dp", "expert"), None)
    wei = P("expert", "dp", None)
    return jax.shard_map(
        shards,
        mesh=mesh,
        in_specs=(tok, tok, tok, wei, wei, wei, tok),
        out_specs=(tok, tok, wei, wei, wei),
        check_vma=False,
    )
```
